32 devices in a mesh: dp: 8 (over y, x, core), seq: 4 (over z).
Axes of the slice: x: 2, y: 2, z: 4, core: 2. Of those that a mesh axis runs over, the one named last changes fastest.
Arguments:
- frames: float32 [8, 1536, 768], P('dp', 'seq'), may hold values from -6 to 6
- clip_ids: int32 [8, 1536], P('dp', 'seq'), may hold values from -1 to 1, as said below
- cotangent: float32 [8, 1536, 768], P('dp', 'seq'), may hold values from -6 to 6
- mats: float32 [3, 768, 3072], P(None, ('dp', 'seq'))
- smalls: float32 [12, 768], P(None, ('dp', 'seq'))
- mats_m: float32 [3, 768, 3072], P(None, ('dp', 'seq')), as said below
- mats_v: float32 [3, 768, 3072], P(None, ('dp', 'seq')), as said below
- smalls_m: float32 [12, 768], P(None, ('dp', 'seq')), as said below
- smalls_v: float32 [12, 768], P(None, ('dp', 'seq')), as said below
Outputs:
- out_frames: float32 [8, 1536, 768], P('dp', 'seq')
- frames_grad: float32 [8, 1536, 768], P('dp', 'seq')
- mats_grad: float32 [3, 768, 3072], P(None, ('dp', 'seq'))
- smalls_grad: float32 [12, 768], P(None, ('dp', 'seq'))
- new_mats: float32 [3, 768, 3072], P(None, ('dp', 'seq'))
- new_smalls: float32 [12, 768], P(None, ('dp', 'seq'))
- new_mats_m: float32 [3, 768, 3072], P(None, ('dp', 'seq'))
- new_mats_v: float32 [3, 768, 3072], P(None, ('dp', 'seq'))
- new_smalls_m: float32 [12, 768], P(None, ('dp', 'seq'))
- new_smalls_v: float32 [12, 768], P(None, ('dp', 'seq'))
The draws below stay inside these ranges and needn't reach their ends.
Inputs may be any that keep to these rules, and one draw needn't show every extreme that they name: `clip_ids`: in each data group (row) the ids that are not -1 count up from 0 in order, each id a run of consecutive frames; every clip has at least 750 and at most 1500 frames, and some clip has exactly 1500; -1 marks padding frames at the end of a group, which attend among themselves. `mats_m`: first moments of the weights' size of gradient over a few steps. `mats_v`: second moments, positive. `smalls_m`: first moments of the gains' and biases' size of gradient over a few steps. `smalls_v`: second moments, positive.
All inputs are finite; a program needn't handle non-finite values.
Results may differ from the reference program's by a relative error of at most 0.012.
Values may be sent and summed in bfloat16 or wider, within the bound.
No kernel may reach another device: no remote copies, remote signals or barrier semaphores. Data moves between devices by JAX's collectives and lax.ppermute only.
A program may use at most 192 MiB of HBM per device.

```python
import math
import jax
import jax.numpy as jnp
from jax import lax

D = 768
H = 12
DH = 64
FF = 3072
CLIP = 1500
STEP = 3
GROUP = 1536
GROUPS = 8
TOKENS = 12288


def draw_clip_ids(key, part):
    length_key, limit_key = jax.random.split(jax.random.fold_in(key, 11))
    slots = GROUP // (CLIP // 2) + 1
    lengths = jax.random.randint(length_key, (GROUPS, slots), CLIP // 2, CLIP + 1)
    lengths = lengths.at[2].set(CLIP // 2)
    lengths = lengths.at[0, 0].set(CLIP)
    ends = jnp.cumsum(lengths, axis=1)
    limits = jax.random.randint(limit_key, (GROUPS,), GROUP // 4, GROUP + 1)
    limits = limits.at[0].set(GROUP).at[1].set(GROUP // 4).at[2].set(GROUP)
    places = jnp.arange(GROUP, dtype=jnp.int32)
    index = jnp.sum((ends[:, None, :] <= places[None, :, None]).astype(jnp.int32), axis=2)
    clip_end = jnp.take_along_axis(ends, index, axis=1)
    return jnp.where(clip_end <= limits[:, None], index, -1).astype(jnp.int32)


def draw_mats(key, part):
    noise_key = jax.random.fold_in(key, 21)
    noise = jax.random.normal(noise_key, (3, D, 4 * D), jnp.float32)
    scale_in = D ** (-0.5)
    first = jnp.concatenate([noise[0, :, :3 * D] * scale_in, noise[0, :, 3 * D:] * (8.0 * scale_in)], axis=1)
    return jnp.stack([first, noise[1] * scale_in, noise[2] * FF ** (-0.5)])


def draw_smalls(key, part):
    gain_key, bias_key = jax.random.split(jax.random.fold_in(key, 31))
    rows = jnp.arange(12)
    gains = jax.random.uniform(gain_key, (12, D), jnp.float32, 0.5, 1.5)
    biases = 0.3 * jax.random.normal(bias_key, (12, D), jnp.float32)
    is_gain = (rows == 0) | (rows == 5)
    return jnp.where(is_gain[:, None], gains, biases)


def mats_size():
    columns = jnp.arange(4 * D)
    first = jnp.where(columns < 3 * D, 0.3, 0.4)
    block = jnp.stack([first, jnp.full((4 * D,), 0.6), jnp.full((4 * D,), 0.6)])
    return jnp.broadcast_to(block[:, None, :], (3, D, 4 * D)) * TOKENS ** 0.5


def smalls_size():
    rows = jnp.arange(12)
    factor = jnp.where(rows >= 8, 0.5, jnp.where((rows == 2) | (rows == 3), 0.5, 1.0))
    return jnp.broadcast_to(factor[:, None], (12, D)) * TOKENS ** 0.5


def first_moment(key, size):
    noise = jax.random.normal(key, size.shape, jnp.float32)
    return 0.2 * size * noise


def second_moment(key, size):
    factor = jnp.exp(jax.random.uniform(key, size.shape, jnp.float32, -0.6931472, 0.6931472))
    return 0.1052632 * size * size * factor


def draw_mats_m(key, part):
    return first_moment(jax.random.fold_in(key, 41), mats_size())


def draw_mats_v(key, part):
    return second_moment(jax.random.fold_in(key, 43), mats_size())


def draw_smalls_m(key, part):
    return first_moment(jax.random.fold_in(key, 47), smalls_size())


def draw_smalls_v(key, part):
    return second_moment(jax.random.fold_in(key, 53), smalls_size())


def levels(key, shape, shards, least, largest):
    def one(position, blocks):
        steps = jax.random.uniform(jax.random.fold_in(jax.random.fold_in(key, 6), position), (blocks,), jnp.float32, least / len(shards), largest / len(shards))
        return jnp.repeat(jnp.exp(steps), shape[position] // blocks).reshape((-1,) + (1,) * (len(shape) - position - 1))

    gain = one(*shards[0])
    for cut in shards[1:]:
        gain = gain * one(*cut)
    return gain


def normal_values(rng, extent, spread, most, pieces=(), kind=jnp.bfloat16):
    loudness = levels(rng, extent, pieces, -0.22, 0.18) if pieces else 1.0
    entries = jax.random.normal(rng, extent, jnp.float32) * spread * loudness
    return jnp.minimum(jnp.maximum(entries, -most), most).astype(kind)


def setup_inputs(seed: int = 0) -> dict:
    splits = jax.random.split(jax.random.key(seed), 10)
    return {
        "frames": normal_values(splits[0], (GROUPS, GROUP, D), 1.0, 6.0, ((0, 8), (1, 4)), jnp.float32),
        "clip_ids": draw_clip_ids(jax.random.fold_in(splits[9], 71), 0),
        "cotangent": normal_values(splits[2], (GROUPS, GROUP, D), 1.0, 6.0, ((0, 8), (1, 4)), jnp.float32),
        "mats": draw_mats(jax.random.fold_in(splits[9], 71), 0),
        "smalls": draw_smalls(jax.random.fold_in(splits[9], 71), 0),
        "mats_m": draw_mats_m(jax.random.fold_in(splits[9], 71), 0),
        "mats_v": draw_mats_v(jax.random.fold_in(splits[9], 71), 0),
        "smalls_m": draw_smalls_m(jax.random.fold_in(splits[9], 71), 0),
        "smalls_v": draw_smalls_v(jax.random.fold_in(splits[9], 71), 0),
    }


NEGATIVE_FILL = -1e+30
NORM_EPSILON = 1e-05
ROOT_HALF = 0.7071067811865476
INV_ROOT_TAU = 0.3989422804014327
BETA_FIRST = 0.9
BETA_SECOND = 0.95
LEARN_RATE = 0.01
SMALL_RATE = 0.1
WEIGHT_DECAY = 0.1
ADAM_EPSILON = 1e-08
HIGHEST_MODE = lax.Precision.HIGHEST

def norm_forward(values, gain_vec, shift_vec):
    row_mean = lax.optimization_barrier(jnp.mean(values, axis=-1, keepdims=True))
    center = values - row_mean
    row_var = lax.optimization_barrier(jnp.mean(center * center, axis=-1, keepdims=True))
    inv_std = lax.rsqrt(row_var + NORM_EPSILON)
    normed = center * inv_std
    return (normed, inv_std, normed * gain_vec + shift_vec)

def norm_backward(incoming, normed, inv_std, gain_vec):
    scaled = incoming * gain_vec
    result = inv_std * (scaled - lax.optimization_barrier(jnp.mean(scaled, axis=-1, keepdims=True)) - normed * lax.optimization_barrier(jnp.mean(scaled * normed, axis=-1, keepdims=True)))
    return (result, lax.optimization_barrier(jnp.sum(incoming * normed, axis=0)), lax.optimization_barrier(jnp.sum(incoming, axis=0)))

def gelu_value(hidden):
    return 0.5 * hidden * (1.0 + jax.scipy.special.erf(hidden * ROOT_HALF))

def gelu_slope(hidden):
    return 0.5 * (1.0 + jax.scipy.special.erf(hidden * ROOT_HALF)) + hidden * jnp.exp(-0.5 * hidden * hidden) * INV_ROOT_TAU

def round_half(values):
    return lax.optimization_barrier(values.astype(jnp.bfloat16)).astype(jnp.float32)

def contract_rows(left, right):
    return lax.dot_general(left, right, (((0,), (0,)), ((), ())), preferred_element_type=jnp.float32)

def contract_cols(left, right):
    return lax.dot_general(left, right, (((1,), (1,)), ((), ())), preferred_element_type=jnp.float32)

def adam_update(weight, gradient, first, second, decay, step_rate):
    first_new = BETA_FIRST * first + (1.0 - BETA_FIRST) * gradient
    second_new = BETA_SECOND * second + (1.0 - BETA_SECOND) * gradient * gradient
    first_hat = first_new / (1.0 - BETA_FIRST ** STEP)
    second_hat = second_new / (1.0 - BETA_SECOND ** STEP)
    weight_new = weight - step_rate * (first_hat / (jnp.sqrt(second_hat) + ADAM_EPSILON) + decay * weight)
    return (weight_new, first_new, second_new)

def attend_forward(query, keys, values, clip_row):
    count = query.shape[0]
    block = math.gcd(count, 512)
    key_full = keys.astype(jnp.float32)
    value_full = values.astype(jnp.float32)

    def one_block(index):
        start = index * block
        query_block = lax.dynamic_slice_in_dim(query, start, block, 0).astype(jnp.float32)
        id_block = lax.dynamic_slice_in_dim(clip_row, start, block, 0)
        allowed = (id_block[:, None] == clip_row[None, :])[None]
        scores = jnp.einsum('qhd,khd->hqk', query_block, key_full, precision=HIGHEST_MODE) * 0.125
        scores = jnp.where(allowed, scores, NEGATIVE_FILL)
        row_max = lax.optimization_barrier(jnp.max(scores, axis=2))
        portion = jnp.where(allowed, jnp.exp(scores - row_max[..., None]), 0.0)
        totals = lax.optimization_barrier(jnp.sum(portion, axis=2))
        mixed = jnp.einsum('hqk,khd->qhd', portion, value_full, precision=HIGHEST_MODE) / jnp.transpose(totals)[..., None]
        return (mixed, row_max + jnp.log(totals))
    mixed_all, lse_all = lax.map(one_block, jnp.arange(count // block, dtype=jnp.int32))
    return (mixed_all.reshape(count, H, DH), jnp.transpose(lse_all, (1, 0, 2)).reshape(H, count))

def attend_backward(query, keys, values, clip_row, lse, grad_heads, mixed_heads):
    count = query.shape[0]
    block = math.gcd(count, 512)
    key_full = keys.astype(jnp.float32)
    value_full = values.astype(jnp.float32)
    delta_all = lax.optimization_barrier(jnp.sum(grad_heads.astype(jnp.float32) * mixed_heads.astype(jnp.float32), axis=2))

    def one_block(carry, index):
        grad_keys, grad_values = carry
        start = index * block
        query_block = lax.dynamic_slice_in_dim(query, start, block, 0).astype(jnp.float32)
        grad_block = lax.dynamic_slice_in_dim(grad_heads, start, block, 0).astype(jnp.float32)
        id_block = lax.dynamic_slice_in_dim(clip_row, start, block, 0)
        delta_block = jnp.transpose(lax.dynamic_slice_in_dim(delta_all, start, block, 0))
        lse_block = lax.dynamic_slice_in_dim(lse, start, block, 1)
        allowed = (id_block[:, None] == clip_row[None, :])[None]
        scores = jnp.einsum('qhd,khd->hqk', query_block, key_full, precision=HIGHEST_MODE) * 0.125
        portion = jnp.where(allowed, jnp.exp(scores - lse_block[..., None]), 0.0)
        portion_half = round_half(portion)
        grad_values = grad_values + jnp.einsum('hqk,qhd->khd', portion_half, grad_block, precision=HIGHEST_MODE)
        portion_grad = jnp.einsum('qhd,khd->hqk', grad_block, value_full, precision=HIGHEST_MODE)
        score_grad = round_half(portion * (portion_grad - delta_block[..., None]) * 0.125)
        grad_query = jnp.einsum('hqk,khd->qhd', score_grad, key_full, precision=HIGHEST_MODE)
        grad_keys = grad_keys + jnp.einsum('hqk,qhd->khd', score_grad, query_block, precision=HIGHEST_MODE)
        return ((grad_keys, grad_values), grad_query)
    zeros = jnp.zeros((count, H, DH), jnp.float32)
    (grad_keys, grad_values), grad_query = lax.scan(one_block, (zeros, zeros), jnp.arange(count // block, dtype=jnp.int32))
    return (grad_query.reshape(count, H, DH), grad_keys, grad_values)

def layer_pass(inputs, clip_row, upstream, wide, small):
    count, width = inputs.shape
    gain_one, shift_one, bias_query, bias_value = (small[0], small[1], small[2], small[3])
    bias_out, gain_two, shift_two, bias_down = (small[4], small[5], small[6], small[7])
    bias_up = small[8:12].reshape(-1)
    w_qkv = wide[0][:, :3 * width]
    w_out = wide[0][:, 3 * width:]
    w_up = wide[1]
    w_down = wide[2]
    normed_one, inv_one, act_one = norm_forward(inputs, gain_one, shift_one)
    act_one = act_one.astype(jnp.bfloat16)
    projected = jnp.dot(act_one, w_qkv, preferred_element_type=jnp.float32)
    query = (projected[:, :width] + bias_query).astype(jnp.bfloat16).reshape(count, H, DH)
    keys = projected[:, width:2 * width].astype(jnp.bfloat16).reshape(count, H, DH)
    values = (projected[:, 2 * width:] + bias_value).astype(jnp.bfloat16).reshape(count, H, DH)
    mixed, lse = attend_forward(query, keys, values, clip_row)
    mixed_half = mixed.reshape(count, width).astype(jnp.bfloat16)
    resid = inputs + jnp.dot(mixed_half, w_out, preferred_element_type=jnp.float32) + bias_out
    normed_two, inv_two, act_two = norm_forward(resid, gain_two, shift_two)
    act_two = act_two.astype(jnp.bfloat16)
    hidden = jnp.dot(act_two, w_up, preferred_element_type=jnp.float32) + bias_up
    hidden_half = gelu_value(hidden).astype(jnp.bfloat16)
    output = resid + contract_cols(hidden_half, w_down) + bias_down
    upstream_half = upstream.astype(jnp.bfloat16)
    grad_down = contract_rows(upstream_half, hidden_half)
    grad_bias_down = lax.optimization_barrier(jnp.sum(upstream, axis=0))
    grad_hidden = jnp.dot(upstream_half, w_down, preferred_element_type=jnp.float32) * gelu_slope(hidden)
    grad_hidden_half = grad_hidden.astype(jnp.bfloat16)
    grad_up = contract_rows(act_two, grad_hidden_half)
    grad_bias_up = lax.optimization_barrier(jnp.sum(grad_hidden, axis=0))
    grad_act_two = contract_cols(grad_hidden_half, w_up)
    grad_norm_two, grad_gain_two, grad_shift_two = norm_backward(grad_act_two, normed_two, inv_two, gain_two)
    grad_resid = upstream + grad_norm_two
    resid_half = grad_resid.astype(jnp.bfloat16)
    grad_out = contract_rows(mixed_half, resid_half)
    grad_bias_out = lax.optimization_barrier(jnp.sum(grad_resid, axis=0))
    grad_mixed = contract_cols(resid_half, w_out).astype(jnp.bfloat16).reshape(count, H, DH)
    grad_query, grad_keys, grad_values = attend_backward(query, keys, values, clip_row, lse, grad_mixed, mixed_half.reshape(count, H, DH))
    grad_proj = jnp.concatenate([grad_query.reshape(count, width), grad_keys.reshape(count, width), grad_values.reshape(count, width)], axis=1)
    grad_proj_half = grad_proj.astype(jnp.bfloat16)
    grad_qkv = contract_rows(act_one, grad_proj_half)
    grad_bias_query = lax.optimization_barrier(jnp.sum(grad_query.reshape(count, width), axis=0))
    grad_bias_value = lax.optimization_barrier(jnp.sum(grad_values.reshape(count, width), axis=0))
    grad_act_one = contract_cols(grad_proj_half, w_qkv)
    grad_norm_one, grad_gain_one, grad_shift_one = norm_backward(grad_act_one, normed_one, inv_one, gain_one)
    grad_inputs = grad_resid + grad_norm_one
    grad_wide = jnp.stack([jnp.concatenate([grad_qkv, grad_out], axis=1), grad_up, grad_down])
    grad_small = jnp.concatenate([jnp.stack([grad_gain_one, grad_shift_one, grad_bias_query, grad_bias_value, grad_bias_out, grad_gain_two, grad_shift_two, grad_bias_down]), grad_bias_up.reshape(4, width)], axis=0)
    return (output, grad_inputs, grad_wide, grad_small)

def reference(frames, clip_ids, cotangent, mats, smalls, mats_m, mats_v, smalls_m, smalls_v):
    wide = mats.astype(jnp.bfloat16)
    small = smalls.astype(jnp.bfloat16).astype(jnp.float32)

    def one_group(carry, batch):
        inputs, clip_row, upstream = batch
        output, grad_inputs, grad_wide, grad_small = layer_pass(inputs, clip_row, upstream, wide, small)
        return ((carry[0] + grad_wide, carry[1] + grad_small), (output, grad_inputs))
    start_sums = (jnp.zeros(mats.shape, jnp.float32), jnp.zeros(smalls.shape, jnp.float32))
    (mats_grad, smalls_grad), (out_frames, frames_grad) = lax.scan(one_group, start_sums, (frames, clip_ids, cotangent))
    new_mats, new_mats_m, new_mats_v = adam_update(mats, mats_grad, mats_m, mats_v, WEIGHT_DECAY, LEARN_RATE)
    new_smalls, new_smalls_m, new_smalls_v = adam_update(smalls, smalls_grad, smalls_m, smalls_v, 0.0, SMALL_RATE)
    return (out_frames, frames_grad, mats_grad, smalls_grad, new_mats, new_smalls, new_mats_m, new_mats_v, new_smalls_m, new_smalls_v)
```

```python
import functools

import jax
import jax.numpy as jnp
from jax import lax
from jax.experimental import pallas as pl
from jax.experimental.pallas import tpu as pltpu
from jax.sharding import PartitionSpec as P


H = 12
DH = 64
STEP = 3
LANES = 128

NEGATIVE_FILL = -1e30
NORM_EPSILON = 1e-05
ROOT_HALF = 0.7071067811865476
INV_ROOT_TAU = 0.3989422804014327
LOG2E = 1.4426950408889634
BETA_FIRST = 0.9
BETA_SECOND = 0.95
LEARN_RATE = 0.01
SMALL_RATE = 0.1
WEIGHT_DECAY = 0.1
ADAM_EPSILON = 1e-08


F32 = jnp.float32
BF16 = jnp.bfloat16


def contract_rows(left, right):
    return lax.dot_general(left, right, (((0,), (0,)), ((), ())), preferred_element_type=F32)


def contract_cols(left, right):
    return lax.dot_general(left, right, (((1,), (1,)), ((), ())), preferred_element_type=F32)


def product(left, right):
    return jnp.dot(left, right, preferred_element_type=F32)


def normalize(values):
    row_mean = jnp.mean(values, axis=-1, keepdims=True)
    center = values - row_mean
    row_var = jnp.mean(center * center, axis=-1, keepdims=True)
    inv_std = lax.rsqrt(row_var + NORM_EPSILON)
    return center * inv_std, inv_std


def norm_backward(incoming, normed, inv_std, gain_vec):
    scaled = incoming * gain_vec
    return inv_std * (
        scaled
        - jnp.mean(scaled, axis=-1, keepdims=True)
        - normed * jnp.mean(scaled * normed, axis=-1, keepdims=True)
    )


def adam_update(weight, gradient, first, second, decay, step_rate):
    first_new = BETA_FIRST * first + (1.0 - BETA_FIRST) * gradient
    second_new = BETA_SECOND * second + (1.0 - BETA_SECOND) * gradient * gradient
    first_hat = first_new / (1.0 - BETA_FIRST**STEP)
    second_hat = second_new / (1.0 - BETA_SECOND**STEP)
    weight_new = weight - step_rate * (
        first_hat / (jnp.sqrt(second_hat) + ADAM_EPSILON) + decay * weight
    )
    return (weight_new, first_new, second_new)


def turn(block, step=1):
    count = lax.axis_size("seq")
    return lax.ppermute(block, "seq", [(i, (i + step) % count) for i in range(count)])


def swap(block, bit):
    count = lax.axis_size("dp")
    return lax.ppermute(block, "dp", [(i, i ^ bit) for i in range(count)])


def tuned():
    return lax.axis_size("dp") == 8 and lax.axis_size("seq") == 4


def call(kernel, here, ins, in_specs, out_shapes, out_specs, grid=(1,), scratch=(), limit=None, cost=None):
    return pl.pallas_call(
        kernel,
        grid_spec=pltpu.PrefetchScalarGridSpec(
            num_scalar_prefetch=1,
            grid=grid,
            in_specs=in_specs,
            out_specs=out_specs,
            scratch_shapes=list(scratch),
        ),
        out_shape=out_shapes,
        compiler_params=pltpu.CompilerParams(vmem_limit_bytes=limit),
        cost_estimate=cost,
    )(here, *ins)


def whole_block(shape):
    return pl.BlockSpec(shape, lambda *_: (0,) * len(shape), pipeline_mode=pl.Buffered(1))


def struct(shape, dtype):
    return jax.ShapeDtypeStruct(shape, dtype)


def far_struct(shape, dtype):
    return pltpu.HBM(shape, dtype)


def far(*arrays):
    return [pltpu.with_memory_space_constraint(array, pltpu.HBM) for array in arrays]


def pack_kernel(here_ref, *refs):
    *pieces, out = refs
    ring = len(pieces)
    for step, piece in enumerate(pieces):
        place = lax.rem(here_ref[1] - step + ring, ring)
        out[pl.ds(place, 1)] = piece[...][None]


def gather_pieces(shard, here, direct):
    ring = lax.axis_size("seq")
    rows, columns = shard.shape
    if not tuned():
        return [(lax.all_gather(shard, ("dp", "seq"), axis=0, tiled=True), None, 0)]
    pieces = [shard]
    for step in range(1, ring):
        if direct:
            pieces.append(turn(shard, step))
        else:
            pieces.append(turn(pieces[-1]))
    block = call(
        pack_kernel,
        here,
        pieces,
        [whole_block((rows, columns))] * ring,
        struct((ring, rows, columns), shard.dtype),
        whole_block((ring, rows, columns)),
    ).reshape(ring * rows, columns)
    half = ring * rows // 2
    from_x = swap(block, 2)
    from_y = swap(block, 4)
    low = swap(from_x[:half], 4)
    high = swap(from_y[half:], 2)
    held = [(block, 0, 0), (from_x, 2, 0), (from_y, 4, 0), (low, 6, 0), (high, 6, half)]
    other = [
        (swap(piece, 1), xor ^ 1, first)
        for piece, xor, first in held
    ]
    return held + other


def first_row(here_ref, block_rows, xor, first):
    if xor is None:
        return 0
    return pl.multiple_of((here_ref[0] ^ xor) * block_rows + first, 8)


def assemble_kernel(block_rows, places, here_ref, *refs):
    *pieces, out, rows_out = refs
    for piece, (xor, first) in zip(pieces, places):
        start = first_row(here_ref, block_rows, xor, first)
        out[pl.ds(start, piece.shape[0]), :] = piece[...]
    rows_out[...] = jnp.transpose(out[:, out.shape[1] - LANES :].astype(F32))


def assemble(pieces, here, rows, block_rows):
    columns = pieces[0][0].shape[1]
    return call(
        functools.partial(assemble_kernel, block_rows, [p[1:] for p in pieces]),
        here,
        [p[0] for p in pieces],
        [whole_block(p[0].shape) for p in pieces],
        [struct((rows, columns), BF16), struct((LANES, rows), F32)],
        [whole_block((rows, columns)), whole_block((LANES, rows))],
        limit=12 << 20,
    )


def join_kernel(here_ref, own_ref, recv_ref, me, x_send, y_send, x_late, y_late):
    rows = me.shape[0]
    half = rows // 2

    def total(slot, first, count):
        part = pl.ds(slot * rows + first, count)
        return (own_ref[part, :].astype(F32) + recv_ref[part, :].astype(F32)).astype(BF16)

    me[...] = total(0, 0, rows)
    x_send[:half, :] = total(3, half, half)
    x_send[half:, :] = total(1, half, half)
    y_send[:half, :] = total(3, 0, half)
    y_send[half:, :] = total(2, 0, half)
    x_late[...] = total(1, 0, half)
    y_late[...] = total(2, half, half)


def close_kernel(ring, here_ref, me, x_early, y_early, x_late, y_late, *refs):
    *outs, total = refs
    half = me.shape[0] // 2
    rows = me.shape[0] // ring
    total[:half, :] = (
        me[:half, :].astype(F32) + y_early[half:, :].astype(F32) + x_late[...].astype(F32)
    )
    total[half:, :] = (
        me[half:, :].astype(F32) + x_early[half:, :].astype(F32) + y_late[...].astype(F32)
    )
    for step, out in enumerate(outs):
        place = lax.rem(here_ref[1] + step, ring)
        out[...] = total[pl.ds(pl.multiple_of(place * rows, 8), rows), :].astype(out.dtype)


def scatter_parts(own, away, here, tile):
    ring = lax.axis_size("seq")
    if not tuned():
        return [lax.psum_scatter(own, ("dp", "seq"), scatter_dimension=0, tiled=True).astype(F32)]
    count, columns = own.shape
    rows = count // 4
    half = rows // 2
    got = swap(away, 1)

    def spec(height):
        return pl.BlockSpec((height, tile), lambda j, *_: (0, j))

    grid = (columns // tile,)
    heights = (rows, rows, rows, half, half)
    me, x_send, y_send, x_late, y_late = call(
        join_kernel,
        here,
        [own, got],
        [spec(count)] * 2,
        [far_struct((rows, columns), BF16)]
        + [struct((height, columns), BF16) for height in heights[1:]],
        [spec(height) for height in heights],
        grid=grid,
        limit=18 << 20,
    )
    x_early = swap(x_send, 2)
    y_early = swap(y_send, 4)
    x_sum = (x_late.astype(F32) + y_early[:half].astype(F32)).astype(BF16)
    y_sum = (y_late.astype(F32) + x_early[:half].astype(F32)).astype(BF16)
    x_late = swap(x_sum, 2)
    y_late = swap(y_sum, 4)
    small = rows // ring
    terms = call(
        functools.partial(close_kernel, ring),
        here,
        [*far(me), x_early, y_early, x_late, y_late],
        [spec(height) for height in heights],
        [struct((small, columns), F32 if step == 0 else BF16) for step in range(ring)],
        [spec(small)] * ring,
        grid=grid,
        scratch=[pltpu.VMEM((rows, tile), F32)],
        limit=12 << 20,
    )
    return [terms[0]] + [turn(terms[step], step) for step in range(1, ring)]


def own_slots():
    if tuned():
        return [0, 2, 4, 6], [1, 3, 5, 7]
    return list(range(lax.axis_size("dp"))), []


def low_lanes(shape):
    return lax.broadcasted_iota(jnp.int32, shape, 1) < DH


def stack(refs):
    if len(refs) == 1:
        return refs[0][...]
    return jnp.concatenate([ref[...] for ref in refs], axis=0)


def id_mask(exts, rows, query_row):
    masks = []
    for ext in exts:
        key_ids = ext[rows : rows + 8, :rows].astype(F32)[0:1, :]
        key_ids = jnp.transpose(jnp.broadcast_to(key_ids, (LANES, rows)))
        masks.append(jnp.where(key_ids[:, 0:1] == query_row, 0.0, NEGATIVE_FILL))
    return masks[0] if len(masks) == 1 else jnp.concatenate(masks, axis=0)


def forward_kernel(count, first, last, here_ref, *refs):
    exts, refs = refs[:count], refs[count:]
    small_ref, wk_ref, wv_ref, bias_ref, qid_ref = refs[:5]
    refs = refs[5:]
    if first:
        wq_ref, refs = refs[0], refs[1:]
    else:
        q_ref, stat_ref, acc_ref = refs[:3]
        refs = refs[3:]
    k_outs, v_outs, refs = refs[:count], refs[count : 2 * count], refs[2 * count :]
    if first:
        q_out, refs = refs[0], refs[1:]
    out_ref, stat_out, act_ref, mask_ref = refs
    rows = qid_ref.shape[1]

    @pl.when(pl.program_id(0) == 0)
    def _():
        for index, ext in enumerate(exts):
            normed = ext[:rows, :].astype(F32)
            act_ref[index * rows : (index + 1) * rows, :] = (
                normed * small_ref[0:1, :] + small_ref[1:2, :]
            ).astype(BF16)
        mask_ref[...] = id_mask(exts, rows, qid_ref[0:1, :])

    both = product(act_ref[...], jnp.concatenate([wk_ref[...], wv_ref[...]], axis=1))
    keys = both[:, :LANES].astype(BF16)
    values = (both[:, LANES:] + bias_ref[3:4, :]).astype(BF16)
    for index in range(count):
        part = slice(index * rows, (index + 1) * rows)
        k_outs[index][...] = keys[part]
        v_outs[index][...] = values[part]
    if first:
        query = (product(act_ref[:rows, :], wq_ref[...]) + bias_ref[2:3, :]).astype(BF16)
        q_out[...] = query
    else:
        query = q_ref[...]
    low = low_lanes(query.shape)
    key_low = low_lanes(keys.shape)
    zero = jnp.zeros_like(query)
    one = jnp.ones_like(values)
    maxima, totals, mixes = [], [], []
    for head in range(2):
        here, there = slice(head * DH, (head + 1) * DH), (1 - head) * DH
        side = low if head == 0 else ~low
        key_side = key_low if head == 0 else ~key_low
        scores = contract_cols(keys, jnp.where(side, query, zero)) * (0.125 * LOG2E)
        scores = scores + mask_ref[...]
        top = jnp.max(scores, axis=0, keepdims=True)
        if not first:
            before = stat_ref[0, head : head + 1, :]
            top = jnp.maximum(top, before)
        portion = jnp.exp2(scores - top).astype(BF16)
        mixed = contract_rows(jnp.where(key_side, values, one), portion)
        total = mixed[there : there + 1, :]
        mixed = mixed[here, :]
        if not first:
            factor = jnp.exp2(before - top)
            total = total + stat_ref[0, 2 + head : 3 + head, :] * factor
            mixed = mixed + acc_ref[here, :] * factor
        maxima.append(top)
        totals.append(total)
        mixes.append(mixed / total if last else mixed)
    mixed = jnp.concatenate(mixes, axis=0)
    if last:
        out_ref[...] = jnp.transpose(mixed).astype(BF16)
        for head in range(2):
            stat_out[0, head : head + 1, :] = maxima[head] + jnp.log2(totals[head])
    else:
        out_ref[...] = mixed
        for head in range(2):
            stat_out[0, head : head + 1, :] = maxima[head]
            stat_out[0, 2 + head : 3 + head, :] = totals[head]


def forward_block(here, exts, small, w_all, query_row, query, state, last):
    count = len(exts)
    rows = query_row.shape[1]
    width = exts[0].shape[1]
    pairs = width // LANES
    first = state is None
    tile = pl.BlockSpec((rows, LANES), lambda j, *_: (0, j))
    flat = pl.BlockSpec((LANES, rows), lambda j, *_: (j, 0))
    stat = pl.BlockSpec((1, 4, rows), lambda j, *_: (j, 0, 0))

    def weight(part):
        return pl.BlockSpec((width, LANES), lambda j, *_: (0, part * pairs + j))

    in_specs = [whole_block(exts[0].shape)] * count + [
        pl.BlockSpec((8, width), lambda *_: (0, 0)),
        weight(1),
        weight(2),
        pl.BlockSpec((8, LANES), lambda j, *_: (0, j)),
        whole_block(query_row.shape),
    ]
    args = [*exts, small, w_all, w_all, small, query_row]
    half = far_struct((rows, width), BF16)
    out_shapes = [half] * (2 * count)
    if first:
        in_specs += [weight(0)]
        args += [w_all]
        out_shapes.append(half)
    else:
        in_specs += [tile, stat, flat]
        args += far(query, *state)
    out_specs = [tile] * len(out_shapes)
    out_shapes += [
        struct((rows, width), BF16) if last else far_struct((width, rows), F32),
        far_struct((pairs, 4, rows), F32),
    ]
    out_specs += [tile if last else flat, stat]
    result = call(
        functools.partial(forward_kernel, count, first, last),
        here,
        args,
        in_specs,
        out_shapes,
        out_specs,
        grid=(pairs,),
        scratch=[pltpu.VMEM((count * rows, width), BF16), pltpu.VMEM((count * rows, rows), F32)],
        limit=16 << 20,
        cost=pl.CostEstimate(
            flops=24 * count * rows * rows * width,
            bytes_accessed=8 * rows * width,
            transcendentals=count * rows * rows * H,
        ),
    )
    keys, values, rest = result[:count], result[count : 2 * count], result[2 * count :]
    if first:
        query, rest = rest[0], rest[1:]
    return keys, values, query, tuple(rest[::-1]) if not last else tuple(rest)


def backward_kernel(count, first, last, here_ref, *refs):
    q_ref, do_ref, o_ref, stat_ref, wk_ref, wv_ref, qid_ref = refs[:7]
    refs = refs[7:]
    exts, keys, values, refs = refs[:count], refs[count : 2 * count], refs[2 * count : 3 * count], refs[3 * count :]
    if not first:
        dq_ref, refs = refs[0], refs[1:]
    if last:
        wq_ref, refs = refs[0], refs[1:]
    dq_out, sum_ref, refs = refs[0], refs[1], refs[2:]
    dk_outs, dv_outs, parts, refs = refs[:count], refs[count : 2 * count], refs[2 * count : 3 * count], refs[3 * count :]
    (mask_ref,) = refs
    rows = q_ref.shape[0]

    @pl.when(pl.program_id(0) == 0)
    def _():
        mask_ref[...] = id_mask(exts, rows, qid_ref[0:1, :])
        for part in parts:
            part[...] = jnp.zeros_like(part)

    query = q_ref[...]
    grad = do_ref[...]
    keys = stack(keys)
    values = stack(values)
    low = low_lanes(query.shape)
    key_low = low_lanes(keys.shape)
    zero = jnp.zeros_like(query)
    flipped = jnp.transpose(grad.astype(F32) * o_ref[...].astype(F32))
    sides = (low, ~low)
    queries = [jnp.where(side, query, zero) for side in sides]
    grads = [jnp.where(side, grad, zero) for side in sides]
    all_scores = contract_cols(keys, jnp.concatenate(queries, axis=0))
    all_changes = contract_cols(values, jnp.concatenate(grads, axis=0))
    dk = dv = dq = None
    for head in range(2):
        span = slice(head * rows, (head + 1) * rows)
        delta = jnp.sum(flipped[head * DH : (head + 1) * DH, :], axis=0, keepdims=True)
        scores = all_scores[:, span] * (0.125 * LOG2E) + mask_ref[...]
        portion = jnp.exp2(scores - stat_ref[0, head : head + 1, :])
        score_grad = (portion * (all_changes[:, span] - delta)).astype(BF16)
        keys_here = jnp.where(key_low if head == 0 else ~key_low, keys, jnp.zeros_like(keys))
        dv_here = product(portion.astype(BF16), grads[head])
        dk_here = product(score_grad, queries[head])
        dq_here = contract_rows(score_grad, keys_here)
        if head == 0:
            dk, dv, dq = dk_here, dv_here, dq_here
        else:
            dk, dv, dq = dk + dk_here, dv + dv_here, dq + dq_here
    dk = (dk * 0.125).astype(BF16)
    dv = dv.astype(BF16)
    dq = dq * 0.125
    if not first:
        dq = dq + dq_ref[...]
    sum_ref[0:1, :] = jnp.sum(dk.astype(F32), axis=0, keepdims=True)
    sum_ref[1:2, :] = jnp.sum(dv.astype(F32), axis=0, keepdims=True)
    part = contract_cols(
        jnp.concatenate([dk, dv], axis=1), jnp.concatenate([wk_ref[...], wv_ref[...]], axis=1)
    )
    for index in range(count):
        span = slice(index * rows, (index + 1) * rows)
        dk_outs[index][...] = dk[span]
        dv_outs[index][...] = dv[span]
        term = part[span]
        if last and index == count - 1:
            dq = dq.astype(BF16)
            sum_ref[2:3, :] = jnp.sum(dq.astype(F32), axis=0, keepdims=True)
            term = term + contract_cols(dq, wq_ref[...])
        parts[index][...] += term
    dq_out[...] = dq


def backward_block(here, query, grad, mixed, stats, keys, values, w_all, query_row, exts, dq, last):
    count = len(exts)
    rows, width = query.shape
    pairs = width // LANES
    first = dq is None
    tile = pl.BlockSpec((rows, LANES), lambda j, *_: (0, j))

    def weight(part):
        return pl.BlockSpec((width, LANES), lambda j, *_: (0, part * pairs + j))

    in_specs = [
        tile,
        tile,
        tile,
        pl.BlockSpec((1, 4, rows), lambda j, *_: (j, 0, 0)),
        weight(1),
        weight(2),
        whole_block(query_row.shape),
    ]
    in_specs += [whole_block(exts[0].shape)] * count + [tile] * (2 * count)
    args = [*far(query), grad, mixed, *far(stats), w_all, w_all, query_row, *exts, *far(*keys, *values)]
    if not first:
        in_specs.append(tile)
        args += far(dq)
    if last:
        in_specs.append(weight(0))
        args.append(w_all)
    half = far_struct((rows, width), BF16)
    full = struct((rows, width), F32)
    result = call(
        functools.partial(backward_kernel, count, first, last),
        here,
        args,
        in_specs,
        [half if last else far_struct((rows, width), F32), struct((8, width), F32)] + [half] * (2 * count) + [full] * count,
        [tile, pl.BlockSpec((8, LANES), lambda j, *_: (0, j))]
        + [tile] * (2 * count)
        + [whole_block((rows, width))] * count,
        grid=(pairs,),
        scratch=[pltpu.VMEM((count * rows, rows), F32)],
        limit=16 << 20,
        cost=pl.CostEstimate(
            flops=40 * count * rows * rows * width,
            bytes_accessed=16 * rows * width,
            transcendentals=count * rows * rows * H,
        ),
    )
    dq, sums, rest = result[0], result[1], result[2:]
    return dq, sums, rest[:count], rest[count : 2 * count], rest[2 * count :]


def transposed_slots(here_ref, values, slots, block_rows, plain_ref, out_ref):
    plain_ref[...] = jnp.transpose(values.astype(F32)).astype(BF16)
    for index, xor in enumerate(slots):
        start = pl.multiple_of((here_ref[0] ^ xor) * block_rows, 8)
        out_ref[index * block_rows : (index + 1) * block_rows, :] = plain_ref[pl.ds(start, block_rows), :]


def middle_kernel(places, block_rows, slots, kept, tile, here_ref, *refs):
    count = len(places)
    frames_ref, mixed_ref, cot_ref, small_ref = refs[:4]
    pieces, refs = refs[4 : 4 + count], refs[4 + count :]
    out_ref, dr_ref, doh_ref, sum_ref = refs[:4]
    grads, refs = refs[4 : 4 + len(kept)], refs[4 + len(kept) :]
    (
        w_ref,
        stage_ref,
        last_ref,
        normed_ref,
        back_ref,
        act_ref,
        half_ref,
        act_flip,
        half_flip,
        plain_ref,
        bias_ref,
        bias_sum,
        in_sems,
        out_sems,
        last_sems,
    ) = refs
    width = frames_ref.shape[1]
    hidden = bias_ref.shape[1]

    copies = []
    for index, (piece, (xor, first, column)) in enumerate(zip(pieces, places)):
        start = first_row(here_ref, block_rows, xor, first)
        height, span = piece.shape
        target = w_ref.at[pl.ds(start, height), column : column + span]
        copies.append(pltpu.make_async_copy(piece, target, in_sems.at[index]))
    for copy in copies:
        copy.start()
    cot = cot_ref[...]
    half_ref[...] = cot.astype(BF16)
    transposed_slots(here_ref, half_ref[...], slots, block_rows, plain_ref, half_flip)
    for index in range(4):
        bias_ref[:, index * width : (index + 1) * width] = small_ref[8 + index : 9 + index, :]
    sum_ref[3:4, :] = jnp.sum(cot, axis=0, keepdims=True)
    for copy in copies:
        copy.wait()

    resid = frames_ref[...] + product(mixed_ref[...], w_ref[:, :width]) + small_ref[4:5, :]
    normed, inv_std = normalize(resid)
    normed_ref[...] = normed
    act_ref[...] = (normed * small_ref[5:6, :] + small_ref[6:7, :]).astype(BF16)
    out_ref[...] = resid + small_ref[7:8, :]
    back_ref[...] = jnp.zeros_like(back_ref)
    transposed_slots(here_ref, act_ref[...], slots, block_rows, plain_ref, act_flip)

    def send(source, column, start, size, sems):
        moves = []
        first = 0
        for index, (grad, height) in enumerate(zip(grads, kept)):
            moves.append(
                pltpu.make_async_copy(
                    source.at[first : first + height, column : column + size],
                    grad.at[:, pl.ds(start, size)],
                    sems.at[index],
                )
            )
            first += height
        return moves

    tiles = hidden // tile

    def columns(index):
        up = pl.multiple_of(width + index * tile, LANES)
        down = pl.multiple_of(width + hidden + index * tile, LANES)
        return up, down, pl.multiple_of(index * tile, LANES)

    def moves_of(index):
        up, down, _ = columns(index)
        slot = lax.rem(index, 2)
        stage = stage_ref.at[slot]
        return send(stage, 0, up, tile, out_sems.at[slot, 0]) + send(
            stage, tile, down, tile, out_sems.at[slot, 1]
        )

    def body(index, carry):
        up, down, at = columns(index)
        slot = lax.rem(index, 2)

        @pl.when(index >= 2)
        def _():
            for move in moves_of(index - 2):
                move.wait()

        w_up = w_ref[:, pl.ds(up, tile)]
        w_down = w_ref[:, pl.ds(down, tile)]
        u = product(act_ref[...], w_up) + bias_ref[:, pl.ds(at, tile)]
        rise = 0.5 * (1.0 + lax.erf(u * ROOT_HALF))
        slope = rise + u * jnp.exp(-0.5 * u * u) * INV_ROOT_TAU
        value = (u * rise).astype(BF16)
        out_ref[...] += contract_cols(value, w_down)
        du = product(half_ref[...], w_down) * slope
        bias_sum[:, pl.ds(at, tile)] = jnp.sum(du, axis=0, keepdims=True)
        du = du.astype(BF16)
        back_ref[...] += contract_cols(du, w_up)
        stage_ref[slot, :, :tile] = product(act_flip[...], du).astype(BF16)
        stage_ref[slot, :, tile:] = product(half_flip[...], value).astype(BF16)
        for move in moves_of(index):
            move.start()
        return carry

    lax.fori_loop(0, tiles, body, 0)

    incoming = back_ref[...]
    normed = normed_ref[...]
    dr = cot_ref[...] + norm_backward(incoming, normed, inv_std, small_ref[5:6, :])
    dr_ref[...] = dr
    sum_ref[0:1, :] = jnp.sum(dr, axis=0, keepdims=True)
    sum_ref[1:2, :] = jnp.sum(incoming * normed, axis=0, keepdims=True)
    sum_ref[2:3, :] = jnp.sum(incoming, axis=0, keepdims=True)
    for index in range(4):
        sum_ref[4 + index : 5 + index, :] = bias_sum[:, index * width : (index + 1) * width]
    drh = dr.astype(BF16)
    transposed_slots(here_ref, mixed_ref[...], slots, block_rows, plain_ref, act_flip)
    last_ref[...] = product(act_flip[...], drh).astype(BF16)
    finals = send(last_ref, 0, 0, width, last_sems)
    for move in finals:
        move.start()
    doh_ref[...] = contract_cols(drh, w_ref[:, :width]).astype(BF16)
    for index in range(max(tiles - 2, 0), tiles):
        finals = finals + moves_of(jnp.int32(index))
    for move in finals:
        move.wait()


def middle(here, frames, mixed, cot, small, pieces, rows_total, block_rows):
    rows, width = frames.shape
    starts = [0, pieces[0][0][0].shape[1]]
    columns = starts[1] + pieces[1][0][0].shape[1]
    pieces = [(*piece, start) for part, start in zip(pieces, starts) for piece in part]
    hidden = (columns - width) // 2
    tile = 2 * LANES
    kept, given = own_slots()
    heights = [len(part) * block_rows for part in (kept, given) if part]
    anywhere = pl.BlockSpec(memory_space=pl.ANY)
    full = whole_block((rows, width))
    outs = [struct((rows, width), F32), struct((rows, width), F32), struct((rows, width), BF16), struct((8, width), F32)]
    return call(
        functools.partial(
            middle_kernel, [p[1:] for p in pieces], block_rows, kept + given, heights, tile
        ),
        here,
        [frames, mixed, cot, small, *[p[0] for p in pieces]],
        [full, full, full, pl.BlockSpec((16, width), lambda *_: (0, 0))] + [anywhere] * len(pieces),
        outs + [struct((height, columns), BF16) for height in heights],
        [full, full, full, whole_block((8, width))] + [anywhere] * len(heights),
        scratch=[
            pltpu.VMEM((rows_total, columns), BF16),
            pltpu.VMEM((2, rows_total, 2 * tile), BF16),
            pltpu.VMEM((rows_total, width), BF16),
            pltpu.VMEM((rows, width), F32),
            pltpu.VMEM((rows, width), F32),
            pltpu.VMEM((rows, width), BF16),
            pltpu.VMEM((rows, width), BF16),
            pltpu.VMEM((width, rows), BF16),
            pltpu.VMEM((width, rows), BF16),
            pltpu.VMEM((width, rows), BF16),
            pltpu.VMEM((1, hidden), F32),
            pltpu.VMEM((1, hidden), F32),
            pltpu.SemaphoreType.DMA((len(pieces),)),
            pltpu.SemaphoreType.DMA((2, 2, len(heights))),
            pltpu.SemaphoreType.DMA((len(heights),)),
        ],
        limit=30 << 20,
        cost=pl.CostEstimate(
            flops=36 * rows * width * hidden // 3, bytes_accessed=4 * rows_total * columns, transcendentals=2 * rows * hidden
        ),
    )


def cross_kernel(ring, sum_count, slots, block_rows, heights, tile, here_ref, *refs):
    exts, refs = refs[:ring], refs[ring:]
    dq_ref, refs = refs[0], refs[1:]
    dks, dvs, refs = refs[:ring], refs[ring : 2 * ring], refs[2 * ring :]
    sums, refs = refs[:sum_count], refs[sum_count:]
    mid_ref, w_ref, cols_ref, refs = refs[0], refs[1], refs[2], refs[3:]
    outs, refs = refs[: len(heights)], refs[len(heights) :]
    flip_ref, plain_ref, cross_ref, line_ref, gain_ref, shift_ref, side_ref, turned_ref = refs
    step = pl.program_id(0)
    rows = dq_ref.shape[0]
    width = plain_ref.shape[0]
    third = width // tile

    def slot_rows(index):
        start = pl.multiple_of((here_ref[0] ^ slots[index]) * block_rows, 8)
        return pl.ds(start, block_rows), pl.ds(index * block_rows, block_rows)

    @pl.when(step == 0)
    def _():
        for index in range(ring):
            plain_ref[...] = jnp.transpose(exts[index][:rows, :].astype(F32)).astype(BF16)
            for slot in range(len(slots)):
                source, target = slot_rows(slot)
                flip_ref[target, index * rows : (index + 1) * rows] = plain_ref[source, :]
        for slot in range(len(slots)):
            source, target = slot_rows(slot)
            side = cols_ref[source, :].astype(F32)
            side_ref[target, :] = jnp.broadcast_to(side[:, 0:1], side.shape)
            turned_ref[target, :] = jnp.broadcast_to(side[:, 1:2], side.shape)
        gain_ref[...] = jnp.zeros_like(gain_ref)
        shift_ref[...] = jnp.zeros_like(shift_ref)

    def line(row, offset):
        total = sums[0][row : row + 1, pl.ds(offset, tile)]
        for other in sums[1:]:
            total = total + other[row : row + 1, pl.ds(offset, tile)]
        return total

    @pl.when(step < third)
    def _():
        cross_ref[...] = product(flip_ref[:, :rows], dq_ref[...])
        line_ref[...] = sums[-1][2:3, pl.ds(pl.multiple_of(step * tile, LANES), tile)]

    for begin, row, terms in ((third, 0, dks), (2 * third, 1, dvs)):

        @pl.when((step >= begin) & (step < begin + third))
        def _(begin=begin, row=row, terms=terms):
            total = product(flip_ref[:, :rows], terms[0][...])
            for index in range(1, ring):
                total += product(flip_ref[:, index * rows : (index + 1) * rows], terms[index][...])
            cross_ref[...] = total
            line_ref[...] = line(row, pl.multiple_of((step - begin) * tile, LANES))

    first = 0
    at = pl.multiple_of(step * tile, LANES)
    for index in range(len(slots)):
        source, target = slot_rows(index)
        part = cross_ref[target, :]
        weight = w_ref[source, :].astype(F32)
        gain = jnp.tile(side_ref[target, :], (1, tile // LANES))
        shift = jnp.tile(turned_ref[target, :], (1, tile // LANES))
        scaled = weight * part
        shifted = weight * line_ref[...]
        gain_ref[target, :] += sum(scaled[:, i : i + LANES] for i in range(0, tile, LANES))
        shift_ref[target, :] += sum(shifted[:, i : i + LANES] for i in range(0, tile, LANES))
        grad = (gain * part + shift * line_ref[...]).astype(BF16)
        out = 0 if index * block_rows < heights[0] else 1
        first = index * block_rows - (heights[0] if out else 0)
        outs[out][first : first + block_rows, pl.ds(at, tile)] = grad

    @pl.when(step == 3 * third - 1)
    def _():
        zero = jnp.zeros((2, width), F32)
        total_value = sums[0][1:2, :]
        for other in sums[1:]:
            total_value = total_value + other[1:2, :]
        lines = jnp.concatenate([zero, sums[-1][2:3, :], total_value, mid_ref[...]], axis=0)
        lines = jnp.concatenate([lines, jnp.zeros((LANES - 12, width), F32)], axis=0)
        turned_ref[...] = jnp.transpose(lines)
        lane = lax.broadcasted_iota(jnp.int32, (block_rows, LANES), 1)
        for index in range(len(slots)):
            source, target = slot_rows(index)
            gain = jnp.sum(gain_ref[target, :], axis=1, keepdims=True)
            shift = jnp.sum(shift_ref[target, :], axis=1, keepdims=True)
            value = jnp.where(lane == 0, gain, jnp.where(lane == 1, shift, turned_ref[source, :]))
            out = 0 if index * block_rows < heights[0] else 1
            start = index * block_rows - (heights[0] if out else 0)
            outs[out][start : start + block_rows, 3 * width :] = value.astype(BF16)


def cross(here, exts, dq, dks, dvs, sums, mid_sums, w_all, block_rows):
    ring = len(exts)
    rows, width = dq.shape
    tile = 2 * LANES
    third = width // tile
    kept, given = own_slots()
    heights = [len(part) * block_rows for part in (kept, given) if part]
    columns = w_all.shape[1]

    def spec(begin):
        return pl.BlockSpec((rows, tile), lambda j, *_: (0, jnp.clip(j - begin, 0, third - 1)))

    return call(
        functools.partial(cross_kernel, ring, len(sums), kept + given, block_rows, heights, tile),
        here,
        [*exts, *far(dq, *dks, *dvs), *sums, mid_sums, w_all, w_all],
        [whole_block(exts[0].shape)] * ring
        + [spec(0)]
        + [spec(third)] * ring
        + [spec(2 * third)] * ring
        + [whole_block((8, width))] * (len(sums) + 1)
        + [
            pl.BlockSpec((width, tile), lambda j, *_: (0, j)),
            pl.BlockSpec((width, LANES), lambda *_: (0, 3 * width // LANES)),
        ],
        [struct((height, columns), BF16) for height in heights],
        [whole_block((height, columns)) for height in heights],
        grid=(3 * third,),
        scratch=[
            pltpu.VMEM((width, ring * rows), BF16),
            pltpu.VMEM((width, rows), BF16),
            pltpu.VMEM((width, tile), F32),
            pltpu.VMEM((1, tile), F32),
            pltpu.VMEM((width, LANES), F32),
            pltpu.VMEM((width, LANES), F32),
            pltpu.VMEM((width, LANES), F32),
            pltpu.VMEM((width, LANES), F32),
        ],
        limit=20 << 20,
        cost=pl.CostEstimate(
            flops=2 * rows * width * width * (2 * ring + 1), bytes_accessed=2 * width * columns * 3, transcendentals=0
        ),
    )


def update_kernel(counts, width, *refs):
    wide_terms, refs = refs[: counts[0]], refs[counts[0] :]
    cross_terms, refs = refs[: counts[1]], refs[counts[1] :]
    weight, first, second, grad_out, weight_out, first_out, second_out = refs

    def total(terms, start, stop):
        value = terms[0][:, start:stop].astype(F32)
        for term in terms[1:]:
            value = value + term[:, start:stop].astype(F32)
        return value

    hidden = weight.shape[2]
    spans = (
        (0, 0, cross_terms, 0, 3 * width),
        (0, 3 * width, wide_terms, 0, width),
        (1, 0, wide_terms, width, hidden),
        (2, 0, wide_terms, width + hidden, hidden),
    )
    for matrix, column, terms, start, size in spans:
        grad = total(terms, start, start + size)
        at = slice(column, column + size)
        new_weight, new_first, new_second = adam_update(
            weight[matrix, :, at], grad, first[matrix, :, at], second[matrix, :, at], WEIGHT_DECAY, LEARN_RATE
        )
        grad_out[matrix, :, at] = grad
        weight_out[matrix, :, at] = new_weight
        first_out[matrix, :, at] = new_first
        second_out[matrix, :, at] = new_second


def update(wide_terms, cross_terms, width, mats, mats_m, mats_v):
    terms = [*wide_terms, *cross_terms]
    block = whole_block(mats.shape)
    return pl.pallas_call(
        functools.partial(update_kernel, (len(wide_terms), len(cross_terms)), width),
        grid=(1,),
        in_specs=[whole_block(term.shape) for term in terms] + [block] * 3,
        out_specs=[block] * 4,
        out_shape=[struct(mats.shape, F32)] * 4,
        compiler_params=pltpu.CompilerParams(vmem_limit_bytes=20 << 20),
        name="update",
    )(*terms, mats, mats_m, mats_v)


def groups(ring):
    ahead = [[i] for i in range(ring)]
    order = list(range(1, ring)) + [0]
    return ahead, [[i] for i in order]


def shards(frames, clip_ids, cotangent, mats, smalls, mats_m, mats_v, smalls_m, smalls_v):
    inputs = frames[0]
    upstream = cotangent[0]
    tok_rows, width = inputs.shape
    ring = lax.axis_size("seq")
    devices = ring * lax.axis_size("dp")
    block_rows = ring * mats.shape[1]
    total_rows = devices * mats.shape[1]
    here_dp = lax.axis_index("dp") if tuned() else jnp.int32(0)
    here = jnp.stack([here_dp, lax.axis_index("seq")]).astype(jnp.int32)

    normed_one, inv_one = normalize(inputs)
    id_row = clip_ids.astype(F32)
    id_rows = jnp.pad(id_row, ((0, 7), (0, width - tok_rows))).astype(BF16)
    piece = jnp.concatenate([normed_one.astype(BF16), id_rows], axis=0)
    normed_one, inv_one, piece = lax.optimization_barrier((normed_one, inv_one, piece))
    exts = [piece]
    for _ in range(1, ring):
        exts.append(turn(exts[-1]))

    mats_half = mats.astype(BF16)
    small_columns = jnp.pad(
        jnp.transpose(smalls.astype(BF16).astype(F32)), ((0, 0), (0, LANES - smalls.shape[0]))
    ).astype(BF16)
    chunk = jnp.concatenate([mats_half[0][:, : 3 * width], small_columns], axis=1)
    w_all, small = assemble(gather_pieces(chunk, here, True), here, total_rows, block_rows)
    chunk = jnp.concatenate([mats_half[0][:, 3 * width :], mats_half[1]], axis=1)
    wide_pieces = [gather_pieces(chunk, here, False), gather_pieces(mats_half[2], here, False)]

    query, state = None, None
    keys, values = [None] * ring, [None] * ring
    ahead, back = groups(ring)
    for group in ahead:
        new_keys, new_values, query, state = forward_block(
            here, [exts[i] for i in group], small, w_all, id_row, query, state, group is ahead[-1]
        )
        for index, key, value in zip(group, new_keys, new_values):
            keys[index], values[index] = key, value
    mixed_half, stats = state

    output, grad_resid, grad_heads, mid_sums, *wide_grads = middle(
        here, inputs, mixed_half, upstream, small, wide_pieces, total_rows, block_rows
    )
    wide_terms = scatter_parts(wide_grads[0], wide_grads[-1], here, 3 * width)

    dq = None
    riding = None
    dks, dvs, sums = [None] * ring, [None] * ring, []
    for group in back:
        dq, some, new_dks, new_dvs, parts = backward_block(
            here,
            query,
            grad_heads,
            mixed_half,
            stats,
            [keys[i] for i in group],
            [values[i] for i in group],
            w_all,
            id_row,
            [exts[i] for i in group],
            dq,
            group is back[-1],
        )
        sums.append(some)
        for index, dk, dv, part in zip(group, new_dks, new_dvs, parts):
            dks[index], dvs[index] = dk, dv
            if riding is not None:
                part = part + riding.astype(F32)
            if index:
                riding = turn(part.astype(BF16))
            else:
                grad_act_one = part

    cross_grads = cross(here, exts, dq, dks, dvs, sums, mid_sums, w_all, block_rows)
    cross_terms = scatter_parts(cross_grads[0], cross_grads[-1], here, w_all.shape[1])
    grad_inputs = grad_resid + norm_backward(grad_act_one, normed_one, inv_one, small[0])

    mats_grad, new_mats, new_mats_m, new_mats_v = update(
        wide_terms, cross_terms, width, mats, mats_m, mats_v
    )
    smalls_grad = jnp.transpose(
        sum(term[:, 3 * width : 3 * width + smalls.shape[0]].astype(F32) for term in cross_terms)
    )
    new_smalls, new_smalls_m, new_smalls_v = adam_update(
        smalls, smalls_grad, smalls_m, smalls_v, 0.0, SMALL_RATE
    )
    return (
        output[None],
        grad_inputs[None],
        mats_grad,
        smalls_grad,
        new_mats,
        new_smalls,
        new_mats_m,
        new_mats_v,
        new_smalls_m,
        new_smalls_v,
    )


def solution(mesh):
    in_specs = (
        P("dp", "seq", None),
        P("dp", "seq"),
        P("dp", "seq", None),
        P(None, ("dp", "seq"), None),
        P(None, ("dp", "seq")),
        P(None, ("dp", "seq"), None),
        P(None, ("dp", "seq"), None),
        P(None, ("dp", "seq")),
        P(None, ("dp", "seq")),
    )
    out_specs = (
        P("dp", "seq", None),
        P("dp", "seq", None),
        P(None, ("dp", "seq"), None),
        P(None, ("dp", "seq")),
        P(None, ("dp", "seq"), None),
        P(None, ("dp", "seq")),
        P(None, ("dp", "seq"), None),
        P(None, ("dp", "seq"), None),
        P(None, ("dp", "seq")),
        P(None, ("dp", "seq")),
    )

    return jax.shard_map(shards, mesh=mesh, in_specs=in_specs, out_specs=out_specs, check_vma=False)
```

```python
import functools

import jax
import jax.numpy as jnp
from jax import lax
from jax.experimental import pallas as pl
from jax.experimental.pallas import tpu as pltpu
from jax.sharding import PartitionSpec as P


H = 12
DH = 64
STEP = 3
LANES = 128

NEGATIVE_FILL = -1e30
NORM_EPSILON = 1e-05
ROOT_HALF = 0.7071067811865476
INV_ROOT_TAU = 0.3989422804014327
LOG2E = 1.4426950408889634
BETA_FIRST = 0.9
BETA_SECOND = 0.95
LEARN_RATE = 0.01
SMALL_RATE = 0.1
WEIGHT_DECAY = 0.1
ADAM_EPSILON = 1e-08


F32 = jnp.float32
BF16 = jnp.bfloat16


def contract_rows(left, right):
    return lax.dot_general(left, right, (((0,), (0,)), ((), ())), preferred_element_type=F32)


def contract_cols(left, right):
    return lax.dot_general(left, right, (((1,), (1,)), ((), ())), preferred_element_type=F32)


def product(left, right):
    return jnp.dot(left, right, preferred_element_type=F32)


def normalize(values):
    row_mean = jnp.mean(values, axis=-1, keepdims=True)
    center = values - row_mean
    row_var = jnp.mean(center * center, axis=-1, keepdims=True)
    inv_std = lax.rsqrt(row_var + NORM_EPSILON)
    return center * inv_std, inv_std


def norm_backward(incoming, normed, inv_std, gain_vec):
    scaled = incoming * gain_vec
    return inv_std * (
        scaled
        - jnp.mean(scaled, axis=-1, keepdims=True)
        - normed * jnp.mean(scaled * normed, axis=-1, keepdims=True)
    )


def adam_update(weight, gradient, first, second, decay, step_rate):
    first_new = BETA_FIRST * first + (1.0 - BETA_FIRST) * gradient
    second_new = BETA_SECOND * second + (1.0 - BETA_SECOND) * gradient * gradient
    first_hat = first_new / (1.0 - BETA_FIRST**STEP)
    second_hat = second_new / (1.0 - BETA_SECOND**STEP)
    weight_new = weight - step_rate * (
        first_hat / (jnp.sqrt(second_hat) + ADAM_EPSILON) + decay * weight
    )
    return (weight_new, first_new, second_new)


def turn(block, step=1):
    count = lax.axis_size("seq")
    return lax.ppermute(block, "seq", [(i, (i + step) % count) for i in range(count)])


def swap(block, bit):
    count = lax.axis_size("dp")
    return lax.ppermute(block, "dp", [(i, i ^ bit) for i in range(count)])


def tuned():
    return lax.axis_size("dp") == 8 and lax.axis_size("seq") == 4


def call(kernel, here, ins, in_specs, out_shapes, out_specs, grid=(1,), scratch=(), limit=None, cost=None):
    return pl.pallas_call(
        kernel,
        grid_spec=pltpu.PrefetchScalarGridSpec(
            num_scalar_prefetch=1,
            grid=grid,
            in_specs=in_specs,
            out_specs=out_specs,
            scratch_shapes=list(scratch),
        ),
        out_shape=out_shapes,
        compiler_params=pltpu.CompilerParams(vmem_limit_bytes=limit),
        cost_estimate=cost,
    )(here, *ins)


def whole_block(shape):
    return pl.BlockSpec(shape, lambda *_: (0,) * len(shape), pipeline_mode=pl.Buffered(1))


def struct(shape, dtype):
    return jax.ShapeDtypeStruct(shape, dtype)


def far_struct(shape, dtype):
    return pltpu.HBM(shape, dtype)


def far(*arrays):
    return [pltpu.with_memory_space_constraint(array, pltpu.HBM) for array in arrays]


def pack_kernel(here_ref, *refs):
    *pieces, out = refs
    ring = len(pieces)
    for step, piece in enumerate(pieces):
        place = lax.rem(here_ref[1] - step + ring, ring)
        out[pl.ds(place, 1)] = piece[...][None]


def gather_pieces(shard, here, direct):
    ring = lax.axis_size("seq")
    rows, columns = shard.shape
    if not tuned():
        return [(lax.all_gather(shard, ("dp", "seq"), axis=0, tiled=True), None, 0)]
    pieces = [shard]
    for step in range(1, ring):
        if direct:
            pieces.append(turn(shard, step))
        else:
            pieces.append(turn(pieces[-1]))
    block = call(
        pack_kernel,
        here,
        pieces,
        [whole_block((rows, columns))] * ring,
        struct((ring, rows, columns), shard.dtype),
        whole_block((ring, rows, columns)),
    ).reshape(ring * rows, columns)
    half = ring * rows // 2
    from_x = swap(block, 2)
    from_y = swap(block, 4)
    low = swap(from_x[:half], 4)
    high = swap(from_y[half:], 2)
    held = [(block, 0, 0), (from_x, 2, 0), (from_y, 4, 0), (low, 6, 0), (high, 6, half)]
    other = [
        (swap(piece, 1), xor ^ 1, first)
        for piece, xor, first in held
    ]
    return held + other


def first_row(here_ref, block_rows, xor, first):
    if xor is None:
        return 0
    return pl.multiple_of((here_ref[0] ^ xor) * block_rows + first, 8)


def assemble_kernel(block_rows, places, here_ref, *refs):
    *pieces, wq_out, wkv_out, side_out, rows_out = refs
    pairs = wq_out.shape[0]
    for piece, (xor, first) in zip(pieces, places):
        at = pl.ds(first_row(here_ref, block_rows, xor, first), piece.shape[0])

        def lanes(index):
            return piece[:, index * LANES : (index + 1) * LANES]

        for pair in range(pairs):
            wq_out[pair, at, :] = lanes(pair)
            wkv_out[pair, at, :LANES] = lanes(pairs + pair)
            wkv_out[pair, at, LANES:] = lanes(2 * pairs + pair)
        side_out[at, :] = lanes(3 * pairs)
    rows_out[...] = jnp.transpose(side_out[...].astype(F32))


def assemble(pieces, here, rows, block_rows):
    pairs = pieces[0][0].shape[1] // (3 * LANES)
    shapes = [(pairs, rows, LANES), (pairs, rows, 2 * LANES), (rows, LANES), (LANES, rows)]
    return call(
        functools.partial(assemble_kernel, block_rows, [p[1:] for p in pieces]),
        here,
        [p[0] for p in pieces],
        [whole_block(p[0].shape) for p in pieces],
        [struct(shape, F32 if shape == shapes[-1] else BF16) for shape in shapes],
        [whole_block(shape) for shape in shapes],
        limit=12 << 20,
    )


def join_kernel(here_ref, own_ref, recv_ref, me, x_send, y_send, x_late, y_late):
    rows = me.shape[0]
    half = rows // 2

    def total(slot, first, count):
        part = pl.ds(slot * rows + first, count)
        return (own_ref[part, :].astype(F32) + recv_ref[part, :].astype(F32)).astype(BF16)

    me[...] = total(0, 0, rows)
    x_send[:half, :] = total(3, half, half)
    x_send[half:, :] = total(1, half, half)
    y_send[:half, :] = total(3, 0, half)
    y_send[half:, :] = total(2, 0, half)
    x_late[...] = total(1, 0, half)
    y_late[...] = total(2, half, half)


def close_kernel(ring, here_ref, me, x_early, y_early, x_late, y_late, *refs):
    *outs, total = refs
    half = me.shape[0] // 2
    rows = me.shape[0] // ring
    total[:half, :] = (
        me[:half, :].astype(F32) + y_early[half:, :].astype(F32) + x_late[...].astype(F32)
    )
    total[half:, :] = (
        me[half:, :].astype(F32) + x_early[half:, :].astype(F32) + y_late[...].astype(F32)
    )
    for step, out in enumerate(outs):
        place = lax.rem(here_ref[1] + step, ring)
        out[...] = total[pl.ds(pl.multiple_of(place * rows, 8), rows), :].astype(out.dtype)


def scatter_parts(own, away, here, tile):
    ring = lax.axis_size("seq")
    if not tuned():
        return [lax.psum_scatter(own, ("dp", "seq"), scatter_dimension=0, tiled=True).astype(F32)]
    count, columns = own.shape
    rows = count // 4
    half = rows // 2
    got = swap(away, 1)

    def spec(height):
        return pl.BlockSpec((height, tile), lambda j, *_: (0, j))

    grid = (columns // tile,)
    heights = (rows, rows, rows, half, half)
    me, x_send, y_send, x_late, y_late = call(
        join_kernel,
        here,
        [own, got],
        [spec(count)] * 2,
        [far_struct((rows, columns), BF16)]
        + [struct((height, columns), BF16) for height in heights[1:]],
        [spec(height) for height in heights],
        grid=grid,
        limit=18 << 20,
    )
    x_early = swap(x_send, 2)
    y_early = swap(y_send, 4)
    x_sum = (x_late.astype(F32) + y_early[:half].astype(F32)).astype(BF16)
    y_sum = (y_late.astype(F32) + x_early[:half].astype(F32)).astype(BF16)
    x_late = swap(x_sum, 2)
    y_late = swap(y_sum, 4)
    small = rows // ring
    terms = call(
        functools.partial(close_kernel, ring),
        here,
        [*far(me), x_early, y_early, x_late, y_late],
        [spec(height) for height in heights],
        [struct((small, columns), F32 if step == 0 else BF16) for step in range(ring)],
        [spec(small)] * ring,
        grid=grid,
        scratch=[pltpu.VMEM((rows, tile), F32)],
        limit=12 << 20,
    )
    return [terms[0]] + [turn(terms[step], step) for step in range(1, ring)]


def own_slots():
    if tuned():
        return [0, 2, 4, 6], [1, 3, 5, 7]
    return list(range(lax.axis_size("dp"))), []


def low_lanes(shape):
    return lax.broadcasted_iota(jnp.int32, shape, 1) < DH


def stack(refs):
    if len(refs) == 1:
        return refs[0][...]
    return jnp.concatenate([ref[...] for ref in refs], axis=0)


def id_mask(exts, rows, query_row):
    masks = []
    for ext in exts:
        key_ids = ext[rows : rows + 8, :rows].astype(F32)[0:1, :]
        key_ids = jnp.transpose(jnp.broadcast_to(key_ids, (LANES, rows)))
        masks.append(jnp.where(key_ids[:, 0:1] == query_row, 0.0, NEGATIVE_FILL))
    return masks[0] if len(masks) == 1 else jnp.concatenate(masks, axis=0)


def forward_kernel(count, first, last, here_ref, *refs):
    exts, refs = refs[:count], refs[count:]
    small_ref, wkv_ref, bias_ref, qid_ref = refs[:4]
    refs = refs[4:]
    if first:
        wq_ref, refs = refs[0], refs[1:]
    else:
        q_ref, stat_ref, acc_ref = refs[:3]
        refs = refs[3:]
    kv_outs, refs = refs[:count], refs[count:]
    if first:
        q_out, refs = refs[0], refs[1:]
    out_ref, stat_out, act_ref, mask_ref = refs
    rows = qid_ref.shape[1]

    @pl.when(pl.program_id(0) == 0)
    def _():
        for index, ext in enumerate(exts):
            normed = ext[:rows, :].astype(F32)
            act_ref[index * rows : (index + 1) * rows, :] = (
                normed * small_ref[0:1, :] + small_ref[1:2, :]
            ).astype(BF16)
        mask_ref[...] = id_mask(exts, rows, qid_ref[0:1, :])

    both = product(act_ref[...], wkv_ref[...])
    keys = both[:, :LANES].astype(BF16)
    values = (both[:, LANES:] + bias_ref[3:4, :]).astype(BF16)
    for index in range(count):
        part = slice(index * rows, (index + 1) * rows)
        kv_outs[index][:, :LANES] = keys[part]
        kv_outs[index][:, LANES:] = values[part]
    if first:
        query = (product(act_ref[:rows, :], wq_ref[...]) + bias_ref[2:3, :]).astype(BF16)
        q_out[...] = query
    else:
        query = q_ref[...]
    low = low_lanes(query.shape)
    key_low = low_lanes(keys.shape)
    zero = jnp.zeros_like(query)
    one = jnp.ones_like(values)
    maxima, totals, mixes = [], [], []
    for head in range(2):
        here, there = slice(head * DH, (head + 1) * DH), (1 - head) * DH
        side = low if head == 0 else ~low
        key_side = key_low if head == 0 else ~key_low
        scores = contract_cols(keys, jnp.where(side, query, zero)) * (0.125 * LOG2E)
        scores = scores + mask_ref[...]
        top = jnp.max(scores, axis=0, keepdims=True)
        if not first:
            before = stat_ref[0, head : head + 1, :]
            top = jnp.maximum(top, before)
        portion = jnp.exp2(scores - top).astype(BF16)
        mixed = contract_rows(jnp.where(key_side, values, one), portion)
        total = mixed[there : there + 1, :]
        mixed = mixed[here, :]
        if not first:
            factor = jnp.exp2(before - top)
            total = total + stat_ref[0, 2 + head : 3 + head, :] * factor
            mixed = mixed + acc_ref[here, :] * factor
        maxima.append(top)
        totals.append(total)
        mixes.append(mixed / total if last else mixed)
    mixed = jnp.concatenate(mixes, axis=0)
    if last:
        out_ref[...] = jnp.transpose(mixed).astype(BF16)
        for head in range(2):
            stat_out[0, head : head + 1, :] = maxima[head] + jnp.log2(totals[head])
    else:
        out_ref[...] = mixed
        for head in range(2):
            stat_out[0, head : head + 1, :] = maxima[head]
            stat_out[0, 2 + head : 3 + head, :] = totals[head]


def pair_block(rows, lanes):
    return pl.BlockSpec((None, rows, lanes), lambda j, *_: (j, 0, 0))


def forward_block(here, exts, small, w_query, w_kv, query_row, query, state, last):
    count = len(exts)
    rows = query_row.shape[1]
    width = exts[0].shape[1]
    pairs = width // LANES
    first = state is None
    flat = pl.BlockSpec((LANES, rows), lambda j, *_: (j, 0))
    stat = pl.BlockSpec((1, 4, rows), lambda j, *_: (j, 0, 0))
    in_specs = [whole_block(exts[0].shape)] * count + [
        pl.BlockSpec((8, width), lambda *_: (0, 0)),
        pair_block(width, 2 * LANES),
        pl.BlockSpec((8, LANES), lambda j, *_: (0, j)),
        whole_block(query_row.shape),
    ]
    args = [*exts, small, w_kv, small, query_row]
    out_shapes = [far_struct((pairs, rows, 2 * LANES), BF16)] * count
    out_specs = [pair_block(rows, 2 * LANES)] * count
    if first:
        in_specs += [pair_block(width, LANES)]
        args += [w_query]
        out_shapes.append(far_struct((pairs, rows, LANES), BF16))
        out_specs.append(pair_block(rows, LANES))
    else:
        in_specs += [pair_block(rows, LANES), stat, flat]
        args += far(query, *state)
    out_shapes += [
        struct((rows, width), BF16) if last else far_struct((width, rows), F32),
        far_struct((pairs, 4, rows), F32),
    ]
    out_specs += [pl.BlockSpec((rows, LANES), lambda j, *_: (0, j)) if last else flat, stat]
    result = call(
        functools.partial(forward_kernel, count, first, last),
        here,
        args,
        in_specs,
        out_shapes,
        out_specs,
        grid=(pairs,),
        scratch=[pltpu.VMEM((count * rows, width), BF16), pltpu.VMEM((count * rows, rows), F32)],
        limit=16 << 20,
        cost=pl.CostEstimate(
            flops=24 * count * rows * rows * width,
            bytes_accessed=8 * rows * width,
            transcendentals=count * rows * rows * H,
        ),
    )
    kvs, rest = result[:count], result[count:]
    if first:
        query, rest = rest[0], rest[1:]
    return kvs, query, tuple(rest[::-1]) if not last else tuple(rest)


def backward_kernel(count, first, last, here_ref, *refs):
    q_ref, do_ref, o_ref, stat_ref, wkv_ref, qid_ref = refs[:6]
    refs = refs[6:]
    exts, kvs, refs = refs[:count], refs[count : 2 * count], refs[2 * count :]
    if not first:
        dq_ref, refs = refs[0], refs[1:]
    if last:
        wq_ref, refs = refs[0], refs[1:]
    dq_out, sum_ref, refs = refs[0], refs[1], refs[2:]
    dkv_outs, parts, refs = refs[:count], refs[count : 2 * count], refs[2 * count :]
    (mask_ref,) = refs
    rows = q_ref.shape[0]

    @pl.when(pl.program_id(0) == 0)
    def _():
        mask_ref[...] = id_mask(exts, rows, qid_ref[0:1, :])
        for part in parts:
            part[...] = jnp.zeros_like(part)

    query = q_ref[...]
    grad = do_ref[...]
    both = stack(kvs)
    keys, values = both[:, :LANES], both[:, LANES:]
    low = low_lanes(query.shape)
    key_low = low_lanes(keys.shape)
    zero = jnp.zeros_like(query)
    flipped = jnp.transpose(grad.astype(F32) * o_ref[...].astype(F32))
    sides = (low, ~low)
    queries = [jnp.where(side, query, zero) for side in sides]
    grads = [jnp.where(side, grad, zero) for side in sides]
    all_scores = contract_cols(keys, jnp.concatenate(queries, axis=0))
    all_changes = contract_cols(values, jnp.concatenate(grads, axis=0))
    dk = dv = dq = None
    for head in range(2):
        span = slice(head * rows, (head + 1) * rows)
        delta = jnp.sum(flipped[head * DH : (head + 1) * DH, :], axis=0, keepdims=True)
        scores = all_scores[:, span] * (0.125 * LOG2E) + mask_ref[...]
        portion = jnp.exp2(scores - stat_ref[0, head : head + 1, :])
        score_grad = (portion * (all_changes[:, span] - delta)).astype(BF16)
        keys_here = jnp.where(key_low if head == 0 else ~key_low, keys, jnp.zeros_like(keys))
        dv_here = product(portion.astype(BF16), grads[head])
        dk_here = product(score_grad, queries[head])
        dq_here = contract_rows(score_grad, keys_here)
        if head == 0:
            dk, dv, dq = dk_here, dv_here, dq_here
        else:
            dk, dv, dq = dk + dk_here, dv + dv_here, dq + dq_here
    dk = (dk * 0.125).astype(BF16)
    dv = dv.astype(BF16)
    dq = dq * 0.125
    if not first:
        dq = dq + dq_ref[...]
    both = jnp.concatenate([dk, dv], axis=1)
    sum_ref[0:1, :] = jnp.sum(both.astype(F32), axis=0, keepdims=True)
    part = contract_cols(both, wkv_ref[...])
    for index in range(count):
        span = slice(index * rows, (index + 1) * rows)
        dkv_outs[index][...] = both[span]
        term = part[span]
        if last and index == count - 1:
            dq = dq.astype(BF16)
            sum_ref[1:2, :LANES] = jnp.sum(dq.astype(F32), axis=0, keepdims=True)
            term = term + contract_cols(dq, wq_ref[...])
        parts[index][...] += term
    dq_out[...] = dq


def backward_block(here, query, grad, mixed, stats, kvs, w_query, w_kv, query_row, exts, dq, last):
    count = len(exts)
    rows, width = grad.shape
    pairs = width // LANES
    first = dq is None
    tile = pl.BlockSpec((rows, LANES), lambda j, *_: (0, j))
    narrow, both = pair_block(rows, LANES), pair_block(rows, 2 * LANES)
    in_specs = [
        narrow,
        tile,
        tile,
        pl.BlockSpec((1, 4, rows), lambda j, *_: (j, 0, 0)),
        pair_block(width, 2 * LANES),
        whole_block(query_row.shape),
    ]
    in_specs += [whole_block(exts[0].shape)] * count + [both] * count
    args = [*far(query), grad, mixed, *far(stats), w_kv, query_row, *exts, *far(*kvs)]
    if not first:
        in_specs.append(narrow)
        args += far(dq)
    if last:
        in_specs.append(pair_block(width, LANES))
        args.append(w_query)
    result = call(
        functools.partial(backward_kernel, count, first, last),
        here,
        args,
        in_specs,
        [far_struct((pairs, rows, LANES), BF16 if last else F32), struct((pairs, 8, 2 * LANES), F32)]
        + [far_struct((pairs, rows, 2 * LANES), BF16)] * count
        + [struct((rows, width), F32)] * count,
        [narrow, pair_block(8, 2 * LANES)]
        + [both] * count
        + [whole_block((rows, width))] * count,
        grid=(pairs,),
        scratch=[pltpu.VMEM((count * rows, rows), F32)],
        limit=16 << 20,
        cost=pl.CostEstimate(
            flops=40 * count * rows * rows * width,
            bytes_accessed=16 * rows * width,
            transcendentals=count * rows * rows * H,
        ),
    )
    dq, sums, rest = result[0], result[1], result[2:]
    return dq, sums, rest[:count], rest[count:]


def transposed_slots(here_ref, values, slots, block_rows, plain_ref, out_ref):
    plain_ref[...] = jnp.transpose(values.astype(F32)).astype(BF16)
    for index, xor in enumerate(slots):
        start = pl.multiple_of((here_ref[0] ^ xor) * block_rows, 8)
        out_ref[index * block_rows : (index + 1) * block_rows, :] = plain_ref[pl.ds(start, block_rows), :]


def middle_kernel(places, block_rows, slots, kept, tile, here_ref, *refs):
    count = len(places)
    frames_ref, mixed_ref, cot_ref, small_ref = refs[:4]
    pieces, refs = refs[4 : 4 + count], refs[4 + count :]
    out_ref, dr_ref, doh_ref, sum_ref = refs[:4]
    grads, refs = refs[4 : 4 + len(kept)], refs[4 + len(kept) :]
    (
        w_ref,
        stage_ref,
        last_ref,
        normed_ref,
        back_ref,
        act_ref,
        half_ref,
        act_flip,
        half_flip,
        plain_ref,
        bias_ref,
        bias_sum,
        in_sems,
        out_sems,
        last_sems,
    ) = refs
    width = frames_ref.shape[1]
    hidden = bias_ref.shape[1]

    copies = []
    for index, (piece, (xor, first, column)) in enumerate(zip(pieces, places)):
        start = first_row(here_ref, block_rows, xor, first)
        height, span = piece.shape
        target = w_ref.at[pl.ds(start, height), column : column + span]
        copies.append(pltpu.make_async_copy(piece, target, in_sems.at[index]))
    for copy in copies:
        copy.start()
    cot = cot_ref[...]
    half_ref[...] = cot.astype(BF16)
    transposed_slots(here_ref, half_ref[...], slots, block_rows, plain_ref, half_flip)
    for index in range(4):
        bias_ref[:, index * width : (index + 1) * width] = small_ref[8 + index : 9 + index, :]
    sum_ref[3:4, :] = jnp.sum(cot, axis=0, keepdims=True)
    for copy in copies:
        copy.wait()

    resid = frames_ref[...] + product(mixed_ref[...], w_ref[:, :width]) + small_ref[4:5, :]
    normed, inv_std = normalize(resid)
    normed_ref[...] = normed
    act_ref[...] = (normed * small_ref[5:6, :] + small_ref[6:7, :]).astype(BF16)
    out_ref[...] = resid + small_ref[7:8, :]
    back_ref[...] = jnp.zeros_like(back_ref)
    transposed_slots(here_ref, act_ref[...], slots, block_rows, plain_ref, act_flip)

    def send(source, column, start, size, sems):
        moves = []
        first = 0
        for index, (grad, height) in enumerate(zip(grads, kept)):
            moves.append(
                pltpu.make_async_copy(
                    source.at[first : first + height, column : column + size],
                    grad.at[:, pl.ds(start, size)],
                    sems.at[index],
                )
            )
            first += height
        return moves

    tiles = hidden // tile

    def columns(index):
        up = pl.multiple_of(width + index * tile, LANES)
        down = pl.multiple_of(width + hidden + index * tile, LANES)
        return up, down, pl.multiple_of(index * tile, LANES)

    def moves_of(index):
        up, down, _ = columns(index)
        slot = lax.rem(index, 2)
        stage = stage_ref.at[slot]
        return send(stage, 0, up, tile, out_sems.at[slot, 0]) + send(
            stage, tile, down, tile, out_sems.at[slot, 1]
        )

    def body(index, carry):
        up, down, at = columns(index)
        slot = lax.rem(index, 2)

        @pl.when(index >= 2)
        def _():
            for move in moves_of(index - 2):
                move.wait()

        w_up = w_ref[:, pl.ds(up, tile)]
        w_down = w_ref[:, pl.ds(down, tile)]
        u = product(act_ref[...], w_up) + bias_ref[:, pl.ds(at, tile)]
        rise = 0.5 * (1.0 + lax.erf(u * ROOT_HALF))
        slope = rise + u * jnp.exp(-0.5 * u * u) * INV_ROOT_TAU
        value = (u * rise).astype(BF16)
        out_ref[...] += contract_cols(value, w_down)
        du = product(half_ref[...], w_down) * slope
        bias_sum[:, pl.ds(at, tile)] = jnp.sum(du, axis=0, keepdims=True)
        du = du.astype(BF16)
        back_ref[...] += contract_cols(du, w_up)
        stage_ref[slot, :, :tile] = product(act_flip[...], du).astype(BF16)
        stage_ref[slot, :, tile:] = product(half_flip[...], value).astype(BF16)
        for move in moves_of(index):
            move.start()
        return carry

    lax.fori_loop(0, tiles, body, 0)

    incoming = back_ref[...]
    normed = normed_ref[...]
    dr = cot_ref[...] + norm_backward(incoming, normed, inv_std, small_ref[5:6, :])
    dr_ref[...] = dr
    sum_ref[0:1, :] = jnp.sum(dr, axis=0, keepdims=True)
    sum_ref[1:2, :] = jnp.sum(incoming * normed, axis=0, keepdims=True)
    sum_ref[2:3, :] = jnp.sum(incoming, axis=0, keepdims=True)
    for index in range(4):
        sum_ref[4 + index : 5 + index, :] = bias_sum[:, index * width : (index + 1) * width]
    drh = dr.astype(BF16)
    transposed_slots(here_ref, mixed_ref[...], slots, block_rows, plain_ref, act_flip)
    last_ref[...] = product(act_flip[...], drh).astype(BF16)
    finals = send(last_ref, 0, 0, width, last_sems)
    for move in finals:
        move.start()
    doh_ref[...] = contract_cols(drh, w_ref[:, :width]).astype(BF16)
    for index in range(max(tiles - 2, 0), tiles):
        finals = finals + moves_of(jnp.int32(index))
    for move in finals:
        move.wait()


def middle(here, frames, mixed, cot, small, pieces, rows_total, block_rows):
    rows, width = frames.shape
    starts = [0, pieces[0][0][0].shape[1]]
    columns = starts[1] + pieces[1][0][0].shape[1]
    pieces = [(*piece, start) for part, start in zip(pieces, starts) for piece in part]
    hidden = (columns - width) // 2
    tile = 2 * LANES
    kept, given = own_slots()
    heights = [len(part) * block_rows for part in (kept, given) if part]
    anywhere = pl.BlockSpec(memory_space=pl.ANY)
    full = whole_block((rows, width))
    outs = [struct((rows, width), F32), struct((rows, width), F32), struct((rows, width), BF16), struct((8, width), F32)]
    return call(
        functools.partial(
            middle_kernel, [p[1:] for p in pieces], block_rows, kept + given, heights, tile
        ),
        here,
        [frames, mixed, cot, small, *[p[0] for p in pieces]],
        [full, full, full, pl.BlockSpec((16, width), lambda *_: (0, 0))] + [anywhere] * len(pieces),
        outs + [struct((height, columns), BF16) for height in heights],
        [full, full, full, whole_block((8, width))] + [anywhere] * len(heights),
        scratch=[
            pltpu.VMEM((rows_total, columns), BF16),
            pltpu.VMEM((2, rows_total, 2 * tile), BF16),
            pltpu.VMEM((rows_total, width), BF16),
            pltpu.VMEM((rows, width), F32),
            pltpu.VMEM((rows, width), F32),
            pltpu.VMEM((rows, width), BF16),
            pltpu.VMEM((rows, width), BF16),
            pltpu.VMEM((width, rows), BF16),
            pltpu.VMEM((width, rows), BF16),
            pltpu.VMEM((width, rows), BF16),
            pltpu.VMEM((1, hidden), F32),
            pltpu.VMEM((1, hidden), F32),
            pltpu.SemaphoreType.DMA((len(pieces),)),
            pltpu.SemaphoreType.DMA((2, 2, len(heights))),
            pltpu.SemaphoreType.DMA((len(heights),)),
        ],
        limit=30 << 20,
        cost=pl.CostEstimate(
            flops=36 * rows * width * hidden // 3, bytes_accessed=4 * rows_total * columns, transcendentals=2 * rows * hidden
        ),
    )


def cross_kernel(ring, slots, block_rows, heights, here_ref, *refs):
    exts, refs = refs[:ring], refs[ring:]
    dq_ref, refs = refs[0], refs[1:]
    dkvs, refs = refs[:ring], refs[ring:]
    sums, refs = refs[:ring], refs[ring:]
    mid_ref, wkv_ref, wq_ref, cols_ref, refs = refs[0], refs[1], refs[2], refs[3], refs[4:]
    outs, refs = refs[: len(heights)], refs[len(heights) :]
    flip_ref, plain_ref, gain_ref, side_ref, turned_ref, shift_ref, line_ref = refs
    step = pl.program_id(0)
    rows = dq_ref.shape[1]
    width = plain_ref.shape[0]
    pairs = width // LANES

    def slot_rows(index):
        start = pl.multiple_of((here_ref[0] ^ slots[index]) * block_rows, 8)
        return pl.ds(start, block_rows), pl.ds(index * block_rows, block_rows)

    @pl.when(step == 0)
    def _():
        for index in range(ring):
            plain_ref[...] = jnp.transpose(exts[index][:rows, :].astype(F32)).astype(BF16)
            for slot in range(len(slots)):
                source, target = slot_rows(slot)
                flip_ref[target, index * rows : (index + 1) * rows] = plain_ref[source, :]
        for slot in range(len(slots)):
            source, target = slot_rows(slot)
            side = cols_ref[source, :].astype(F32)
            side_ref[target, :] = jnp.broadcast_to(side[:, 0:1], side.shape)
            turned_ref[target, :] = jnp.broadcast_to(side[:, 1:2], side.shape)
        gain_ref[...] = jnp.zeros_like(gain_ref)
        shift_ref[...] = jnp.zeros_like(shift_ref)
        line_ref[...] = jnp.zeros_like(line_ref)

    def finish(crossed, line, weights, columns):
        wide = jnp.broadcast_to(line, (8, 2 * LANES))
        high = wide.astype(BF16)
        low = (wide - high.astype(F32)).astype(BF16)
        full = weights[...] if len(weights.shape) == 2 else jnp.concatenate([weights[0], weights[1]], axis=1)
        shift_ref[...] += contract_cols(high, full) + contract_cols(low, full)
        for index in range(len(slots)):
            source, target = slot_rows(index)
            part = crossed[index * block_rows : (index + 1) * block_rows, :]
            gain, shift = side_ref[target, :], turned_ref[target, :]
            out = 0 if index * block_rows < heights[0] else 1
            first = index * block_rows - (heights[0] if out else 0)
            total = gain_ref[target, :]
            for half in range(2):
                lanes = slice(half * LANES, (half + 1) * LANES)
                if len(weights.shape) == 2:
                    weight = weights[source, lanes]
                else:
                    weight = weights[half, source, :]
                total = total + weight.astype(F32) * part[:, lanes]
                grad = gain * part[:, lanes] + shift * line[:, lanes]
                outs[out][first : first + block_rows, pl.ds(columns[half], LANES)] = grad.astype(BF16)
            gain_ref[target, :] = total

    @pl.when(step < pairs)
    def _():
        crossed = product(flip_ref[:, :rows], dkvs[0][...])
        for index in range(1, ring):
            crossed += product(flip_ref[:, index * rows : (index + 1) * rows], dkvs[index][...])
        line = sums[0][step, 0:1, :]
        for other in sums[1:]:
            line = line + other[step, 0:1, :]
        at = pl.multiple_of(step * LANES, LANES)
        line_ref[3:4, pl.ds(at, LANES)] = line[:, LANES:]
        finish(crossed, line, wkv_ref, (at + width, at + 2 * width))

    @pl.when(step >= pairs)
    def _():
        pair = 2 * (step - pairs)
        grads = jnp.concatenate([dq_ref[0], dq_ref[1]], axis=1)
        line = jnp.concatenate(
            [sums[-1][pair, 1:2, :LANES], sums[-1][pair + 1, 1:2, :LANES]], axis=1
        )
        at = pl.multiple_of(pair * LANES, LANES)
        line_ref[2:3, pl.ds(at, 2 * LANES)] = line
        finish(product(flip_ref[:, :rows], grads), line, wq_ref, (at, at + LANES))

    @pl.when(step == pl.num_programs(0) - 1)
    def _():
        line_ref[1:2, :] = shift_ref[0:1, :]
        line_ref[4:12, :] = mid_ref[...]
        turned_ref[...] = jnp.transpose(line_ref[...])
        lane = lax.broadcasted_iota(jnp.int32, (block_rows, LANES), 1)
        for index in range(len(slots)):
            source, target = slot_rows(index)
            gain = jnp.sum(gain_ref[target, :], axis=1, keepdims=True)
            value = jnp.where(lane == 0, gain, turned_ref[source, :])
            out = 0 if index * block_rows < heights[0] else 1
            start = index * block_rows - (heights[0] if out else 0)
            outs[out][start : start + block_rows, 3 * width :] = value.astype(BF16)


def cross(here, exts, dq, dkvs, sums, mid_sums, w_query, w_kv, side, block_rows):
    ring = len(exts)
    pairs, rows, _ = dq.shape
    width = pairs * LANES
    kept, given = own_slots()
    heights = [len(part) * block_rows for part in (kept, given) if part]
    columns = 3 * width + LANES

    def kv_spec(height):
        return pl.BlockSpec(
            (None, height, 2 * LANES), lambda j, *_: (jnp.minimum(j, pairs - 1), 0, 0)
        )

    def q_spec(height):
        return pl.BlockSpec((2, height, LANES), lambda j, *_: (jnp.maximum(j - pairs, 0), 0, 0))

    return call(
        functools.partial(cross_kernel, ring, kept + given, block_rows, heights),
        here,
        [*exts, *far(dq, *dkvs), *sums, mid_sums, w_kv, w_query, side],
        [whole_block(exts[0].shape)] * ring
        + [q_spec(rows)]
        + [kv_spec(rows)] * ring
        + [whole_block(sums[0].shape)] * ring
        + [whole_block((8, width)), kv_spec(width), q_spec(width), whole_block((width, LANES))],
        [struct((height, columns), BF16) for height in heights],
        [whole_block((height, columns)) for height in heights],
        grid=(pairs + pairs // 2,),
        scratch=[
            pltpu.VMEM((width, ring * rows), BF16),
            pltpu.VMEM((width, rows), BF16),
            pltpu.VMEM((width, LANES), F32),
            pltpu.VMEM((width, LANES), F32),
            pltpu.VMEM((width, LANES), F32),
            pltpu.VMEM((8, width), F32),
            pltpu.VMEM((LANES, width), F32),
        ],
        limit=20 << 20,
        cost=pl.CostEstimate(
            flops=2 * rows * width * width * (2 * ring + 1), bytes_accessed=2 * width * columns * 3, transcendentals=0
        ),
    )


def add_up(terms, start, stop):
    value = terms[0][:, start:stop].astype(F32)
    for term in terms[1:]:
        value = value + term[:, start:stop].astype(F32)
    return value


def wide_kernel(count, width, *refs):
    terms, refs = refs[:count], refs[count:]
    weight, first, second, grad_out, weight_out, first_out, second_out = refs
    hidden = weight.shape[2]
    spans = ((0, 3 * width, 0, width), (1, 0, width, hidden), (2, 0, width + hidden, hidden))
    for matrix, column, start, size in spans:
        grad = add_up(terms, start, start + size)
        at = slice(column, column + size)
        new_weight, new_first, new_second = adam_update(
            weight[matrix, :, at], grad, first[matrix, :, at], second[matrix, :, at], WEIGHT_DECAY, LEARN_RATE
        )
        grad_out[matrix, :, at] = grad
        weight_out[matrix, :, at] = new_weight
        first_out[matrix, :, at] = new_first
        second_out[matrix, :, at] = new_second


def wide_update(terms, width, mats, mats_m, mats_v):
    block = whole_block(mats.shape)
    return pl.pallas_call(
        functools.partial(wide_kernel, len(terms), width),
        grid=(1,),
        in_specs=[whole_block(term.shape) for term in terms] + [block] * 3,
        out_specs=[block] * 4,
        out_shape=[far_struct(mats.shape, F32)] * 4,
        compiler_params=pltpu.CompilerParams(vmem_limit_bytes=16 << 20),
        name="wide_update",
    )(*terms, *far(mats, mats_m, mats_v))


def narrow_kernel(count, *refs):
    terms, refs = refs[:count], refs[count:]
    weight, first, second, small, small_first, small_second = refs[:6]
    outs = refs[10:]
    size = weight.shape[2]
    grad = add_up(terms, 0, size)
    results = adam_update(weight[0], grad, first[0], second[0], WEIGHT_DECAY, LEARN_RATE)
    for out, value in zip(outs[:4], (grad, *results)):
        out[0] = value
    grad = jnp.transpose(add_up(terms, size, terms[0].shape[1]))[: small.shape[0], :]
    results = adam_update(small[...], grad, small_first[...], small_second[...], 0.0, SMALL_RATE)
    for out, value in zip(outs[4:], (grad, *results)):
        out[...] = value


def narrow_update(terms, width, mats, mats_m, mats_v, smalls, smalls_m, smalls_v, outs):
    count = len(terms)
    rows = mats.shape[1]
    block = pl.BlockSpec((1, rows, 3 * width), lambda i: (0, 0, 0))
    small = whole_block(smalls.shape)
    return pl.pallas_call(
        functools.partial(narrow_kernel, count),
        grid=(1,),
        in_specs=[whole_block(term.shape) for term in terms]
        + [block] * 3
        + [small] * 3
        + [pl.BlockSpec(memory_space=pl.ANY)] * 4,
        out_specs=[block] * 4 + [small] * 4,
        out_shape=[far_struct(mats.shape, F32)] * 4 + [struct(smalls.shape, F32)] * 4,
        input_output_aliases={count + 6 + index: index for index in range(4)},
        compiler_params=pltpu.CompilerParams(vmem_limit_bytes=12 << 20),
        name="narrow_update",
    )(*terms, *far(mats, mats_m, mats_v), smalls, smalls_m, smalls_v, *outs)


def groups(ring):
    ahead = [[i] for i in range(ring)]
    order = list(range(1, ring)) + [0]
    return ahead, [[i] for i in order]


def shards(frames, clip_ids, cotangent, mats, smalls, mats_m, mats_v, smalls_m, smalls_v):
    inputs = frames[0]
    upstream = cotangent[0]
    tok_rows, width = inputs.shape
    ring = lax.axis_size("seq")
    devices = ring * lax.axis_size("dp")
    block_rows = ring * mats.shape[1]
    total_rows = devices * mats.shape[1]
    here_dp = lax.axis_index("dp") if tuned() else jnp.int32(0)
    here = jnp.stack([here_dp, lax.axis_index("seq")]).astype(jnp.int32)

    normed_one, inv_one = normalize(inputs)
    id_row = clip_ids.astype(F32)
    id_rows = jnp.pad(id_row, ((0, 7), (0, width - tok_rows))).astype(BF16)
    piece = jnp.concatenate([normed_one.astype(BF16), id_rows], axis=0)
    normed_one, inv_one, piece = lax.optimization_barrier((normed_one, inv_one, piece))
    exts = [piece]
    for _ in range(1, ring):
        exts.append(turn(exts[-1]))

    mats_half = mats.astype(BF16)
    small_columns = jnp.pad(
        jnp.transpose(smalls.astype(BF16).astype(F32)), ((0, 0), (0, LANES - smalls.shape[0]))
    ).astype(BF16)
    chunk = jnp.concatenate([mats_half[0][:, : 3 * width], small_columns], axis=1)
    w_query, w_kv, side, small = assemble(
        gather_pieces(chunk, here, True), here, total_rows, block_rows
    )
    chunk = jnp.concatenate([mats_half[0][:, 3 * width :], mats_half[1]], axis=1)
    wide_pieces = [gather_pieces(chunk, here, False), gather_pieces(mats_half[2], here, False)]

    query, state = None, None
    kvs = [None] * ring
    ahead, back = groups(ring)
    for group in ahead:
        some, query, state = forward_block(
            here, [exts[i] for i in group], small, w_query, w_kv, id_row, query, state, group is ahead[-1]
        )
        for index, kv in zip(group, some):
            kvs[index] = kv
    mixed_half, stats = state

    output, grad_resid, grad_heads, mid_sums, *wide_grads = middle(
        here, inputs, mixed_half, upstream, small, wide_pieces, total_rows, block_rows
    )
    wide_terms = scatter_parts(wide_grads[0], wide_grads[-1], here, 3 * width)

    dq = None
    riding = None
    dkvs, sums = [None] * ring, []
    for group in back:
        dq, some, new_dkvs, parts = backward_block(
            here,
            query,
            grad_heads,
            mixed_half,
            stats,
            [kvs[i] for i in group],
            w_query,
            w_kv,
            id_row,
            [exts[i] for i in group],
            dq,
            group is back[-1],
        )
        sums.append(some)
        for index, dkv, part in zip(group, new_dkvs, parts):
            dkvs[index] = dkv
            if riding is not None:
                part = part + riding.astype(F32)
            if index:
                riding = turn(part.astype(BF16))
            else:
                grad_act_one = part

    cross_grads = cross(here, exts, dq, dkvs, sums, mid_sums, w_query, w_kv, side, block_rows)
    cross_terms = scatter_parts(cross_grads[0], cross_grads[-1], here, cross_grads[0].shape[1])
    grad_inputs = grad_resid + norm_backward(grad_act_one, normed_one, inv_one, small[0])

    begun = wide_update(wide_terms, width, mats, mats_m, mats_v)
    updated = narrow_update(
        cross_terms, width, mats, mats_m, mats_v, smalls, smalls_m, smalls_v, begun
    )
    mats_grad, new_mats, new_mats_m, new_mats_v = updated[:4]
    smalls_grad, new_smalls, new_smalls_m, new_smalls_v = updated[4:]
    return (
        output[None],
        grad_inputs[None],
        mats_grad,
        smalls_grad,
        new_mats,
        new_smalls,
        new_mats_m,
        new_mats_v,
        new_smalls_m,
        new_smalls_v,
    )


def solution(mesh):
    in_specs = (
        P("dp", "seq", None),
        P("dp", "seq"),
        P("dp", "seq", None),
        P(None, ("dp", "seq"), None),
        P(None, ("dp", "seq")),
        P(None, ("dp", "seq"), None),
        P(None, ("dp", "seq"), None),
        P(None, ("dp", "seq")),
        P(None, ("dp", "seq")),
    )
    out_specs = (
        P("dp", "seq", None),
        P("dp", "seq", None),
        P(None, ("dp", "seq"), None),
        P(None, ("dp", "seq")),
        P(None, ("dp", "seq"), None),
        P(None, ("dp", "seq")),
        P(None, ("dp", "seq"), None),
        P(None, ("dp", "seq"), None),
        P(None, ("dp", "seq")),
        P(None, ("dp", "seq")),
    )

    return jax.shard_map(shards, mesh=mesh, in_specs=in_specs, out_specs=out_specs, check_vma=False)
```

```python
import functools

import jax
import jax.numpy as jnp
from jax import lax
from jax.experimental import pallas as pl
from jax.experimental.pallas import tpu as pltpu
from jax.sharding import PartitionSpec as P


H = 12
DH = 64
STEP = 3
LANES = 128

NEGATIVE_FILL = -1e30
NORM_EPSILON = 1e-05
ROOT_HALF = 0.7071067811865476
INV_ROOT_TAU = 0.3989422804014327
LOG2E = 1.4426950408889634
BETA_FIRST = 0.9
BETA_SECOND = 0.95
LEARN_RATE = 0.01
SMALL_RATE = 0.1
WEIGHT_DECAY = 0.1
ADAM_EPSILON = 1e-08


F32 = jnp.float32
BF16 = jnp.bfloat16


def contract_rows(left, right):
    return lax.dot_general(left, right, (((0,), (0,)), ((), ())), preferred_element_type=F32)


def contract_cols(left, right):
    return lax.dot_general(left, right, (((1,), (1,)), ((), ())), preferred_element_type=F32)


def product(left, right):
    return jnp.dot(left, right, preferred_element_type=F32)


def normalize(values):
    row_mean = jnp.mean(values, axis=-1, keepdims=True)
    center = values - row_mean
    row_var = jnp.mean(center * center, axis=-1, keepdims=True)
    inv_std = lax.rsqrt(row_var + NORM_EPSILON)
    return center * inv_std, inv_std


def norm_backward(incoming, normed, inv_std, gain_vec):
    scaled = incoming * gain_vec
    return inv_std * (
        scaled
        - jnp.mean(scaled, axis=-1, keepdims=True)
        - normed * jnp.mean(scaled * normed, axis=-1, keepdims=True)
    )


def adam_update(weight, gradient, first, second, decay, step_rate):
    first_new = BETA_FIRST * first + (1.0 - BETA_FIRST) * gradient
    second_new = BETA_SECOND * second + (1.0 - BETA_SECOND) * gradient * gradient
    first_hat = first_new / (1.0 - BETA_FIRST**STEP)
    second_hat = second_new / (1.0 - BETA_SECOND**STEP)
    weight_new = weight - step_rate * (
        first_hat / (jnp.sqrt(second_hat) + ADAM_EPSILON) + decay * weight
    )
    return (weight_new, first_new, second_new)


def turn(block, step=1):
    count = lax.axis_size("seq")
    return lax.ppermute(block, "seq", [(i, (i + step) % count) for i in range(count)])


def swap(block, bit):
    count = lax.axis_size("dp")
    return lax.ppermute(block, "dp", [(i, i ^ bit) for i in range(count)])


def tuned():
    return lax.axis_size("dp") == 8 and lax.axis_size("seq") == 4


def call(kernel, here, ins, in_specs, out_shapes, out_specs, grid=(1,), scratch=(), limit=None, cost=None):
    return pl.pallas_call(
        kernel,
        grid_spec=pltpu.PrefetchScalarGridSpec(
            num_scalar_prefetch=1,
            grid=grid,
            in_specs=in_specs,
            out_specs=out_specs,
            scratch_shapes=list(scratch),
        ),
        out_shape=out_shapes,
        compiler_params=pltpu.CompilerParams(vmem_limit_bytes=limit),
        cost_estimate=cost,
    )(here, *ins)


def whole_block(shape):
    return pl.BlockSpec(shape, lambda *_: (0,) * len(shape), pipeline_mode=pl.Buffered(1))


def struct(shape, dtype):
    return jax.ShapeDtypeStruct(shape, dtype)


def far_struct(shape, dtype):
    return pltpu.HBM(shape, dtype)


def near():
    return pl.BlockSpec(memory_space=pltpu.VMEM)


def far(*arrays):
    return [pltpu.with_memory_space_constraint(array, pltpu.HBM) for array in arrays]


def pack_kernel(here_ref, *refs):
    *pieces, out = refs
    ring = len(pieces)
    for step, piece in enumerate(pieces):
        place = lax.rem(here_ref[1] - step + ring, ring)
        out[pl.ds(place, 1)] = piece[...][None]


def gather_pieces(shard, here, direct):
    ring = lax.axis_size("seq")
    rows, columns = shard.shape
    if not tuned():
        return [(lax.all_gather(shard, ("dp", "seq"), axis=0, tiled=True), None, 0)]
    pieces = [shard]
    for step in range(1, ring):
        if direct:
            pieces.append(turn(shard, step))
        else:
            pieces.append(turn(pieces[-1]))
    block = call(
        pack_kernel,
        here,
        pieces,
        [near()] * ring,
        struct((ring, rows, columns), shard.dtype),
        near(),
        limit=2 << 20,
    ).reshape(ring * rows, columns)
    half = ring * rows // 2
    from_x = swap(block, 2)
    from_y = swap(block, 4)
    low = swap(from_x[:half], 4)
    high = swap(from_y[half:], 2)
    held = [(block, 0, 0), (from_x, 2, 0), (from_y, 4, 0), (low, 6, 0), (high, 6, half)]
    other = [
        (swap(piece, 1), xor ^ 1, first)
        for piece, xor, first in held
    ]
    return held + other


def first_row(here_ref, block_rows, xor, first):
    if xor is None:
        return 0
    return pl.multiple_of((here_ref[0] ^ xor) * block_rows + first, 8)


def assemble_kernel(block_rows, places, here_ref, *refs):
    *pieces, wq_out, wkv_out, side_out, rows_out = refs
    pairs = wq_out.shape[0]
    for piece, (xor, first) in zip(pieces, places):
        at = pl.ds(first_row(here_ref, block_rows, xor, first), piece.shape[0])

        def lanes(index):
            return piece[:, index * LANES : (index + 1) * LANES]

        for pair in range(pairs):
            wq_out[pair, at, :] = lanes(pair)
            wkv_out[pair, at, :LANES] = lanes(pairs + pair)
            wkv_out[pair, at, LANES:] = lanes(2 * pairs + pair)
        side_out[at, :] = lanes(3 * pairs)
    rows_out[...] = jnp.transpose(side_out[...].astype(F32))


def assemble(pieces, here, rows, block_rows):
    pairs = pieces[0][0].shape[1] // (3 * LANES)
    shapes = [(pairs, rows, LANES), (pairs, rows, 2 * LANES), (rows, LANES), (LANES, rows)]
    return call(
        functools.partial(assemble_kernel, block_rows, [p[1:] for p in pieces]),
        here,
        [p[0] for p in pieces],
        [near()] * len(pieces),
        [struct(shape, F32 if shape == shapes[-1] else BF16) for shape in shapes],
        [near()] * len(shapes),
        limit=12 << 20,
    )


def join_kernel(here_ref, own_ref, recv_ref, me, x_send, y_send, x_late, y_late):
    rows = me.shape[0]
    half = rows // 2

    def total(slot, first, count):
        part = pl.ds(slot * rows + first, count)
        return (own_ref[part, :].astype(F32) + recv_ref[part, :].astype(F32)).astype(BF16)

    me[...] = total(0, 0, rows)
    x_send[:half, :] = total(3, half, half)
    x_send[half:, :] = total(1, half, half)
    y_send[:half, :] = total(3, 0, half)
    y_send[half:, :] = total(2, 0, half)
    x_late[...] = total(1, 0, half)
    y_late[...] = total(2, half, half)


def close_kernel(ring, here_ref, me, x_early, y_early, x_late, y_late, *refs):
    *outs, total = refs
    half = me.shape[0] // 2
    rows = me.shape[0] // ring
    total[:half, :] = (
        me[:half, :].astype(F32) + y_early[half:, :].astype(F32) + x_late[...].astype(F32)
    )
    total[half:, :] = (
        me[half:, :].astype(F32) + x_early[half:, :].astype(F32) + y_late[...].astype(F32)
    )
    for step, out in enumerate(outs):
        place = lax.rem(here_ref[1] + step, ring)
        out[...] = total[pl.ds(pl.multiple_of(place * rows, 8), rows), :].astype(out.dtype)


def scatter_parts(own, away, here, tile):
    ring = lax.axis_size("seq")
    if not tuned():
        return [lax.psum_scatter(own, ("dp", "seq"), scatter_dimension=0, tiled=True).astype(F32)]
    count, columns = own.shape
    rows = count // 4
    half = rows // 2
    got = swap(away, 1)

    alone = tile == columns

    def spec(height):
        return near() if alone else pl.BlockSpec((height, tile), lambda j, *_: (0, j))

    grid = (columns // tile,)
    heights = (rows, rows, rows, half, half)
    me, x_send, y_send, x_late, y_late = call(
        join_kernel,
        here,
        [own, got],
        [spec(count)] * 2,
        [(struct if alone else far_struct)((rows, columns), BF16)]
        + [struct((height, columns), BF16) for height in heights[1:]],
        [spec(height) for height in heights],
        grid=grid,
        limit=(2 if alone else 18) << 20,
    )
    x_early = swap(x_send, 2)
    y_early = swap(y_send, 4)
    x_sum = (x_late.astype(F32) + y_early[:half].astype(F32)).astype(BF16)
    y_sum = (y_late.astype(F32) + x_early[:half].astype(F32)).astype(BF16)
    x_late = swap(x_sum, 2)
    y_late = swap(y_sum, 4)
    small = rows // ring
    terms = call(
        functools.partial(close_kernel, ring),
        here,
        [*((me,) if alone else far(me)), x_early, y_early, x_late, y_late],
        [spec(height) for height in heights],
        [struct((small, columns), F32 if step == 0 else BF16) for step in range(ring)],
        [spec(small)] * ring,
        grid=grid,
        scratch=[pltpu.VMEM((rows, tile), F32)],
        limit=(3 if alone else 12) << 20,
    )
    return [terms[0]] + [turn(terms[step], step) for step in range(1, ring)]


def own_slots():
    if tuned():
        return [0, 2, 4, 6], [1, 3, 5, 7]
    return list(range(lax.axis_size("dp"))), []


def low_lanes(shape):
    return lax.broadcasted_iota(jnp.int32, shape, 1) < DH


def stack(refs):
    if len(refs) == 1:
        return refs[0][...]
    return jnp.concatenate([ref[...] for ref in refs], axis=0)


def id_mask(exts, rows, query_row):
    masks = []
    for ext in exts:
        key_ids = ext[rows : rows + 8, :rows].astype(F32)[0:1, :]
        key_ids = jnp.transpose(jnp.broadcast_to(key_ids, (LANES, rows)))
        masks.append(jnp.where(key_ids[:, 0:1] == query_row, 0.0, NEGATIVE_FILL))
    return masks[0] if len(masks) == 1 else jnp.concatenate(masks, axis=0)


def forward_kernel(count, first, last, here_ref, *refs):
    exts, refs = refs[:count], refs[count:]
    small_ref, wkv_ref, qid_ref = refs[:3]
    refs = refs[3:]
    if first:
        wq_ref, refs = refs[0], refs[1:]
    else:
        q_ref, stat_ref, acc_ref = refs[:3]
        refs = refs[3:]
    kv_outs, refs = refs[:count], refs[count:]
    if first:
        q_out, refs = refs[0], refs[1:]
    out_ref, stat_out, act_ref, mask_ref = refs
    rows = qid_ref.shape[1]
    pair = pl.program_id(0)
    lanes = pl.ds(pl.multiple_of(pair * LANES, LANES), LANES)

    @pl.when(pair == 0)
    def _():
        for index, ext in enumerate(exts):
            normed = ext[:rows, :].astype(F32)
            act_ref[index * rows : (index + 1) * rows, :] = (
                normed * small_ref[0:1, :] + small_ref[1:2, :]
            ).astype(BF16)
        mask_ref[...] = id_mask(exts, rows, qid_ref[0:1, :])

    both = product(act_ref[...], wkv_ref[pair])
    keys = both[:, :LANES].astype(BF16)
    values = (both[:, LANES:] + small_ref[3:4, lanes]).astype(BF16)
    for index in range(count):
        part = slice(index * rows, (index + 1) * rows)
        kv_outs[index][:, :LANES] = keys[part]
        kv_outs[index][:, LANES:] = values[part]
    if first:
        query = (product(act_ref[:rows, :], wq_ref[pair]) + small_ref[2:3, lanes]).astype(BF16)
        q_out[pair] = query
    else:
        query = q_ref[pair]
    low = low_lanes(query.shape)
    key_low = low_lanes(keys.shape)
    zero = jnp.zeros_like(query)
    one = jnp.ones_like(values)
    maxima, totals, mixes = [], [], []
    for head in range(2):
        here, there = slice(head * DH, (head + 1) * DH), (1 - head) * DH
        side = low if head == 0 else ~low
        key_side = key_low if head == 0 else ~key_low
        scores = contract_cols(keys, jnp.where(side, query, zero)) * (0.125 * LOG2E)
        scores = scores + mask_ref[...]
        top = jnp.max(scores, axis=0, keepdims=True)
        if not first:
            before = stat_ref[pair, head : head + 1, :]
            top = jnp.maximum(top, before)
        portion = jnp.exp2(scores - top).astype(BF16)
        mixed = contract_rows(jnp.where(key_side, values, one), portion)
        total = mixed[there : there + 1, :]
        mixed = mixed[here, :]
        if not first:
            factor = jnp.exp2(before - top)
            total = total + stat_ref[pair, 2 + head : 3 + head, :] * factor
            start = pl.multiple_of(pair * LANES + head * DH, DH)
            mixed = mixed + acc_ref[pl.ds(start, DH), :] * factor
        maxima.append(top)
        totals.append(total)
        mixes.append(mixed / total if last else mixed)
    mixed = jnp.concatenate(mixes, axis=0)
    if last:
        out_ref[:, lanes] = jnp.transpose(mixed).astype(BF16)
        for head in range(2):
            stat_out[pair, head : head + 1, :] = maxima[head] + jnp.log2(totals[head])
    else:
        out_ref[lanes, :] = mixed
        for head in range(2):
            stat_out[pair, head : head + 1, :] = maxima[head]
            stat_out[pair, 2 + head : 3 + head, :] = totals[head]


def pair_block(rows, lanes):
    return pl.BlockSpec((None, rows, lanes), lambda j, *_: (j, 0, 0))


def forward_block(here, exts, small, w_query, w_kv, query_row, query, state, last):
    count = len(exts)
    rows = query_row.shape[1]
    width = exts[0].shape[1]
    pairs = width // LANES
    first = state is None
    args = [*exts, small, w_kv, query_row]
    out_shapes = [far_struct((pairs, rows, 2 * LANES), BF16)] * count
    out_specs = [pair_block(rows, 2 * LANES)] * count
    if first:
        args += [w_query]
        out_shapes.append(struct((pairs, rows, LANES), BF16))
        out_specs.append(near())
    else:
        args += [query, *state]
    out_shapes += [
        struct((rows, width), BF16) if last else struct((width, rows), F32),
        struct((pairs, 4, rows), F32),
    ]
    out_specs += [near(), near()]
    in_specs = [near()] * len(args)
    result = call(
        functools.partial(forward_kernel, count, first, last),
        here,
        args,
        in_specs,
        out_shapes,
        out_specs,
        grid=(pairs,),
        scratch=[pltpu.VMEM((count * rows, width), BF16), pltpu.VMEM((count * rows, rows), F32)],
        limit=16 << 20,
        cost=pl.CostEstimate(
            flops=24 * count * rows * rows * width,
            bytes_accessed=8 * rows * width,
            transcendentals=count * rows * rows * H,
        ),
    )
    kvs, rest = result[:count], result[count:]
    if first:
        query, rest = rest[0], rest[1:]
    return kvs, query, tuple(rest[::-1]) if not last else tuple(rest)


def backward_kernel(count, first, last, here_ref, *refs):
    q_ref, do_ref, o_ref, stat_ref, wkv_ref, qid_ref = refs[:6]
    refs = refs[6:]
    exts, kvs, refs = refs[:count], refs[count : 2 * count], refs[2 * count :]
    if not first:
        dq_ref, refs = refs[0], refs[1:]
    if last:
        wq_ref, refs = refs[0], refs[1:]
    dq_out, sum_ref, refs = refs[0], refs[1], refs[2:]
    dkv_outs, parts, refs = refs[:count], refs[count : 2 * count], refs[2 * count :]
    (mask_ref,) = refs
    rows = do_ref.shape[0]
    pair = pl.program_id(0)
    lanes = pl.ds(pl.multiple_of(pair * LANES, LANES), LANES)

    @pl.when(pair == 0)
    def _():
        mask_ref[...] = id_mask(exts, rows, qid_ref[0:1, :])
        for part in parts:
            part[...] = jnp.zeros_like(part)

    query = q_ref[pair]
    grad = do_ref[:, lanes]
    both = stack(kvs)
    keys, values = both[:, :LANES], both[:, LANES:]
    low = low_lanes(query.shape)
    key_low = low_lanes(keys.shape)
    zero = jnp.zeros_like(query)
    flipped = jnp.transpose(grad.astype(F32) * o_ref[:, lanes].astype(F32))
    sides = (low, ~low)
    queries = [jnp.where(side, query, zero) for side in sides]
    grads = [jnp.where(side, grad, zero) for side in sides]
    all_scores = contract_cols(keys, jnp.concatenate(queries, axis=0))
    all_changes = contract_cols(values, jnp.concatenate(grads, axis=0))
    dk = dv = dq = None
    for head in range(2):
        span = slice(head * rows, (head + 1) * rows)
        delta = jnp.sum(flipped[head * DH : (head + 1) * DH, :], axis=0, keepdims=True)
        scores = all_scores[:, span] * (0.125 * LOG2E) + mask_ref[...]
        portion = jnp.exp2(scores - stat_ref[pair, head : head + 1, :])
        score_grad = (portion * (all_changes[:, span] - delta)).astype(BF16)
        keys_here = jnp.where(key_low if head == 0 else ~key_low, keys, jnp.zeros_like(keys))
        dv_here = product(portion.astype(BF16), grads[head])
        dk_here = product(score_grad, queries[head])
        dq_here = contract_rows(score_grad, keys_here)
        if head == 0:
            dk, dv, dq = dk_here, dv_here, dq_here
        else:
            dk, dv, dq = dk + dk_here, dv + dv_here, dq + dq_here
    dk = (dk * 0.125).astype(BF16)
    dv = dv.astype(BF16)
    dq = dq * 0.125
    if not first:
        dq = dq + dq_ref[pair]
    both = jnp.concatenate([dk, dv], axis=1)
    sum_ref[pair, 0:1, :] = jnp.sum(both.astype(F32), axis=0, keepdims=True)
    part = contract_cols(both, wkv_ref[pair])
    for index in range(count):
        span = slice(index * rows, (index + 1) * rows)
        dkv_outs[index][...] = both[span]
        term = part[span]
        if last and index == count - 1:
            dq = dq.astype(BF16)
            sum_ref[pair, 1:2, :LANES] = jnp.sum(dq.astype(F32), axis=0, keepdims=True)
            term = term + contract_cols(dq, wq_ref[pair])
        parts[index][...] += term
    dq_out[pair] = dq


def backward_block(here, query, grad, mixed, stats, kvs, w_query, w_kv, query_row, exts, dq, last):
    count = len(exts)
    rows, width = grad.shape
    pairs = width // LANES
    first = dq is None
    both = pair_block(rows, 2 * LANES)
    args = [query, grad, mixed, stats, w_kv, query_row, *exts, *far(*kvs)]
    in_specs = [near()] * (6 + count) + [both] * count
    if not first:
        in_specs.append(near())
        args.append(dq)
    if last:
        in_specs.append(near())
        args.append(w_query)
    result = call(
        functools.partial(backward_kernel, count, first, last),
        here,
        args,
        in_specs,
        [struct((pairs, rows, LANES), BF16 if last else F32), struct((pairs, 8, 2 * LANES), F32)]
        + [far_struct((pairs, rows, 2 * LANES), BF16)] * count
        + [struct((rows, width), F32)] * count,
        [near(), near()] + [both] * count + [near()] * count,
        grid=(pairs,),
        scratch=[pltpu.VMEM((count * rows, rows), F32)],
        limit=16 << 20,
        cost=pl.CostEstimate(
            flops=40 * count * rows * rows * width,
            bytes_accessed=16 * rows * width,
            transcendentals=count * rows * rows * H,
        ),
    )
    dq, sums, rest = result[0], result[1], result[2:]
    return dq, sums, rest[:count], rest[count:]


def transposed_slots(here_ref, values, slots, block_rows, plain_ref, out_ref):
    plain_ref[...] = jnp.transpose(values.astype(F32)).astype(BF16)
    for index, xor in enumerate(slots):
        start = pl.multiple_of((here_ref[0] ^ xor) * block_rows, 8)
        out_ref[index * block_rows : (index + 1) * block_rows, :] = plain_ref[pl.ds(start, block_rows), :]


def middle_kernel(places, block_rows, slots, kept, tile, here_ref, *refs):
    count = len(places)
    frames_ref, mixed_ref, cot_ref, small_ref = refs[:4]
    pieces, refs = refs[4 : 4 + count], refs[4 + count :]
    out_ref, dr_ref, doh_ref, sum_ref = refs[:4]
    grads, refs = refs[4 : 4 + len(kept)], refs[4 + len(kept) :]
    (
        w_ref,
        stage_ref,
        last_ref,
        normed_ref,
        back_ref,
        act_ref,
        half_ref,
        act_flip,
        half_flip,
        plain_ref,
        bias_ref,
        bias_sum,
        in_sems,
        out_sems,
        last_sems,
    ) = refs
    width = frames_ref.shape[1]
    hidden = bias_ref.shape[1]

    copies = []
    for index, (piece, (xor, first, column)) in enumerate(zip(pieces, places)):
        start = first_row(here_ref, block_rows, xor, first)
        height, span = piece.shape
        target = w_ref.at[pl.ds(start, height), column : column + span]
        copies.append(pltpu.make_async_copy(piece, target, in_sems.at[index]))
    for copy in copies:
        copy.start()
    cot = cot_ref[...]
    half_ref[...] = cot.astype(BF16)
    transposed_slots(here_ref, half_ref[...], slots, block_rows, plain_ref, half_flip)
    for index in range(4):
        bias_ref[:, index * width : (index + 1) * width] = small_ref[8 + index : 9 + index, :]
    sum_ref[3:4, :] = jnp.sum(cot, axis=0, keepdims=True)
    for copy in copies:
        copy.wait()

    resid = frames_ref[...] + product(mixed_ref[...], w_ref[:, :width]) + small_ref[4:5, :]
    normed, inv_std = normalize(resid)
    normed_ref[...] = normed
    act_ref[...] = (normed * small_ref[5:6, :] + small_ref[6:7, :]).astype(BF16)
    out_ref[...] = resid + small_ref[7:8, :]
    back_ref[...] = jnp.zeros_like(back_ref)
    transposed_slots(here_ref, act_ref[...], slots, block_rows, plain_ref, act_flip)

    def send(source, column, start, size, sems):
        moves = []
        first = 0
        for index, (grad, height) in enumerate(zip(grads, kept)):
            moves.append(
                pltpu.make_async_copy(
                    source.at[first : first + height, column : column + size],
                    grad.at[:, pl.ds(start, size)],
                    sems.at[index],
                )
            )
            first += height
        return moves

    tiles = hidden // tile

    def columns(index):
        up = pl.multiple_of(width + index * tile, LANES)
        down = pl.multiple_of(width + hidden + index * tile, LANES)
        return up, down, pl.multiple_of(index * tile, LANES)

    def moves_of(index):
        up, down, _ = columns(index)
        slot = lax.rem(index, 2)
        stage = stage_ref.at[slot]
        return send(stage, 0, up, tile, out_sems.at[slot, 0]) + send(
            stage, tile, down, tile, out_sems.at[slot, 1]
        )

    def body(index, carry):
        up, down, at = columns(index)
        slot = lax.rem(index, 2)

        @pl.when(index >= 2)
        def _():
            for move in moves_of(index - 2):
                move.wait()

        w_up = w_ref[:, pl.ds(up, tile)]
        w_down = w_ref[:, pl.ds(down, tile)]
        u = product(act_ref[...], w_up) + bias_ref[:, pl.ds(at, tile)]
        rise = 0.5 * (1.0 + lax.erf(u * ROOT_HALF))
        slope = rise + u * jnp.exp(-0.5 * u * u) * INV_ROOT_TAU
        value = (u * rise).astype(BF16)
        out_ref[...] += contract_cols(value, w_down)
        du = product(half_ref[...], w_down) * slope
        bias_sum[:, pl.ds(at, tile)] = jnp.sum(du, axis=0, keepdims=True)
        du = du.astype(BF16)
        back_ref[...] += contract_cols(du, w_up)
        stage_ref[slot, :, :tile] = product(act_flip[...], du).astype(BF16)
        stage_ref[slot, :, tile:] = product(half_flip[...], value).astype(BF16)
        for move in moves_of(index):
            move.start()
        return carry

    lax.fori_loop(0, tiles, body, 0)

    incoming = back_ref[...]
    normed = normed_ref[...]
    dr = cot_ref[...] + norm_backward(incoming, normed, inv_std, small_ref[5:6, :])
    dr_ref[...] = dr
    sum_ref[0:1, :] = jnp.sum(dr, axis=0, keepdims=True)
    sum_ref[1:2, :] = jnp.sum(incoming * normed, axis=0, keepdims=True)
    sum_ref[2:3, :] = jnp.sum(incoming, axis=0, keepdims=True)
    for index in range(4):
        sum_ref[4 + index : 5 + index, :] = bias_sum[:, index * width : (index + 1) * width]
    drh = dr.astype(BF16)
    transposed_slots(here_ref, mixed_ref[...], slots, block_rows, plain_ref, act_flip)
    last_ref[...] = product(act_flip[...], drh).astype(BF16)
    finals = send(last_ref, 0, 0, width, last_sems)
    for move in finals:
        move.start()
    doh_ref[...] = contract_cols(drh, w_ref[:, :width]).astype(BF16)
    for index in range(max(tiles - 2, 0), tiles):
        finals = finals + moves_of(jnp.int32(index))
    for move in finals:
        move.wait()


def middle(here, frames, mixed, cot, small, pieces, rows_total, block_rows):
    rows, width = frames.shape
    starts = [0, pieces[0][0][0].shape[1]]
    columns = starts[1] + pieces[1][0][0].shape[1]
    pieces = [(*piece, start) for part, start in zip(pieces, starts) for piece in part]
    hidden = (columns - width) // 2
    tile = 2 * LANES
    kept, given = own_slots()
    heights = [len(part) * block_rows for part in (kept, given) if part]
    anywhere = pl.BlockSpec(memory_space=pl.ANY)
    full = whole_block((rows, width))
    outs = [struct((rows, width), F32), struct((rows, width), F32), struct((rows, width), BF16), struct((8, width), F32)]
    return call(
        functools.partial(
            middle_kernel, [p[1:] for p in pieces], block_rows, kept + given, heights, tile
        ),
        here,
        [frames, mixed, cot, small, *[p[0] for p in pieces]],
        [full, full, full, pl.BlockSpec((16, width), lambda *_: (0, 0))] + [anywhere] * len(pieces),
        outs + [struct((height, columns), BF16) for height in heights],
        [full, full, full, whole_block((8, width))] + [anywhere] * len(heights),
        scratch=[
            pltpu.VMEM((rows_total, columns), BF16),
            pltpu.VMEM((2, rows_total, 2 * tile), BF16),
            pltpu.VMEM((rows_total, width), BF16),
            pltpu.VMEM((rows, width), F32),
            pltpu.VMEM((rows, width), F32),
            pltpu.VMEM((rows, width), BF16),
            pltpu.VMEM((rows, width), BF16),
            pltpu.VMEM((width, rows), BF16),
            pltpu.VMEM((width, rows), BF16),
            pltpu.VMEM((width, rows), BF16),
            pltpu.VMEM((1, hidden), F32),
            pltpu.VMEM((1, hidden), F32),
            pltpu.SemaphoreType.DMA((len(pieces),)),
            pltpu.SemaphoreType.DMA((2, 2, len(heights))),
            pltpu.SemaphoreType.DMA((len(heights),)),
        ],
        limit=30 << 20,
        cost=pl.CostEstimate(
            flops=36 * rows * width * hidden // 3, bytes_accessed=4 * rows_total * columns, transcendentals=2 * rows * hidden
        ),
    )


def cross_kernel(ring, slots, block_rows, heights, here_ref, *refs):
    exts, refs = refs[:ring], refs[ring:]
    dq_ref, refs = refs[0], refs[1:]
    dkvs, refs = refs[:ring], refs[ring:]
    sums, refs = refs[:ring], refs[ring:]
    mid_ref, wkv_ref, wq_ref, cols_ref, refs = refs[0], refs[1], refs[2], refs[3], refs[4:]
    outs, refs = refs[: len(heights)], refs[len(heights) :]
    flip_ref, plain_ref, gain_ref, side_ref, turned_ref, shift_ref, line_ref = refs
    step = pl.program_id(0)
    rows = dq_ref.shape[1]
    width = plain_ref.shape[0]
    pairs = width // LANES

    def slot_rows(index):
        start = pl.multiple_of((here_ref[0] ^ slots[index]) * block_rows, 8)
        return pl.ds(start, block_rows), pl.ds(index * block_rows, block_rows)

    @pl.when(step == 0)
    def _():
        for index in range(ring):
            plain_ref[...] = jnp.transpose(exts[index][:rows, :].astype(F32)).astype(BF16)
            for slot in range(len(slots)):
                source, target = slot_rows(slot)
                flip_ref[target, index * rows : (index + 1) * rows] = plain_ref[source, :]
        for slot in range(len(slots)):
            source, target = slot_rows(slot)
            side = cols_ref[source, :].astype(F32)
            side_ref[target, :] = jnp.broadcast_to(side[:, 0:1], side.shape)
            turned_ref[target, :] = jnp.broadcast_to(side[:, 1:2], side.shape)
        gain_ref[...] = jnp.zeros_like(gain_ref)
        shift_ref[...] = jnp.zeros_like(shift_ref)
        line_ref[...] = jnp.zeros_like(line_ref)

    def finish(crossed, line, weights, columns):
        wide = jnp.broadcast_to(line, (8, 2 * LANES))
        high = wide.astype(BF16)
        low = (wide - high.astype(F32)).astype(BF16)
        full = weights[...] if len(weights.shape) == 2 else jnp.concatenate([weights[0], weights[1]], axis=1)
        shift_ref[...] += contract_cols(high, full) + contract_cols(low, full)
        for index in range(len(slots)):
            source, target = slot_rows(index)
            part = crossed[index * block_rows : (index + 1) * block_rows, :]
            gain, shift = side_ref[target, :], turned_ref[target, :]
            out = 0 if index * block_rows < heights[0] else 1
            first = index * block_rows - (heights[0] if out else 0)
            total = gain_ref[target, :]
            for half in range(2):
                lanes = slice(half * LANES, (half + 1) * LANES)
                if len(weights.shape) == 2:
                    weight = weights[source, lanes]
                else:
                    weight = weights[half, source, :]
                total = total + weight.astype(F32) * part[:, lanes]
                grad = gain * part[:, lanes] + shift * line[:, lanes]
                outs[out][first : first + block_rows, pl.ds(columns[half], LANES)] = grad.astype(BF16)
            gain_ref[target, :] = total

    @pl.when(step < pairs)
    def _():
        crossed = product(flip_ref[:, :rows], dkvs[0][...])
        for index in range(1, ring):
            crossed += product(flip_ref[:, index * rows : (index + 1) * rows], dkvs[index][...])
        line = sums[0][step, 0:1, :]
        for other in sums[1:]:
            line = line + other[step, 0:1, :]
        at = pl.multiple_of(step * LANES, LANES)
        line_ref[3:4, pl.ds(at, LANES)] = line[:, LANES:]
        finish(crossed, line, wkv_ref, (at + width, at + 2 * width))

    @pl.when(step >= pairs)
    def _():
        pair = 2 * (step - pairs)
        grads = jnp.concatenate([dq_ref[0], dq_ref[1]], axis=1)
        line = jnp.concatenate(
            [sums[-1][pair, 1:2, :LANES], sums[-1][pair + 1, 1:2, :LANES]], axis=1
        )
        at = pl.multiple_of(pair * LANES, LANES)
        line_ref[2:3, pl.ds(at, 2 * LANES)] = line
        finish(product(flip_ref[:, :rows], grads), line, wq_ref, (at, at + LANES))

    @pl.when(step == pl.num_programs(0) - 1)
    def _():
        line_ref[1:2, :] = shift_ref[0:1, :]
        line_ref[4:12, :] = mid_ref[...]
        turned_ref[...] = jnp.transpose(line_ref[...])
        lane = lax.broadcasted_iota(jnp.int32, (block_rows, LANES), 1)
        for index in range(len(slots)):
            source, target = slot_rows(index)
            gain = jnp.sum(gain_ref[target, :], axis=1, keepdims=True)
            value = jnp.where(lane == 0, gain, turned_ref[source, :])
            out = 0 if index * block_rows < heights[0] else 1
            start = index * block_rows - (heights[0] if out else 0)
            outs[out][start : start + block_rows, 3 * width :] = value.astype(BF16)


def cross(here, exts, dq, dkvs, sums, mid_sums, w_query, w_kv, side, block_rows):
    ring = len(exts)
    pairs, rows, _ = dq.shape
    width = pairs * LANES
    kept, given = own_slots()
    heights = [len(part) * block_rows for part in (kept, given) if part]
    columns = 3 * width + LANES

    def kv_spec(height):
        return pl.BlockSpec(
            (None, height, 2 * LANES), lambda j, *_: (jnp.minimum(j, pairs - 1), 0, 0)
        )

    def q_spec(height):
        return pl.BlockSpec((2, height, LANES), lambda j, *_: (jnp.maximum(j - pairs, 0), 0, 0))

    return call(
        functools.partial(cross_kernel, ring, kept + given, block_rows, heights),
        here,
        [*exts, dq, *far(*dkvs), *sums, mid_sums, w_kv, w_query, side],
        [near()] * ring
        + [q_spec(rows)]
        + [kv_spec(rows)] * ring
        + [near()] * (ring + 1)
        + [kv_spec(width), q_spec(width), near()],
        [struct((height, columns), BF16) for height in heights],
        [near()] * len(heights),
        grid=(pairs + pairs // 2,),
        scratch=[
            pltpu.VMEM((width, ring * rows), BF16),
            pltpu.VMEM((width, rows), BF16),
            pltpu.VMEM((width, LANES), F32),
            pltpu.VMEM((width, LANES), F32),
            pltpu.VMEM((width, LANES), F32),
            pltpu.VMEM((8, width), F32),
            pltpu.VMEM((LANES, width), F32),
        ],
        limit=20 << 20,
        cost=pl.CostEstimate(
            flops=2 * rows * width * width * (2 * ring + 1), bytes_accessed=2 * width * columns * 3, transcendentals=0
        ),
    )


def add_up(terms, start, stop):
    value = terms[0][:, start:stop].astype(F32)
    for term in terms[1:]:
        value = value + term[:, start:stop].astype(F32)
    return value


def wide_kernel(count, width, *refs):
    terms, refs = refs[:count], refs[count:]
    weight, first, second, grad_out, weight_out, first_out, second_out = refs
    hidden = weight.shape[2]
    spans = ((0, 3 * width, 0, width), (1, 0, width, hidden), (2, 0, width + hidden, hidden))
    for matrix, column, start, size in spans:
        grad = add_up(terms, start, start + size)
        at = slice(column, column + size)
        new_weight, new_first, new_second = adam_update(
            weight[matrix, :, at], grad, first[matrix, :, at], second[matrix, :, at], WEIGHT_DECAY, LEARN_RATE
        )
        grad_out[matrix, :, at] = grad
        weight_out[matrix, :, at] = new_weight
        first_out[matrix, :, at] = new_first
        second_out[matrix, :, at] = new_second


def wide_update(terms, width, mats, mats_m, mats_v):
    block = whole_block(mats.shape)
    return pl.pallas_call(
        functools.partial(wide_kernel, len(terms), width),
        grid=(1,),
        in_specs=[whole_block(term.shape) for term in terms] + [block] * 3,
        out_specs=[block] * 4,
        out_shape=[far_struct(mats.shape, F32)] * 4,
        compiler_params=pltpu.CompilerParams(vmem_limit_bytes=16 << 20),
        name="wide_update",
    )(*terms, *far(mats, mats_m, mats_v))


def narrow_kernel(count, *refs):
    terms, refs = refs[:count], refs[count:]
    weight, first, second, small, small_first, small_second = refs[:6]
    outs = refs[10:]
    size = weight.shape[2]
    grad = add_up(terms, 0, size)
    results = adam_update(weight[0], grad, first[0], second[0], WEIGHT_DECAY, LEARN_RATE)
    for out, value in zip(outs[:4], (grad, *results)):
        out[0] = value
    grad = jnp.transpose(add_up(terms, size, terms[0].shape[1]))[: small.shape[0], :]
    results = adam_update(small[...], grad, small_first[...], small_second[...], 0.0, SMALL_RATE)
    for out, value in zip(outs[4:], (grad, *results)):
        out[...] = value


def narrow_update(terms, width, mats, mats_m, mats_v, smalls, smalls_m, smalls_v, outs):
    count = len(terms)
    rows = mats.shape[1]
    block = pl.BlockSpec((1, rows, 3 * width), lambda i: (0, 0, 0))
    small = whole_block(smalls.shape)
    return pl.pallas_call(
        functools.partial(narrow_kernel, count),
        grid=(1,),
        in_specs=[whole_block(term.shape) for term in terms]
        + [block] * 3
        + [small] * 3
        + [pl.BlockSpec(memory_space=pl.ANY)] * 4,
        out_specs=[block] * 4 + [small] * 4,
        out_shape=[far_struct(mats.shape, F32)] * 4 + [struct(smalls.shape, F32)] * 4,
        input_output_aliases={count + 6 + index: index for index in range(4)},
        compiler_params=pltpu.CompilerParams(vmem_limit_bytes=12 << 20),
        name="narrow_update",
    )(*terms, *far(mats, mats_m, mats_v), smalls, smalls_m, smalls_v, *outs)


def groups(ring):
    ahead = [[i] for i in range(ring)]
    order = list(range(1, ring)) + [0]
    return ahead, [[i] for i in order]


def shards(frames, clip_ids, cotangent, mats, smalls, mats_m, mats_v, smalls_m, smalls_v):
    inputs = frames[0]
    upstream = cotangent[0]
    tok_rows, width = inputs.shape
    ring = lax.axis_size("seq")
    devices = ring * lax.axis_size("dp")
    block_rows = ring * mats.shape[1]
    total_rows = devices * mats.shape[1]
    here_dp = lax.axis_index("dp") if tuned() else jnp.int32(0)
    here = jnp.stack([here_dp, lax.axis_index("seq")]).astype(jnp.int32)

    normed_one, inv_one = normalize(inputs)
    id_row = clip_ids.astype(F32)
    id_rows = jnp.pad(id_row, ((0, 7), (0, width - tok_rows))).astype(BF16)
    piece = jnp.concatenate([normed_one.astype(BF16), id_rows], axis=0)
    normed_one, inv_one, piece = lax.optimization_barrier((normed_one, inv_one, piece))
    exts = [piece]
    for _ in range(1, ring):
        exts.append(turn(exts[-1]))

    mats_half = mats.astype(BF16)
    small_columns = jnp.pad(
        jnp.transpose(smalls.astype(BF16).astype(F32)), ((0, 0), (0, LANES - smalls.shape[0]))
    ).astype(BF16)
    chunk = jnp.concatenate([mats_half[0][:, : 3 * width], small_columns], axis=1)
    w_query, w_kv, side, small = assemble(
        gather_pieces(chunk, here, True), here, total_rows, block_rows
    )
    chunk = jnp.concatenate([mats_half[0][:, 3 * width :], mats_half[1]], axis=1)
    wide_pieces = [gather_pieces(chunk, here, False), gather_pieces(mats_half[2], here, False)]

    query, state = None, None
    kvs = [None] * ring
    ahead, back = groups(ring)
    for group in ahead:
        some, query, state = forward_block(
            here, [exts[i] for i in group], small, w_query, w_kv, id_row, query, state, group is ahead[-1]
        )
        for index, kv in zip(group, some):
            kvs[index] = kv
    mixed_half, stats = state

    output, grad_resid, grad_heads, mid_sums, *wide_grads = middle(
        here, inputs, mixed_half, upstream, small, wide_pieces, total_rows, block_rows
    )
    wide_terms = scatter_parts(wide_grads[0], wide_grads[-1], here, 3 * width)

    dq = None
    riding = None
    dkvs, sums = [None] * ring, []
    for group in back:
        dq, some, new_dkvs, parts = backward_block(
            here,
            query,
            grad_heads,
            mixed_half,
            stats,
            [kvs[i] for i in group],
            w_query,
            w_kv,
            id_row,
            [exts[i] for i in group],
            dq,
            group is back[-1],
        )
        sums.append(some)
        for index, dkv, part in zip(group, new_dkvs, parts):
            dkvs[index] = dkv
            if riding is not None:
                part = part + riding.astype(F32)
            if index:
                riding = turn(part.astype(BF16))
            else:
                grad_act_one = part

    cross_grads = cross(here, exts, dq, dkvs, sums, mid_sums, w_query, w_kv, side, block_rows)
    cross_terms = scatter_parts(cross_grads[0], cross_grads[-1], here, cross_grads[0].shape[1])
    grad_inputs = grad_resid + norm_backward(grad_act_one, normed_one, inv_one, small[0])

    begun = wide_update(wide_terms, width, mats, mats_m, mats_v)
    updated = narrow_update(
        cross_terms, width, mats, mats_m, mats_v, smalls, smalls_m, smalls_v, begun
    )
    mats_grad, new_mats, new_mats_m, new_mats_v = updated[:4]
    smalls_grad, new_smalls, new_smalls_m, new_smalls_v = updated[4:]
    return (
        output[None],
        grad_inputs[None],
        mats_grad,
        smalls_grad,
        new_mats,
        new_smalls,
        new_mats_m,
        new_mats_v,
        new_smalls_m,
        new_smalls_v,
    )


def solution(mesh):
    in_specs = (
        P("dp", "seq", None),
        P("dp", "seq"),
        P("dp", "seq", None),
        P(None, ("dp", "seq"), None),
        P(None, ("dp", "seq")),
        P(None, ("dp", "seq"), None),
        P(None, ("dp", "seq"), None),
        P(None, ("dp", "seq")),
        P(None, ("dp", "seq")),
    )
    out_specs = (
        P("dp", "seq", None),
        P("dp", "seq", None),
        P(None, ("dp", "seq"), None),
        P(None, ("dp", "seq")),
        P(None, ("dp", "seq"), None),
        P(None, ("dp", "seq")),
        P(None, ("dp", "seq"), None),
        P(None, ("dp", "seq"), None),
        P(None, ("dp", "seq")),
        P(None, ("dp", "seq")),
    )

    return jax.shard_map(shards, mesh=mesh, in_specs=in_specs, out_specs=out_specs, check_vma=False)
```

```python
import functools

import jax
import jax.numpy as jnp
from jax import lax
from jax.experimental import pallas as pl
from jax.experimental.pallas import tpu as pltpu
from jax.sharding import PartitionSpec as P


H = 12
DH = 64
STEP = 3
LANES = 128

NEGATIVE_FILL = -1e30
NORM_EPSILON = 1e-05
ROOT_HALF = 0.7071067811865476
INV_ROOT_TAU = 0.3989422804014327
LOG2E = 1.4426950408889634
BETA_FIRST = 0.9
BETA_SECOND = 0.95
LEARN_RATE = 0.01
SMALL_RATE = 0.1
WEIGHT_DECAY = 0.1
ADAM_EPSILON = 1e-08


F32 = jnp.float32
BF16 = jnp.bfloat16


def contract_rows(left, right):
    return lax.dot_general(left, right, (((0,), (0,)), ((), ())), preferred_element_type=F32)


def contract_cols(left, right):
    return lax.dot_general(left, right, (((1,), (1,)), ((), ())), preferred_element_type=F32)


def product(left, right):
    return jnp.dot(left, right, preferred_element_type=F32)


def normalize(values):
    row_mean = jnp.mean(values, axis=-1, keepdims=True)
    center = values - row_mean
    row_var = jnp.mean(center * center, axis=-1, keepdims=True)
    inv_std = lax.rsqrt(row_var + NORM_EPSILON)
    return center * inv_std, inv_std


def norm_backward(incoming, normed, inv_std, gain_vec):
    scaled = incoming * gain_vec
    return inv_std * (
        scaled
        - jnp.mean(scaled, axis=-1, keepdims=True)
        - normed * jnp.mean(scaled * normed, axis=-1, keepdims=True)
    )


def adam_update(weight, gradient, first, second, decay, step_rate):
    first_new = BETA_FIRST * first + (1.0 - BETA_FIRST) * gradient
    second_new = BETA_SECOND * second + (1.0 - BETA_SECOND) * gradient * gradient
    first_hat = first_new / (1.0 - BETA_FIRST**STEP)
    second_hat = second_new / (1.0 - BETA_SECOND**STEP)
    weight_new = weight - step_rate * (
        first_hat / (jnp.sqrt(second_hat) + ADAM_EPSILON) + decay * weight
    )
    return (weight_new, first_new, second_new)


def turn(block, step=1):
    count = lax.axis_size("seq")
    return lax.ppermute(block, "seq", [(i, (i + step) % count) for i in range(count)])


def swap(block, bit):
    count = lax.axis_size("dp")
    return lax.ppermute(block, "dp", [(i, i ^ bit) for i in range(count)])


def tuned():
    return lax.axis_size("dp") == 8 and lax.axis_size("seq") == 4


def call(kernel, here, ins, in_specs, out_shapes, out_specs, grid=(1,), scratch=(), limit=None, cost=None):
    return pl.pallas_call(
        kernel,
        grid_spec=pltpu.PrefetchScalarGridSpec(
            num_scalar_prefetch=1,
            grid=grid,
            in_specs=in_specs,
            out_specs=out_specs,
            scratch_shapes=list(scratch),
        ),
        out_shape=out_shapes,
        compiler_params=pltpu.CompilerParams(vmem_limit_bytes=limit),
        cost_estimate=cost,
    )(here, *ins)


def whole_block(shape):
    return pl.BlockSpec(shape, lambda *_: (0,) * len(shape), pipeline_mode=pl.Buffered(1))


def struct(shape, dtype):
    return jax.ShapeDtypeStruct(shape, dtype)


def far_struct(shape, dtype):
    return pltpu.HBM(shape, dtype)


def near():
    return pl.BlockSpec(memory_space=pltpu.VMEM)


def far(*arrays):
    return [pltpu.with_memory_space_constraint(array, pltpu.HBM) for array in arrays]


def pack_kernel(here_ref, *refs):
    *pieces, out = refs
    ring = len(pieces)
    for step, piece in enumerate(pieces):
        place = lax.rem(here_ref[1] - step + ring, ring)
        out[pl.ds(place, 1)] = piece[...][None]


def gather_pieces(shard, here, direct):
    ring = lax.axis_size("seq")
    rows, columns = shard.shape
    if not tuned():
        return [(lax.all_gather(shard, ("dp", "seq"), axis=0, tiled=True), None, 0)]
    pieces = [shard]
    for step in range(1, ring):
        if direct:
            pieces.append(turn(shard, step))
        else:
            pieces.append(turn(pieces[-1]))
    block = call(
        pack_kernel,
        here,
        pieces,
        [near()] * ring,
        struct((ring, rows, columns), shard.dtype),
        near(),
        limit=2 << 20,
    ).reshape(ring * rows, columns)
    half = ring * rows // 2
    from_x = swap(block, 2)
    from_y = swap(block, 4)
    low = swap(from_x[:half], 4)
    high = swap(from_y[half:], 2)
    held = [(block, 0, 0), (from_x, 2, 0), (from_y, 4, 0), (low, 6, 0), (high, 6, half)]
    other = [
        (swap(piece, 1), xor ^ 1, first)
        for piece, xor, first in held
    ]
    return held + other


def first_row(here_ref, block_rows, xor, first):
    if xor is None:
        return 0
    return pl.multiple_of((here_ref[0] ^ xor) * block_rows + first, 8)


def assemble_kernel(block_rows, places, here_ref, *refs):
    *pieces, wq_out, wkv_out, side_out, rows_out = refs
    pairs = wq_out.shape[0]
    for piece, (xor, first) in zip(pieces, places):
        at = pl.ds(first_row(here_ref, block_rows, xor, first), piece.shape[0])

        def lanes(index):
            return piece[:, index * LANES : (index + 1) * LANES]

        for pair in range(pairs):
            wq_out[pair, at, :] = lanes(pair)
            wkv_out[pair, at, :LANES] = lanes(pairs + pair)
            wkv_out[pair, at, LANES:] = lanes(2 * pairs + pair)
        side_out[at, :] = lanes(3 * pairs)
    rows_out[...] = jnp.transpose(side_out[...].astype(F32))


def assemble(pieces, here, rows, block_rows):
    pairs = pieces[0][0].shape[1] // (3 * LANES)
    shapes = [(pairs, rows, LANES), (pairs, rows, 2 * LANES), (rows, LANES), (LANES, rows)]
    return call(
        functools.partial(assemble_kernel, block_rows, [p[1:] for p in pieces]),
        here,
        [p[0] for p in pieces],
        [near()] * len(pieces),
        [struct(shape, F32 if shape == shapes[-1] else BF16) for shape in shapes],
        [near()] * len(shapes),
        limit=12 << 20,
    )


def join_kernel(here_ref, own_ref, recv_ref, me, x_send, y_send, x_late, y_late):
    rows = me.shape[0]
    half = rows // 2

    def total(slot, first, count):
        part = pl.ds(slot * rows + first, count)
        return (own_ref[part, :].astype(F32) + recv_ref[part, :].astype(F32)).astype(BF16)

    me[...] = total(0, 0, rows)
    x_send[:half, :] = total(3, half, half)
    x_send[half:, :] = total(1, half, half)
    y_send[:half, :] = total(3, 0, half)
    y_send[half:, :] = total(2, 0, half)
    x_late[...] = total(1, 0, half)
    y_late[...] = total(2, half, half)


def close_kernel(ring, here_ref, me, x_early, y_early, x_late, y_late, *refs):
    *outs, total = refs
    half = me.shape[0] // 2
    rows = me.shape[0] // ring
    total[:half, :] = (
        me[:half, :].astype(F32) + y_early[half:, :].astype(F32) + x_late[...].astype(F32)
    )
    total[half:, :] = (
        me[half:, :].astype(F32) + x_early[half:, :].astype(F32) + y_late[...].astype(F32)
    )
    for step, out in enumerate(outs):
        place = lax.rem(here_ref[1] + step, ring)
        out[...] = total[pl.ds(pl.multiple_of(place * rows, 8), rows), :].astype(out.dtype)


def scatter_parts(own, away, here, tile):
    ring = lax.axis_size("seq")
    if not tuned():
        return [lax.psum_scatter(own, ("dp", "seq"), scatter_dimension=0, tiled=True).astype(F32)]
    count, columns = own.shape
    rows = count // 4
    half = rows // 2
    got = swap(away, 1)

    alone = tile == columns

    def spec(height):
        return near() if alone else pl.BlockSpec((height, tile), lambda j, *_: (0, j))

    grid = (columns // tile,)
    heights = (rows, rows, rows, half, half)
    me, x_send, y_send, x_late, y_late = call(
        join_kernel,
        here,
        [own, got],
        [spec(count)] * 2,
        [(struct if alone else far_struct)((rows, columns), BF16)]
        + [struct((height, columns), BF16) for height in heights[1:]],
        [spec(height) for height in heights],
        grid=grid,
        limit=(2 if alone else 18) << 20,
    )
    x_early = swap(x_send, 2)
    y_early = swap(y_send, 4)
    x_sum = (x_late.astype(F32) + y_early[:half].astype(F32)).astype(BF16)
    y_sum = (y_late.astype(F32) + x_early[:half].astype(F32)).astype(BF16)
    x_late = swap(x_sum, 2)
    y_late = swap(y_sum, 4)
    small = rows // ring
    terms = call(
        functools.partial(close_kernel, ring),
        here,
        [*((me,) if alone else far(me)), x_early, y_early, x_late, y_late],
        [spec(height) for height in heights],
        [struct((small, columns), F32 if step == 0 else BF16) for step in range(ring)],
        [spec(small)] * ring,
        grid=grid,
        scratch=[pltpu.VMEM((rows, tile), F32)],
        limit=(3 if alone else 12) << 20,
    )
    return [terms[0]] + [turn(terms[step], step) for step in range(1, ring)]


def own_slots():
    if tuned():
        return [0, 2, 4, 6], [1, 3, 5, 7]
    return list(range(lax.axis_size("dp"))), []


def low_lanes(shape):
    return lax.broadcasted_iota(jnp.int32, shape, 1) < DH


def stack(refs):
    if len(refs) == 1:
        return refs[0][...]
    return jnp.concatenate([ref[...] for ref in refs], axis=0)


def id_mask(exts, rows, query_row):
    masks = []
    for ext in exts:
        key_ids = ext[rows : rows + 8, :rows].astype(F32)[0:1, :]
        key_ids = jnp.transpose(jnp.broadcast_to(key_ids, (LANES, rows)))
        masks.append(jnp.where(key_ids[:, 0:1] == query_row, 0.0, NEGATIVE_FILL))
    return masks[0] if len(masks) == 1 else jnp.concatenate(masks, axis=0)


def forward_kernel(count, first, last, here_ref, *refs):
    exts, refs = refs[:count], refs[count:]
    small_ref, wkv_ref, qid_ref = refs[:3]
    refs = refs[3:]
    if first:
        wq_ref, refs = refs[0], refs[1:]
    else:
        q_ref, stat_ref, acc_ref = refs[:3]
        refs = refs[3:]
    kv_outs, refs = refs[:count], refs[count:]
    if first:
        q_out, refs = refs[0], refs[1:]
    out_ref, stat_out, act_ref, mask_ref = refs
    rows = qid_ref.shape[1]
    pair = pl.program_id(0)
    lanes = pl.ds(pl.multiple_of(pair * LANES, LANES), LANES)

    @pl.when(pair == 0)
    def _():
        for index, ext in enumerate(exts):
            normed = ext[:rows, :].astype(F32)
            act_ref[index * rows : (index + 1) * rows, :] = (
                normed * small_ref[0:1, :] + small_ref[1:2, :]
            ).astype(BF16)
        mask_ref[...] = id_mask(exts, rows, qid_ref[0:1, :])

    both = product(act_ref[...], wkv_ref[pair])
    keys = both[:, :LANES].astype(BF16)
    values = (both[:, LANES:] + small_ref[3:4, lanes]).astype(BF16)
    for index in range(count):
        part = slice(index * rows, (index + 1) * rows)
        kv_outs[index][pair, :, :LANES] = keys[part]
        kv_outs[index][pair, :, LANES:] = values[part]
    if first:
        query = (product(act_ref[:rows, :], wq_ref[pair]) + small_ref[2:3, lanes]).astype(BF16)
        q_out[pair] = query
    else:
        query = q_ref[pair]
    low = low_lanes(query.shape)
    key_low = low_lanes(keys.shape)
    zero = jnp.zeros_like(query)
    one = jnp.ones_like(values)
    maxima, totals, mixes = [], [], []
    for head in range(2):
        here, there = slice(head * DH, (head + 1) * DH), (1 - head) * DH
        side = low if head == 0 else ~low
        key_side = key_low if head == 0 else ~key_low
        scores = contract_cols(keys, jnp.where(side, query, zero)) * (0.125 * LOG2E)
        scores = scores + mask_ref[...]
        top = jnp.max(scores, axis=0, keepdims=True)
        if not first:
            before = stat_ref[pair, head : head + 1, :]
            top = jnp.maximum(top, before)
        portion = jnp.exp2(scores - top).astype(BF16)
        mixed = contract_rows(jnp.where(key_side, values, one), portion)
        total = mixed[there : there + 1, :]
        mixed = mixed[here, :]
        if not first:
            factor = jnp.exp2(before - top)
            total = total + stat_ref[pair, 2 + head : 3 + head, :] * factor
            start = pl.multiple_of(pair * LANES + head * DH, DH)
            mixed = mixed + acc_ref[pl.ds(start, DH), :] * factor
        maxima.append(top)
        totals.append(total)
        mixes.append(mixed / total if last else mixed)
    mixed = jnp.concatenate(mixes, axis=0)
    if last:
        out_ref[:, lanes] = jnp.transpose(mixed).astype(BF16)
        for head in range(2):
            stat_out[pair, head : head + 1, :] = maxima[head] + jnp.log2(totals[head])
    else:
        out_ref[lanes, :] = mixed
        for head in range(2):
            stat_out[pair, head : head + 1, :] = maxima[head]
            stat_out[pair, 2 + head : 3 + head, :] = totals[head]


def forward_block(here, exts, small, w_query, w_kv, query_row, query, state, last):
    count = len(exts)
    rows = query_row.shape[1]
    width = exts[0].shape[1]
    pairs = width // LANES
    first = state is None
    args = [*exts, small, w_kv, query_row]
    out_shapes = [struct((pairs, rows, 2 * LANES), BF16)] * count
    out_specs = [near()] * count
    if first:
        args += [w_query]
        out_shapes.append(struct((pairs, rows, LANES), BF16))
        out_specs.append(near())
    else:
        args += [query, *state]
    out_shapes += [
        struct((rows, width), BF16) if last else struct((width, rows), F32),
        struct((pairs, 4, rows), F32),
    ]
    out_specs += [near(), near()]
    in_specs = [near()] * len(args)
    result = call(
        functools.partial(forward_kernel, count, first, last),
        here,
        args,
        in_specs,
        out_shapes,
        out_specs,
        grid=(pairs,),
        scratch=[pltpu.VMEM((count * rows, width), BF16), pltpu.VMEM((count * rows, rows), F32)],
        limit=16 << 20,
        cost=pl.CostEstimate(
            flops=24 * count * rows * rows * width,
            bytes_accessed=8 * rows * width,
            transcendentals=count * rows * rows * H,
        ),
    )
    kvs, rest = result[:count], result[count:]
    if first:
        query, rest = rest[0], rest[1:]
    return kvs, query, tuple(rest[::-1]) if not last else tuple(rest)


def backward_kernel(count, first, last, here_ref, *refs):
    q_ref, do_ref, o_ref, stat_ref, wkv_ref, qid_ref = refs[:6]
    refs = refs[6:]
    exts, kvs, refs = refs[:count], refs[count : 2 * count], refs[2 * count :]
    if not first:
        dq_ref, refs = refs[0], refs[1:]
    if last:
        wq_ref, refs = refs[0], refs[1:]
    dq_out, sum_ref, refs = refs[0], refs[1], refs[2:]
    dkv_outs, parts, refs = refs[:count], refs[count : 2 * count], refs[2 * count :]
    (mask_ref,) = refs
    rows = do_ref.shape[0]
    pair = pl.program_id(0)
    lanes = pl.ds(pl.multiple_of(pair * LANES, LANES), LANES)

    @pl.when(pair == 0)
    def _():
        mask_ref[...] = id_mask(exts, rows, qid_ref[0:1, :])
        for part in parts:
            part[...] = jnp.zeros_like(part)

    query = q_ref[pair]
    grad = do_ref[:, lanes]
    both = stack([kv.at[pair] for kv in kvs])
    keys, values = both[:, :LANES], both[:, LANES:]
    low = low_lanes(query.shape)
    key_low = low_lanes(keys.shape)
    zero = jnp.zeros_like(query)
    flipped = jnp.transpose(grad.astype(F32) * o_ref[:, lanes].astype(F32))
    sides = (low, ~low)
    queries = [jnp.where(side, query, zero) for side in sides]
    grads = [jnp.where(side, grad, zero) for side in sides]
    all_scores = contract_cols(keys, jnp.concatenate(queries, axis=0))
    all_changes = contract_cols(values, jnp.concatenate(grads, axis=0))
    dk = dv = dq = None
    for head in range(2):
        span = slice(head * rows, (head + 1) * rows)
        delta = jnp.sum(flipped[head * DH : (head + 1) * DH, :], axis=0, keepdims=True)
        scores = all_scores[:, span] * (0.125 * LOG2E) + mask_ref[...]
        portion = jnp.exp2(scores - stat_ref[pair, head : head + 1, :])
        score_grad = (portion * (all_changes[:, span] - delta)).astype(BF16)
        keys_here = jnp.where(key_low if head == 0 else ~key_low, keys, jnp.zeros_like(keys))
        dv_here = product(portion.astype(BF16), grads[head])
        dk_here = product(score_grad, queries[head])
        dq_here = contract_rows(score_grad, keys_here)
        if head == 0:
            dk, dv, dq = dk_here, dv_here, dq_here
        else:
            dk, dv, dq = dk + dk_here, dv + dv_here, dq + dq_here
    dk = (dk * 0.125).astype(BF16)
    dv = dv.astype(BF16)
    dq = dq * 0.125
    if not first:
        dq = dq + dq_ref[pair]
    both = jnp.concatenate([dk, dv], axis=1)
    sum_ref[pair, 0:1, :] = jnp.sum(both.astype(F32), axis=0, keepdims=True)
    part = contract_cols(both, wkv_ref[pair])
    for index in range(count):
        span = slice(index * rows, (index + 1) * rows)
        dkv_outs[index][pair] = both[span]
        term = part[span]
        if last and index == count - 1:
            dq = dq.astype(BF16)
            sum_ref[pair, 1:2, :LANES] = jnp.sum(dq.astype(F32), axis=0, keepdims=True)
            term = term + contract_cols(dq, wq_ref[pair])
        parts[index][...] += term
    dq_out[pair] = dq


def backward_block(here, query, grad, mixed, stats, kvs, w_query, w_kv, query_row, exts, dq, last):
    count = len(exts)
    rows, width = grad.shape
    pairs = width // LANES
    first = dq is None
    args = [query, grad, mixed, stats, w_kv, query_row, *exts, *kvs]
    in_specs = [near()] * (6 + 2 * count)
    if not first:
        in_specs.append(near())
        args.append(dq)
    if last:
        in_specs.append(near())
        args.append(w_query)
    result = call(
        functools.partial(backward_kernel, count, first, last),
        here,
        args,
        in_specs,
        [struct((pairs, rows, LANES), BF16 if last else F32), struct((pairs, 8, 2 * LANES), F32)]
        + [struct((pairs, rows, 2 * LANES), BF16)] * count
        + [struct((rows, width), F32)] * count,
        [near()] * (2 + 2 * count),
        grid=(pairs,),
        scratch=[pltpu.VMEM((count * rows, rows), F32)],
        limit=16 << 20,
        cost=pl.CostEstimate(
            flops=40 * count * rows * rows * width,
            bytes_accessed=16 * rows * width,
            transcendentals=count * rows * rows * H,
        ),
    )
    dq, sums, rest = result[0], result[1], result[2:]
    return dq, sums, rest[:count], rest[count:]


def transposed_slots(here_ref, values, slots, block_rows, plain_ref, out_ref):
    plain_ref[...] = jnp.transpose(values.astype(F32)).astype(BF16)
    for index, xor in enumerate(slots):
        start = pl.multiple_of((here_ref[0] ^ xor) * block_rows, 8)
        out_ref[index * block_rows : (index + 1) * block_rows, :] = plain_ref[pl.ds(start, block_rows), :]


def middle_kernel(places, block_rows, slots, kept, tile, here_ref, *refs):
    count = len(places)
    frames_ref, mixed_ref, cot_ref, small_ref = refs[:4]
    pieces, refs = refs[4 : 4 + count], refs[4 + count :]
    out_ref, dr_ref, doh_ref, sum_ref = refs[:4]
    grads, refs = refs[4 : 4 + len(kept)], refs[4 + len(kept) :]
    (
        w_ref,
        stage_ref,
        last_ref,
        normed_ref,
        back_ref,
        act_ref,
        half_ref,
        act_flip,
        half_flip,
        plain_ref,
        bias_ref,
        bias_sum,
        in_sems,
        out_sems,
        last_sems,
    ) = refs
    width = frames_ref.shape[1]
    hidden = bias_ref.shape[1]

    copies = []
    for index, (piece, (xor, first, column)) in enumerate(zip(pieces, places)):
        start = first_row(here_ref, block_rows, xor, first)
        height, span = piece.shape
        target = w_ref.at[pl.ds(start, height), column : column + span]
        copies.append(pltpu.make_async_copy(piece, target, in_sems.at[index]))
    for copy in copies:
        copy.start()
    cot = cot_ref[...]
    half_ref[...] = cot.astype(BF16)
    transposed_slots(here_ref, half_ref[...], slots, block_rows, plain_ref, half_flip)
    for index in range(4):
        bias_ref[:, index * width : (index + 1) * width] = small_ref[8 + index : 9 + index, :]
    sum_ref[3:4, :] = jnp.sum(cot, axis=0, keepdims=True)
    for copy in copies:
        copy.wait()

    resid = frames_ref[...] + product(mixed_ref[...], w_ref[:, :width]) + small_ref[4:5, :]
    normed, inv_std = normalize(resid)
    normed_ref[...] = normed
    act_ref[...] = (normed * small_ref[5:6, :] + small_ref[6:7, :]).astype(BF16)
    out_ref[...] = resid + small_ref[7:8, :]
    back_ref[...] = jnp.zeros_like(back_ref)
    transposed_slots(here_ref, act_ref[...], slots, block_rows, plain_ref, act_flip)

    def send(source, column, start, size, sems):
        moves = []
        first = 0
        for index, (grad, height) in enumerate(zip(grads, kept)):
            moves.append(
                pltpu.make_async_copy(
                    source.at[first : first + height, column : column + size],
                    grad.at[:, pl.ds(start, size)],
                    sems.at[index],
                )
            )
            first += height
        return moves

    tiles = hidden // tile

    def columns(index):
        up = pl.multiple_of(width + index * tile, LANES)
        down = pl.multiple_of(width + hidden + index * tile, LANES)
        return up, down, pl.multiple_of(index * tile, LANES)

    def moves_of(index):
        up, down, _ = columns(index)
        slot = lax.rem(index, 2)
        stage = stage_ref.at[slot]
        return send(stage, 0, up, tile, out_sems.at[slot, 0]) + send(
            stage, tile, down, tile, out_sems.at[slot, 1]
        )

    def body(index, carry):
        up, down, at = columns(index)
        slot = lax.rem(index, 2)

        @pl.when(index >= 2)
        def _():
            for move in moves_of(index - 2):
                move.wait()

        w_up = w_ref[:, pl.ds(up, tile)]
        w_down = w_ref[:, pl.ds(down, tile)]
        u = product(act_ref[...], w_up) + bias_ref[:, pl.ds(at, tile)]
        rise = 0.5 * (1.0 + lax.erf(u * ROOT_HALF))
        slope = rise + u * jnp.exp(-0.5 * u * u) * INV_ROOT_TAU
        value = (u * rise).astype(BF16)
        out_ref[...] += contract_cols(value, w_down)
        du = product(half_ref[...], w_down) * slope
        bias_sum[:, pl.ds(at, tile)] = jnp.sum(du, axis=0, keepdims=True)
        du = du.astype(BF16)
        back_ref[...] += contract_cols(du, w_up)
        stage_ref[slot, :, :tile] = product(act_flip[...], du).astype(BF16)
        stage_ref[slot, :, tile:] = product(half_flip[...], value).astype(BF16)
        for move in moves_of(index):
            move.start()
        return carry

    lax.fori_loop(0, tiles, body, 0)

    incoming = back_ref[...]
    normed = normed_ref[...]
    dr = cot_ref[...] + norm_backward(incoming, normed, inv_std, small_ref[5:6, :])
    dr_ref[...] = dr
    sum_ref[0:1, :] = jnp.sum(dr, axis=0, keepdims=True)
    sum_ref[1:2, :] = jnp.sum(incoming * normed, axis=0, keepdims=True)
    sum_ref[2:3, :] = jnp.sum(incoming, axis=0, keepdims=True)
    for index in range(4):
        sum_ref[4 + index : 5 + index, :] = bias_sum[:, index * width : (index + 1) * width]
    drh = dr.astype(BF16)
    transposed_slots(here_ref, mixed_ref[...], slots, block_rows, plain_ref, act_flip)
    last_ref[...] = product(act_flip[...], drh).astype(BF16)
    finals = send(last_ref, 0, 0, width, last_sems)
    for move in finals:
        move.start()
    doh_ref[...] = contract_cols(drh, w_ref[:, :width]).astype(BF16)
    for index in range(max(tiles - 2, 0), tiles):
        finals = finals + moves_of(jnp.int32(index))
    for move in finals:
        move.wait()


def middle(here, frames, mixed, cot, small, pieces, rows_total, block_rows):
    rows, width = frames.shape
    starts = [0, pieces[0][0][0].shape[1]]
    columns = starts[1] + pieces[1][0][0].shape[1]
    pieces = [(*piece, start) for part, start in zip(pieces, starts) for piece in part]
    hidden = (columns - width) // 2
    tile = 2 * LANES
    kept, given = own_slots()
    heights = [len(part) * block_rows for part in (kept, given) if part]
    anywhere = pl.BlockSpec(memory_space=pl.ANY)
    full = whole_block((rows, width))
    outs = [struct((rows, width), F32), struct((rows, width), F32), struct((rows, width), BF16), struct((8, width), F32)]
    return call(
        functools.partial(
            middle_kernel, [p[1:] for p in pieces], block_rows, kept + given, heights, tile
        ),
        here,
        [frames, mixed, cot, small, *[p[0] for p in pieces]],
        [full, full, full, pl.BlockSpec((16, width), lambda *_: (0, 0))] + [anywhere] * len(pieces),
        outs + [struct((height, columns), BF16) for height in heights],
        [full, full, full, whole_block((8, width))] + [anywhere] * len(heights),
        scratch=[
            pltpu.VMEM((rows_total, columns), BF16),
            pltpu.VMEM((2, rows_total, 2 * tile), BF16),
            pltpu.VMEM((rows_total, width), BF16),
            pltpu.VMEM((rows, width), F32),
            pltpu.VMEM((rows, width), F32),
            pltpu.VMEM((rows, width), BF16),
            pltpu.VMEM((rows, width), BF16),
            pltpu.VMEM((width, rows), BF16),
            pltpu.VMEM((width, rows), BF16),
            pltpu.VMEM((width, rows), BF16),
            pltpu.VMEM((1, hidden), F32),
            pltpu.VMEM((1, hidden), F32),
            pltpu.SemaphoreType.DMA((len(pieces),)),
            pltpu.SemaphoreType.DMA((2, 2, len(heights))),
            pltpu.SemaphoreType.DMA((len(heights),)),
        ],
        limit=27 << 20,
        cost=pl.CostEstimate(
            flops=36 * rows * width * hidden // 3, bytes_accessed=4 * rows_total * columns, transcendentals=2 * rows * hidden
        ),
    )


def cross_kernel(ring, slots, block_rows, heights, here_ref, *refs):
    exts, refs = refs[:ring], refs[ring:]
    dq_ref, refs = refs[0], refs[1:]
    dkvs, refs = refs[:ring], refs[ring:]
    sums, refs = refs[:ring], refs[ring:]
    mid_ref, wkv_ref, wq_ref, cols_ref, refs = refs[0], refs[1], refs[2], refs[3], refs[4:]
    outs, refs = refs[: len(heights)], refs[len(heights) :]
    flip_ref, plain_ref, gain_ref, side_ref, turned_ref, shift_ref, line_ref = refs
    step = pl.program_id(0)
    rows = dq_ref.shape[1]
    width = plain_ref.shape[0]
    pairs = width // LANES

    def slot_rows(index):
        start = pl.multiple_of((here_ref[0] ^ slots[index]) * block_rows, 8)
        return pl.ds(start, block_rows), pl.ds(index * block_rows, block_rows)

    @pl.when(step == 0)
    def _():
        for index in range(ring):
            plain_ref[...] = jnp.transpose(exts[index][:rows, :].astype(F32)).astype(BF16)
            for slot in range(len(slots)):
                source, target = slot_rows(slot)
                flip_ref[target, index * rows : (index + 1) * rows] = plain_ref[source, :]
        for slot in range(len(slots)):
            source, target = slot_rows(slot)
            side = cols_ref[source, :].astype(F32)
            side_ref[target, :] = jnp.broadcast_to(side[:, 0:1], side.shape)
            turned_ref[target, :] = jnp.broadcast_to(side[:, 1:2], side.shape)
        gain_ref[...] = jnp.zeros_like(gain_ref)
        shift_ref[...] = jnp.zeros_like(shift_ref)
        line_ref[...] = jnp.zeros_like(line_ref)

    def finish(crossed, line, weights, columns):
        wide = jnp.broadcast_to(line, (8, 2 * LANES))
        high = wide.astype(BF16)
        low = (wide - high.astype(F32)).astype(BF16)
        full = weights[...] if len(weights.shape) == 2 else jnp.concatenate([weights[0], weights[1]], axis=1)
        shift_ref[...] += contract_cols(high, full) + contract_cols(low, full)
        for index in range(len(slots)):
            source, target = slot_rows(index)
            part = crossed[index * block_rows : (index + 1) * block_rows, :]
            gain, shift = side_ref[target, :], turned_ref[target, :]
            out = 0 if index * block_rows < heights[0] else 1
            first = index * block_rows - (heights[0] if out else 0)
            total = gain_ref[target, :]
            for half in range(2):
                lanes = slice(half * LANES, (half + 1) * LANES)
                if len(weights.shape) == 2:
                    weight = weights[source, lanes]
                else:
                    weight = weights[half, source, :]
                total = total + weight.astype(F32) * part[:, lanes]
                grad = gain * part[:, lanes] + shift * line[:, lanes]
                outs[out][first : first + block_rows, pl.ds(columns[half], LANES)] = grad.astype(BF16)
            gain_ref[target, :] = total

    @pl.when(step < pairs)
    def _():
        crossed = product(flip_ref[:, :rows], dkvs[0][step])
        for index in range(1, ring):
            crossed += product(flip_ref[:, index * rows : (index + 1) * rows], dkvs[index][step])
        line = sums[0][step, 0:1, :]
        for other in sums[1:]:
            line = line + other[step, 0:1, :]
        at = pl.multiple_of(step * LANES, LANES)
        line_ref[3:4, pl.ds(at, LANES)] = line[:, LANES:]
        finish(crossed, line, wkv_ref.at[step], (at + width, at + 2 * width))

    @pl.when(step >= pairs)
    def _():
        pair = 2 * (step - pairs)
        grads = jnp.concatenate([dq_ref[pair], dq_ref[pair + 1]], axis=1)
        line = jnp.concatenate(
            [sums[-1][pair, 1:2, :LANES], sums[-1][pair + 1, 1:2, :LANES]], axis=1
        )
        at = pl.multiple_of(pair * LANES, LANES)
        line_ref[2:3, pl.ds(at, 2 * LANES)] = line
        finish(product(flip_ref[:, :rows], grads), line, wq_ref.at[pl.ds(pair, 2)], (at, at + LANES))

    @pl.when(step == pl.num_programs(0) - 1)
    def _():
        line_ref[1:2, :] = shift_ref[0:1, :]
        line_ref[4:12, :] = mid_ref[...]
        turned_ref[...] = jnp.transpose(line_ref[...])
        lane = lax.broadcasted_iota(jnp.int32, (block_rows, LANES), 1)
        for index in range(len(slots)):
            source, target = slot_rows(index)
            gain = jnp.sum(gain_ref[target, :], axis=1, keepdims=True)
            value = jnp.where(lane == 0, gain, turned_ref[source, :])
            out = 0 if index * block_rows < heights[0] else 1
            start = index * block_rows - (heights[0] if out else 0)
            outs[out][start : start + block_rows, 3 * width :] = value.astype(BF16)


def cross(here, exts, dq, dkvs, sums, mid_sums, w_query, w_kv, side, block_rows):
    ring = len(exts)
    pairs, rows, _ = dq.shape
    width = pairs * LANES
    kept, given = own_slots()
    heights = [len(part) * block_rows for part in (kept, given) if part]
    columns = 3 * width + LANES

    return call(
        functools.partial(cross_kernel, ring, kept + given, block_rows, heights),
        here,
        [*exts, dq, *dkvs, *sums, mid_sums, w_kv, w_query, side],
        [near()] * (3 * ring + 5),
        [struct((height, columns), BF16) for height in heights],
        [near()] * len(heights),
        grid=(pairs + pairs // 2,),
        scratch=[
            pltpu.VMEM((width, ring * rows), BF16),
            pltpu.VMEM((width, rows), BF16),
            pltpu.VMEM((width, LANES), F32),
            pltpu.VMEM((width, LANES), F32),
            pltpu.VMEM((width, LANES), F32),
            pltpu.VMEM((8, width), F32),
            pltpu.VMEM((LANES, width), F32),
        ],
        limit=20 << 20,
        cost=pl.CostEstimate(
            flops=2 * rows * width * width * (2 * ring + 1), bytes_accessed=2 * width * columns * 3, transcendentals=0
        ),
    )


def add_up(terms, start, stop):
    value = terms[0][:, start:stop].astype(F32)
    for term in terms[1:]:
        value = value + term[:, start:stop].astype(F32)
    return value


def wide_kernel(count, width, *refs):
    terms, refs = refs[:count], refs[count:]
    weight, first, second, grad_out, weight_out, first_out, second_out = refs
    hidden = weight.shape[2]
    spans = ((0, 3 * width, 0, width), (1, 0, width, hidden), (2, 0, width + hidden, hidden))
    for matrix, column, start, size in spans:
        grad = add_up(terms, start, start + size)
        at = slice(column, column + size)
        new_weight, new_first, new_second = adam_update(
            weight[matrix, :, at], grad, first[matrix, :, at], second[matrix, :, at], WEIGHT_DECAY, LEARN_RATE
        )
        grad_out[matrix, :, at] = grad
        weight_out[matrix, :, at] = new_weight
        first_out[matrix, :, at] = new_first
        second_out[matrix, :, at] = new_second


def wide_update(terms, width, mats, mats_m, mats_v):
    block = whole_block(mats.shape)
    return pl.pallas_call(
        functools.partial(wide_kernel, len(terms), width),
        grid=(1,),
        in_specs=[whole_block(term.shape) for term in terms] + [block] * 3,
        out_specs=[block] * 4,
        out_shape=[far_struct(mats.shape, F32)] * 4,
        compiler_params=pltpu.CompilerParams(vmem_limit_bytes=16 << 20),
        name="wide_update",
    )(*terms, *far(mats, mats_m, mats_v))


def narrow_kernel(count, *refs):
    terms, refs = refs[:count], refs[count:]
    weight, first, second, small, small_first, small_second = refs[:6]
    outs = refs[10:]
    size = weight.shape[2]
    grad = add_up(terms, 0, size)
    results = adam_update(weight[0], grad, first[0], second[0], WEIGHT_DECAY, LEARN_RATE)
    for out, value in zip(outs[:4], (grad, *results)):
        out[0] = value
    grad = jnp.transpose(add_up(terms, size, terms[0].shape[1]))[: small.shape[0], :]
    results = adam_update(small[...], grad, small_first[...], small_second[...], 0.0, SMALL_RATE)
    for out, value in zip(outs[4:], (grad, *results)):
        out[...] = value


def narrow_update(terms, width, mats, mats_m, mats_v, smalls, smalls_m, smalls_v, outs):
    count = len(terms)
    rows = mats.shape[1]
    block = pl.BlockSpec((1, rows, 3 * width), lambda i: (0, 0, 0))
    small = whole_block(smalls.shape)
    return pl.pallas_call(
        functools.partial(narrow_kernel, count),
        grid=(1,),
        in_specs=[whole_block(term.shape) for term in terms]
        + [block] * 3
        + [small] * 3
        + [pl.BlockSpec(memory_space=pl.ANY)] * 4,
        out_specs=[block] * 4 + [small] * 4,
        out_shape=[far_struct(mats.shape, F32)] * 4 + [struct(smalls.shape, F32)] * 4,
        input_output_aliases={count + 6 + index: index for index in range(4)},
        compiler_params=pltpu.CompilerParams(vmem_limit_bytes=12 << 20),
        name="narrow_update",
    )(*terms, *far(mats, mats_m, mats_v), smalls, smalls_m, smalls_v, *outs)


def groups(ring):
    ahead = [[i] for i in range(ring)]
    order = list(range(1, ring)) + [0]
    return ahead, [[i] for i in order]


def shards(frames, clip_ids, cotangent, mats, smalls, mats_m, mats_v, smalls_m, smalls_v):
    inputs = frames[0]
    upstream = cotangent[0]
    tok_rows, width = inputs.shape
    ring = lax.axis_size("seq")
    devices = ring * lax.axis_size("dp")
    block_rows = ring * mats.shape[1]
    total_rows = devices * mats.shape[1]
    here_dp = lax.axis_index("dp") if tuned() else jnp.int32(0)
    here = jnp.stack([here_dp, lax.axis_index("seq")]).astype(jnp.int32)

    normed_one, inv_one = normalize(inputs)
    id_row = clip_ids.astype(F32)
    id_rows = jnp.pad(id_row, ((0, 7), (0, width - tok_rows))).astype(BF16)
    piece = jnp.concatenate([normed_one.astype(BF16), id_rows], axis=0)
    normed_one, inv_one, piece = lax.optimization_barrier((normed_one, inv_one, piece))
    exts = [piece]
    for _ in range(1, ring):
        exts.append(turn(exts[-1]))

    mats_half = mats.astype(BF16)
    small_columns = jnp.pad(
        jnp.transpose(smalls.astype(BF16).astype(F32)), ((0, 0), (0, LANES - smalls.shape[0]))
    ).astype(BF16)
    chunk = jnp.concatenate([mats_half[0][:, : 3 * width], small_columns], axis=1)
    w_query, w_kv, side, small = assemble(
        gather_pieces(chunk, here, True), here, total_rows, block_rows
    )
    chunk = jnp.concatenate([mats_half[0][:, 3 * width :], mats_half[1]], axis=1)
    wide_pieces = [gather_pieces(chunk, here, False), gather_pieces(mats_half[2], here, False)]

    query, state = None, None
    kvs = [None] * ring
    ahead, back = groups(ring)
    for group in ahead:
        some, query, state = forward_block(
            here, [exts[i] for i in group], small, w_query, w_kv, id_row, query, state, group is ahead[-1]
        )
        for index, kv in zip(group, some):
            kvs[index] = kv
    mixed_half, stats = state

    output, grad_resid, grad_heads, mid_sums, *wide_grads = middle(
        here, inputs, mixed_half, upstream, small, wide_pieces, total_rows, block_rows
    )
    wide_terms = scatter_parts(wide_grads[0], wide_grads[-1], here, 3 * width)

    dq = None
    riding = None
    dkvs, sums = [None] * ring, []
    for group in back:
        dq, some, new_dkvs, parts = backward_block(
            here,
            query,
            grad_heads,
            mixed_half,
            stats,
            [kvs[i] for i in group],
            w_query,
            w_kv,
            id_row,
            [exts[i] for i in group],
            dq,
            group is back[-1],
        )
        sums.append(some)
        for index, dkv, part in zip(group, new_dkvs, parts):
            dkvs[index] = dkv
            if riding is not None:
                part = part + riding.astype(F32)
            if index:
                riding = turn(part.astype(BF16))
            else:
                grad_act_one = part

    cross_grads = cross(here, exts, dq, dkvs, sums, mid_sums, w_query, w_kv, side, block_rows)
    cross_terms = scatter_parts(cross_grads[0], cross_grads[-1], here, cross_grads[0].shape[1])
    grad_inputs = grad_resid + norm_backward(grad_act_one, normed_one, inv_one, small[0])

    begun = wide_update(wide_terms, width, mats, mats_m, mats_v)
    updated = narrow_update(
        cross_terms, width, mats, mats_m, mats_v, smalls, smalls_m, smalls_v, begun
    )
    mats_grad, new_mats, new_mats_m, new_mats_v = updated[:4]
    smalls_grad, new_smalls, new_smalls_m, new_smalls_v = updated[4:]
    return (
        output[None],
        grad_inputs[None],
        mats_grad,
        smalls_grad,
        new_mats,
        new_smalls,
        new_mats_m,
        new_mats_v,
        new_smalls_m,
        new_smalls_v,
    )


def solution(mesh):
    in_specs = (
        P("dp", "seq", None),
        P("dp", "seq"),
        P("dp", "seq", None),
        P(None, ("dp", "seq"), None),
        P(None, ("dp", "seq")),
        P(None, ("dp", "seq"), None),
        P(None, ("dp", "seq"), None),
        P(None, ("dp", "seq")),
        P(None, ("dp", "seq")),
    )
    out_specs = (
        P("dp", "seq", None),
        P("dp", "seq", None),
        P(None, ("dp", "seq"), None),
        P(None, ("dp", "seq")),
        P(None, ("dp", "seq"), None),
        P(None, ("dp", "seq")),
        P(None, ("dp", "seq"), None),
        P(None, ("dp", "seq"), None),
        P(None, ("dp", "seq")),
        P(None, ("dp", "seq")),
    )

    return jax.shard_map(shards, mesh=mesh, in_specs=in_specs, out_specs=out_specs, check_vma=False)
```

```python
import functools

import jax
import jax.numpy as jnp
from jax import lax
from jax.experimental import pallas as pl
from jax.experimental.pallas import tpu as pltpu
from jax.sharding import PartitionSpec as P


H = 12
DH = 64
STEP = 3
LANES = 128

NEGATIVE_FILL = -1e30
NORM_EPSILON = 1e-05
ROOT_HALF = 0.7071067811865476
INV_ROOT_TAU = 0.3989422804014327
LOG2E = 1.4426950408889634
BETA_FIRST = 0.9
BETA_SECOND = 0.95
LEARN_RATE = 0.01
SMALL_RATE = 0.1
WEIGHT_DECAY = 0.1
ADAM_EPSILON = 1e-08


F32 = jnp.float32
BF16 = jnp.bfloat16


def contract_rows(left, right):
    return lax.dot_general(left, right, (((0,), (0,)), ((), ())), preferred_element_type=F32)


def contract_cols(left, right):
    return lax.dot_general(left, right, (((1,), (1,)), ((), ())), preferred_element_type=F32)


def product(left, right):
    return jnp.dot(left, right, preferred_element_type=F32)


def normalize(values):
    row_mean = jnp.mean(values, axis=-1, keepdims=True)
    center = values - row_mean
    row_var = jnp.mean(center * center, axis=-1, keepdims=True)
    inv_std = lax.rsqrt(row_var + NORM_EPSILON)
    return center * inv_std, inv_std


def norm_backward(incoming, normed, inv_std, gain_vec):
    scaled = incoming * gain_vec
    return inv_std * (
        scaled
        - jnp.mean(scaled, axis=-1, keepdims=True)
        - normed * jnp.mean(scaled * normed, axis=-1, keepdims=True)
    )


def adam_update(weight, gradient, first, second, decay, step_rate):
    first_new = BETA_FIRST * first + (1.0 - BETA_FIRST) * gradient
    second_new = BETA_SECOND * second + (1.0 - BETA_SECOND) * gradient * gradient
    first_hat = first_new / (1.0 - BETA_FIRST**STEP)
    second_hat = second_new / (1.0 - BETA_SECOND**STEP)
    weight_new = weight - step_rate * (
        first_hat / (jnp.sqrt(second_hat) + ADAM_EPSILON) + decay * weight
    )
    return (weight_new, first_new, second_new)


def turn(block, step=1):
    count = lax.axis_size("seq")
    return lax.ppermute(block, "seq", [(i, (i + step) % count) for i in range(count)])


def swap(block, bit):
    count = lax.axis_size("dp")
    return lax.ppermute(block, "dp", [(i, i ^ bit) for i in range(count)])


def tuned():
    return lax.axis_size("dp") == 8 and lax.axis_size("seq") == 4


def call(kernel, here, ins, in_specs, out_shapes, out_specs, grid=(1,), scratch=(), limit=None, cost=None):
    return pl.pallas_call(
        kernel,
        grid_spec=pltpu.PrefetchScalarGridSpec(
            num_scalar_prefetch=1,
            grid=grid,
            in_specs=in_specs,
            out_specs=out_specs,
            scratch_shapes=list(scratch),
        ),
        out_shape=out_shapes,
        compiler_params=pltpu.CompilerParams(vmem_limit_bytes=limit),
        cost_estimate=cost,
    )(here, *ins)


def whole_block(shape):
    return pl.BlockSpec(shape, lambda *_: (0,) * len(shape), pipeline_mode=pl.Buffered(1))


def struct(shape, dtype):
    return jax.ShapeDtypeStruct(shape, dtype)


def far_struct(shape, dtype):
    return pltpu.HBM(shape, dtype)


def near():
    return pl.BlockSpec(memory_space=pltpu.VMEM)


def far(*arrays):
    return [pltpu.with_memory_space_constraint(array, pltpu.HBM) for array in arrays]


def pack_kernel(here_ref, *refs):
    *pieces, out = refs
    ring = len(pieces)
    for step, piece in enumerate(pieces):
        place = lax.rem(here_ref[1] - step + ring, ring)
        out[pl.ds(place, 1)] = piece[...][None]


def gather_pieces(shard, here, direct):
    ring = lax.axis_size("seq")
    rows, columns = shard.shape
    if not tuned():
        return [(lax.all_gather(shard, ("dp", "seq"), axis=0, tiled=True), None, 0)]
    pieces = [shard]
    for step in range(1, ring):
        if direct:
            pieces.append(turn(shard, step))
        else:
            pieces.append(turn(pieces[-1]))
    block = call(
        pack_kernel,
        here,
        pieces,
        [near()] * ring,
        struct((ring, rows, columns), shard.dtype),
        near(),
        limit=2 << 20,
    ).reshape(ring * rows, columns)
    half = ring * rows // 2
    from_x = swap(block, 2)
    from_y = swap(block, 4)
    low = swap(from_x[:half], 4)
    high = swap(from_y[half:], 2)
    held = [(block, 0, 0), (from_x, 2, 0), (from_y, 4, 0), (low, 6, 0), (high, 6, half)]
    other = [
        (swap(piece, 1), xor ^ 1, first)
        for piece, xor, first in held
    ]
    return held + other


def first_row(here_ref, block_rows, xor, first):
    if xor is None:
        return 0
    return pl.multiple_of((here_ref[0] ^ xor) * block_rows + first, 8)


def assemble_kernel(block_rows, places, here_ref, *refs):
    *pieces, wq_out, wkv_out, side_out, rows_out = refs
    pairs = wq_out.shape[0]
    for piece, (xor, first) in zip(pieces, places):
        at = pl.ds(first_row(here_ref, block_rows, xor, first), piece.shape[0])

        def lanes(index):
            return piece[:, index * LANES : (index + 1) * LANES]

        for pair in range(pairs):
            wq_out[pair, at, :] = lanes(pair)
            wkv_out[pair, at, :LANES] = lanes(pairs + pair)
            wkv_out[pair, at, LANES:] = lanes(2 * pairs + pair)
        side_out[at, :] = lanes(3 * pairs)
    rows_out[...] = jnp.transpose(side_out[...].astype(F32))


def assemble(pieces, here, rows, block_rows):
    pairs = pieces[0][0].shape[1] // (3 * LANES)
    shapes = [(pairs, rows, LANES), (pairs, rows, 2 * LANES), (rows, LANES), (LANES, rows)]
    return call(
        functools.partial(assemble_kernel, block_rows, [p[1:] for p in pieces]),
        here,
        [p[0] for p in pieces],
        [near()] * len(pieces),
        [struct(shape, F32 if shape == shapes[-1] else BF16) for shape in shapes],
        [near()] * len(shapes),
        limit=12 << 20,
    )


def join_kernel(here_ref, own_ref, recv_ref, me, x_send, y_send, x_late, y_late):
    rows = me.shape[0]
    half = rows // 2

    def total(slot, first, count):
        part = pl.ds(slot * rows + first, count)
        return (own_ref[part, :].astype(F32) + recv_ref[part, :].astype(F32)).astype(BF16)

    me[...] = total(0, 0, rows)
    x_send[:half, :] = total(3, half, half)
    x_send[half:, :] = total(1, half, half)
    y_send[:half, :] = total(3, 0, half)
    y_send[half:, :] = total(2, 0, half)
    x_late[...] = total(1, 0, half)
    y_late[...] = total(2, half, half)


def close_kernel(ring, here_ref, me, x_early, y_early, x_late, y_late, *refs):
    *outs, total = refs
    half = me.shape[0] // 2
    rows = me.shape[0] // ring
    total[:half, :] = (
        me[:half, :].astype(F32) + y_early[half:, :].astype(F32) + x_late[...].astype(F32)
    )
    total[half:, :] = (
        me[half:, :].astype(F32) + x_early[half:, :].astype(F32) + y_late[...].astype(F32)
    )
    for step, out in enumerate(outs):
        place = lax.rem(here_ref[1] + step, ring)
        out[...] = total[pl.ds(pl.multiple_of(place * rows, 8), rows), :].astype(out.dtype)


def scatter_parts(own, away, here, tile):
    ring = lax.axis_size("seq")
    if not tuned():
        return [lax.psum_scatter(own, ("dp", "seq"), scatter_dimension=0, tiled=True).astype(F32)]
    count, columns = own.shape
    rows = count // 4
    half = rows // 2
    got = swap(away, 1)

    alone = tile == columns

    def spec(height):
        return near() if alone else pl.BlockSpec((height, tile), lambda j, *_: (0, j))

    grid = (columns // tile,)
    heights = (rows, rows, rows, half, half)
    me, x_send, y_send, x_late, y_late = call(
        join_kernel,
        here,
        [own, got],
        [spec(count)] * 2,
        [struct((height, columns), BF16) for height in heights],
        [spec(height) for height in heights],
        grid=grid,
        limit=(2 if alone else 18) << 20,
    )
    x_early = swap(x_send, 2)
    y_early = swap(y_send, 4)
    x_sum = (x_late.astype(F32) + y_early[:half].astype(F32)).astype(BF16)
    y_sum = (y_late.astype(F32) + x_early[:half].astype(F32)).astype(BF16)
    x_late = swap(x_sum, 2)
    y_late = swap(y_sum, 4)
    small = rows // ring
    terms = call(
        functools.partial(close_kernel, ring),
        here,
        [me, x_early, y_early, x_late, y_late],
        [near()] * len(heights),
        [struct((small, columns), F32 if step == 0 else BF16) for step in range(ring)],
        [near()] * ring,
        scratch=[pltpu.VMEM((rows, columns), F32)],
        limit=(5 if alone else 14) << 20,
    )
    return [terms[0]] + [turn(terms[step], step) for step in range(1, ring)]


def own_slots():
    if tuned():
        return [0, 2, 4, 6], [1, 3, 5, 7]
    return list(range(lax.axis_size("dp"))), []


def low_lanes(shape):
    return lax.broadcasted_iota(jnp.int32, shape, 1) < DH


def stack(refs):
    if len(refs) == 1:
        return refs[0][...]
    return jnp.concatenate([ref[...] for ref in refs], axis=0)


def id_mask(exts, rows, query_row):
    masks = []
    for ext in exts:
        key_ids = ext[rows : rows + 8, :rows].astype(F32)[0:1, :]
        key_ids = jnp.transpose(jnp.broadcast_to(key_ids, (LANES, rows)))
        masks.append(jnp.where(key_ids[:, 0:1] == query_row, 0.0, NEGATIVE_FILL))
    return masks[0] if len(masks) == 1 else jnp.concatenate(masks, axis=0)


def forward_kernel(count, first, last, here_ref, *refs):
    exts, refs = refs[:count], refs[count:]
    small_ref, wkv_ref, qid_ref = refs[:3]
    refs = refs[3:]
    if first:
        wq_ref, refs = refs[0], refs[1:]
    else:
        q_ref, stat_ref, acc_ref = refs[:3]
        refs = refs[3:]
    kv_outs, refs = refs[:count], refs[count:]
    if first:
        q_out, refs = refs[0], refs[1:]
    out_ref, stat_out, act_ref, mask_ref = refs
    rows = qid_ref.shape[1]
    pair = pl.program_id(0)
    lanes = pl.ds(pl.multiple_of(pair * LANES, LANES), LANES)

    @pl.when(pair == 0)
    def _():
        for index, ext in enumerate(exts):
            normed = ext[:rows, :].astype(F32)
            act_ref[index * rows : (index + 1) * rows, :] = (
                normed * small_ref[0:1, :] + small_ref[1:2, :]
            ).astype(BF16)
        mask_ref[...] = id_mask(exts, rows, qid_ref[0:1, :])

    both = product(act_ref[...], wkv_ref[pair])
    keys = both[:, :LANES].astype(BF16)
    values = (both[:, LANES:] + small_ref[3:4, lanes]).astype(BF16)
    for index in range(count):
        part = slice(index * rows, (index + 1) * rows)
        kv_outs[index][pair, :, :LANES] = keys[part]
        kv_outs[index][pair, :, LANES:] = values[part]
    if first:
        query = (product(act_ref[:rows, :], wq_ref[pair]) + small_ref[2:3, lanes]).astype(BF16)
        q_out[pair] = query
    else:
        query = q_ref[pair]
    low = low_lanes(query.shape)
    key_low = low_lanes(keys.shape)
    zero = jnp.zeros_like(query)
    one = jnp.ones_like(values)
    maxima, totals, mixes = [], [], []
    for head in range(2):
        here, there = slice(head * DH, (head + 1) * DH), (1 - head) * DH
        side = low if head == 0 else ~low
        key_side = key_low if head == 0 else ~key_low
        scores = contract_cols(keys, jnp.where(side, query, zero)) * (0.125 * LOG2E)
        scores = scores + mask_ref[...]
        top = jnp.max(scores, axis=0, keepdims=True)
        if not first:
            before = stat_ref[pair, head : head + 1, :]
            top = jnp.maximum(top, before)
        portion = jnp.exp2(scores - top).astype(BF16)
        mixed = contract_rows(jnp.where(key_side, values, one), portion)
        total = mixed[there : there + 1, :]
        mixed = mixed[here, :]
        if not first:
            factor = jnp.exp2(before - top)
            total = total + stat_ref[pair, 2 + head : 3 + head, :] * factor
            start = pl.multiple_of(pair * LANES + head * DH, DH)
            mixed = mixed + acc_ref[pl.ds(start, DH), :] * factor
        maxima.append(top)
        totals.append(total)
        mixes.append(mixed / total if last else mixed)
    mixed = jnp.concatenate(mixes, axis=0)
    if last:
        out_ref[:, lanes] = jnp.transpose(mixed).astype(BF16)
        for head in range(2):
            stat_out[pair, head : head + 1, :] = maxima[head] + jnp.log2(totals[head])
    else:
        out_ref[lanes, :] = mixed
        for head in range(2):
            stat_out[pair, head : head + 1, :] = maxima[head]
            stat_out[pair, 2 + head : 3 + head, :] = totals[head]


def forward_block(here, exts, small, w_query, w_kv, query_row, query, state, last):
    count = len(exts)
    rows = query_row.shape[1]
    width = exts[0].shape[1]
    pairs = width // LANES
    first = state is None
    args = [*exts, small, w_kv, query_row]
    out_shapes = [struct((pairs, rows, 2 * LANES), BF16)] * count
    out_specs = [near()] * count
    if first:
        args += [w_query]
        out_shapes.append(struct((pairs, rows, LANES), BF16))
        out_specs.append(near())
    else:
        args += [query, *state]
    out_shapes += [
        struct((rows, width), BF16) if last else struct((width, rows), F32),
        struct((pairs, 4, rows), F32),
    ]
    out_specs += [near(), near()]
    in_specs = [near()] * len(args)
    result = call(
        functools.partial(forward_kernel, count, first, last),
        here,
        args,
        in_specs,
        out_shapes,
        out_specs,
        grid=(pairs,),
        scratch=[pltpu.VMEM((count * rows, width), BF16), pltpu.VMEM((count * rows, rows), F32)],
        limit=16 << 20,
        cost=pl.CostEstimate(
            flops=24 * count * rows * rows * width,
            bytes_accessed=8 * rows * width,
            transcendentals=count * rows * rows * H,
        ),
    )
    kvs, rest = result[:count], result[count:]
    if first:
        query, rest = rest[0], rest[1:]
    return kvs, query, tuple(rest[::-1]) if not last else tuple(rest)


def backward_kernel(count, first, last, here_ref, *refs):
    q_ref, do_ref, o_ref, stat_ref, wkv_ref, qid_ref = refs[:6]
    refs = refs[6:]
    exts, kvs, refs = refs[:count], refs[count : 2 * count], refs[2 * count :]
    if not first:
        dq_ref, refs = refs[0], refs[1:]
    if last:
        wq_ref, refs = refs[0], refs[1:]
    dq_out, sum_ref, refs = refs[0], refs[1], refs[2:]
    dkv_outs, parts, refs = refs[:count], refs[count : 2 * count], refs[2 * count :]
    (mask_ref,) = refs
    rows = do_ref.shape[0]
    pair = pl.program_id(0)
    lanes = pl.ds(pl.multiple_of(pair * LANES, LANES), LANES)

    @pl.when(pair == 0)
    def _():
        mask_ref[...] = id_mask(exts, rows, qid_ref[0:1, :])
        for part in parts:
            part[...] = jnp.zeros_like(part)

    query = q_ref[pair]
    grad = do_ref[:, lanes]
    both = stack([kv.at[pair] for kv in kvs])
    keys, values = both[:, :LANES], both[:, LANES:]
    low = low_lanes(query.shape)
    key_low = low_lanes(keys.shape)
    zero = jnp.zeros_like(query)
    flipped = jnp.transpose(grad.astype(F32) * o_ref[:, lanes].astype(F32))
    sides = (low, ~low)
    queries = [jnp.where(side, query, zero) for side in sides]
    grads = [jnp.where(side, grad, zero) for side in sides]
    all_scores = contract_cols(keys, jnp.concatenate(queries, axis=0))
    all_changes = contract_cols(values, jnp.concatenate(grads, axis=0))
    dk = dv = dq = None
    for head in range(2):
        span = slice(head * rows, (head + 1) * rows)
        delta = jnp.sum(flipped[head * DH : (head + 1) * DH, :], axis=0, keepdims=True)
        scores = all_scores[:, span] * (0.125 * LOG2E) + mask_ref[...]
        portion = jnp.exp2(scores - stat_ref[pair, head : head + 1, :])
        score_grad = (portion * (all_changes[:, span] - delta)).astype(BF16)
        keys_here = jnp.where(key_low if head == 0 else ~key_low, keys, jnp.zeros_like(keys))
        dv_here = product(portion.astype(BF16), grads[head])
        dk_here = product(score_grad, queries[head])
        dq_here = contract_rows(score_grad, keys_here)
        if head == 0:
            dk, dv, dq = dk_here, dv_here, dq_here
        else:
            dk, dv, dq = dk + dk_here, dv + dv_here, dq + dq_here
    dk = (dk * 0.125).astype(BF16)
    dv = dv.astype(BF16)
    dq = dq * 0.125
    if not first:
        dq = dq + dq_ref[pair]
    both = jnp.concatenate([dk, dv], axis=1)
    sum_ref[pair, 0:1, :] = jnp.sum(both.astype(F32), axis=0, keepdims=True)
    part = contract_cols(both, wkv_ref[pair])
    for index in range(count):
        span = slice(index * rows, (index + 1) * rows)
        dkv_outs[index][pair] = both[span]
        term = part[span]
        if last and index == count - 1:
            dq = dq.astype(BF16)
            sum_ref[pair, 1:2, :LANES] = jnp.sum(dq.astype(F32), axis=0, keepdims=True)
            term = term + contract_cols(dq, wq_ref[pair])
        parts[index][...] += term
    dq_out[pair] = dq


def backward_block(here, query, grad, mixed, stats, kvs, w_query, w_kv, query_row, exts, dq, last):
    count = len(exts)
    rows, width = grad.shape
    pairs = width // LANES
    first = dq is None
    args = [query, grad, mixed, stats, w_kv, query_row, *exts, *kvs]
    in_specs = [near()] * (6 + 2 * count)
    if not first:
        in_specs.append(near())
        args.append(dq)
    if last:
        in_specs.append(near())
        args.append(w_query)
    result = call(
        functools.partial(backward_kernel, count, first, last),
        here,
        args,
        in_specs,
        [struct((pairs, rows, LANES), BF16 if last else F32), struct((pairs, 8, 2 * LANES), F32)]
        + [struct((pairs, rows, 2 * LANES), BF16)] * count
        + [struct((rows, width), F32)] * count,
        [near()] * (2 + 2 * count),
        grid=(pairs,),
        scratch=[pltpu.VMEM((count * rows, rows), F32)],
        limit=16 << 20,
        cost=pl.CostEstimate(
            flops=40 * count * rows * rows * width,
            bytes_accessed=16 * rows * width,
            transcendentals=count * rows * rows * H,
        ),
    )
    dq, sums, rest = result[0], result[1], result[2:]
    return dq, sums, rest[:count], rest[count:]


def transposed_slots(here_ref, values, slots, block_rows, plain_ref, out_ref):
    plain_ref[...] = jnp.transpose(values.astype(F32)).astype(BF16)
    for index, xor in enumerate(slots):
        start = pl.multiple_of((here_ref[0] ^ xor) * block_rows, 8)
        out_ref[index * block_rows : (index + 1) * block_rows, :] = plain_ref[pl.ds(start, block_rows), :]


def middle_kernel(places, block_rows, slots, kept, tile, here_ref, *refs):
    count = len(places)
    frames_ref, mixed_ref, cot_ref, small_ref = refs[:4]
    pieces, refs = refs[4 : 4 + count], refs[4 + count :]
    out_ref, dr_ref, doh_ref, sum_ref = refs[:4]
    grads, refs = refs[4 : 4 + len(kept)], refs[4 + len(kept) :]
    (
        w_ref,
        stage_ref,
        last_ref,
        normed_ref,
        back_ref,
        act_ref,
        half_ref,
        act_flip,
        half_flip,
        plain_ref,
        bias_ref,
        bias_sum,
        in_sems,
        out_sems,
        last_sems,
    ) = refs
    width = frames_ref.shape[1]
    hidden = bias_ref.shape[1]

    copies = []
    for index, (piece, (xor, first, column)) in enumerate(zip(pieces, places)):
        start = first_row(here_ref, block_rows, xor, first)
        height, span = piece.shape
        target = w_ref.at[pl.ds(start, height), column : column + span]
        copies.append(pltpu.make_async_copy(piece, target, in_sems.at[index]))
    for copy in copies:
        copy.start()
    cot = cot_ref[...]
    half_ref[...] = cot.astype(BF16)
    transposed_slots(here_ref, half_ref[...], slots, block_rows, plain_ref, half_flip)
    for index in range(4):
        bias_ref[:, index * width : (index + 1) * width] = small_ref[8 + index : 9 + index, :]
    sum_ref[3:4, :] = jnp.sum(cot, axis=0, keepdims=True)
    for copy in copies:
        copy.wait()

    resid = frames_ref[...] + product(mixed_ref[...], w_ref[:, :width]) + small_ref[4:5, :]
    normed, inv_std = normalize(resid)
    normed_ref[...] = normed
    act_ref[...] = (normed * small_ref[5:6, :] + small_ref[6:7, :]).astype(BF16)
    out_ref[...] = resid + small_ref[7:8, :]
    back_ref[...] = jnp.zeros_like(back_ref)
    transposed_slots(here_ref, act_ref[...], slots, block_rows, plain_ref, act_flip)

    def send(source, column, start, size, sems):
        moves = []
        first = 0
        for index, (grad, height) in enumerate(zip(grads, kept)):
            moves.append(
                pltpu.make_async_copy(
                    source.at[first : first + height, column : column + size],
                    grad.at[:, pl.ds(start, size)],
                    sems.at[index],
                )
            )
            first += height
        return moves

    tiles = hidden // tile

    def columns(index):
        up = pl.multiple_of(width + index * tile, LANES)
        down = pl.multiple_of(width + hidden + index * tile, LANES)
        return up, down, pl.multiple_of(index * tile, LANES)

    def moves_of(index):
        up, down, _ = columns(index)
        slot = lax.rem(index, 2)
        stage = stage_ref.at[slot]
        return send(stage, 0, up, tile, out_sems.at[slot, 0]) + send(
            stage, tile, down, tile, out_sems.at[slot, 1]
        )

    def body(index, carry):
        up, down, at = columns(index)
        slot = lax.rem(index, 2)

        @pl.when(index >= 2)
        def _():
            for move in moves_of(index - 2):
                move.wait()

        w_up = w_ref[:, pl.ds(up, tile)]
        w_down = w_ref[:, pl.ds(down, tile)]
        u = product(act_ref[...], w_up) + bias_ref[:, pl.ds(at, tile)]
        rise = 0.5 * (1.0 + lax.erf(u * ROOT_HALF))
        slope = rise + u * jnp.exp(-0.5 * u * u) * INV_ROOT_TAU
        value = (u * rise).astype(BF16)
        out_ref[...] += contract_cols(value, w_down)
        du = product(half_ref[...], w_down) * slope
        bias_sum[:, pl.ds(at, tile)] = jnp.sum(du, axis=0, keepdims=True)
        du = du.astype(BF16)
        back_ref[...] += contract_cols(du, w_up)
        stage_ref[slot, :, :tile] = product(act_flip[...], du).astype(BF16)
        stage_ref[slot, :, tile:] = product(half_flip[...], value).astype(BF16)
        for move in moves_of(index):
            move.start()
        return carry

    lax.fori_loop(0, tiles, body, 0)

    incoming = back_ref[...]
    normed = normed_ref[...]
    dr = cot_ref[...] + norm_backward(incoming, normed, inv_std, small_ref[5:6, :])
    dr_ref[...] = dr
    sum_ref[0:1, :] = jnp.sum(dr, axis=0, keepdims=True)
    sum_ref[1:2, :] = jnp.sum(incoming * normed, axis=0, keepdims=True)
    sum_ref[2:3, :] = jnp.sum(incoming, axis=0, keepdims=True)
    for index in range(4):
        sum_ref[4 + index : 5 + index, :] = bias_sum[:, index * width : (index + 1) * width]
    drh = dr.astype(BF16)
    transposed_slots(here_ref, mixed_ref[...], slots, block_rows, plain_ref, act_flip)
    last_ref[...] = product(act_flip[...], drh).astype(BF16)
    finals = send(last_ref, 0, 0, width, last_sems)
    for move in finals:
        move.start()
    doh_ref[...] = contract_cols(drh, w_ref[:, :width]).astype(BF16)
    for index in range(max(tiles - 2, 0), tiles):
        finals = finals + moves_of(jnp.int32(index))
    for move in finals:
        move.wait()


def middle(here, frames, mixed, cot, small, pieces, rows_total, block_rows):
    rows, width = frames.shape
    starts = [0, pieces[0][0][0].shape[1]]
    columns = starts[1] + pieces[1][0][0].shape[1]
    pieces = [(*piece, start) for part, start in zip(pieces, starts) for piece in part]
    hidden = (columns - width) // 2
    tile = 4 * LANES
    kept, given = own_slots()
    heights = [len(part) * block_rows for part in (kept, given) if part]
    anywhere = pl.BlockSpec(memory_space=pl.ANY)
    full = whole_block((rows, width))
    outs = [struct((rows, width), F32), struct((rows, width), F32), struct((rows, width), BF16), struct((8, width), F32)]
    return call(
        functools.partial(
            middle_kernel, [p[1:] for p in pieces], block_rows, kept + given, heights, tile
        ),
        here,
        [frames, mixed, cot, small, *[p[0] for p in pieces]],
        [full, full, full, pl.BlockSpec((16, width), lambda *_: (0, 0))] + [anywhere] * len(pieces),
        outs + [struct((height, columns), BF16) for height in heights],
        [full, full, full, whole_block((8, width))] + [anywhere] * len(heights),
        scratch=[
            pltpu.VMEM((rows_total, columns), BF16),
            pltpu.VMEM((2, rows_total, 2 * tile), BF16),
            pltpu.VMEM((rows_total, width), BF16),
            pltpu.VMEM((rows, width), F32),
            pltpu.VMEM((rows, width), F32),
            pltpu.VMEM((rows, width), BF16),
            pltpu.VMEM((rows, width), BF16),
            pltpu.VMEM((width, rows), BF16),
            pltpu.VMEM((width, rows), BF16),
            pltpu.VMEM((width, rows), BF16),
            pltpu.VMEM((1, hidden), F32),
            pltpu.VMEM((1, hidden), F32),
            pltpu.SemaphoreType.DMA((len(pieces),)),
            pltpu.SemaphoreType.DMA((2, 2, len(heights))),
            pltpu.SemaphoreType.DMA((len(heights),)),
        ],
        limit=31 << 20,
        cost=pl.CostEstimate(
            flops=36 * rows * width * hidden // 3, bytes_accessed=4 * rows_total * columns, transcendentals=2 * rows * hidden
        ),
    )


def cross_kernel(ring, slots, block_rows, heights, here_ref, *refs):
    exts, refs = refs[:ring], refs[ring:]
    dq_ref, refs = refs[0], refs[1:]
    dkvs, refs = refs[:ring], refs[ring:]
    sums, refs = refs[:ring], refs[ring:]
    mid_ref, wkv_ref, wq_ref, cols_ref, refs = refs[0], refs[1], refs[2], refs[3], refs[4:]
    outs, refs = refs[: len(heights)], refs[len(heights) :]
    flip_ref, plain_ref, gain_ref, side_ref, turned_ref, shift_ref, line_ref = refs
    step = pl.program_id(0)
    rows = dq_ref.shape[1]
    width = plain_ref.shape[0]
    pairs = width // LANES

    def slot_rows(index):
        start = pl.multiple_of((here_ref[0] ^ slots[index]) * block_rows, 8)
        return pl.ds(start, block_rows), pl.ds(index * block_rows, block_rows)

    @pl.when(step == 0)
    def _():
        for index in range(ring):
            plain_ref[...] = jnp.transpose(exts[index][:rows, :].astype(F32)).astype(BF16)
            for slot in range(len(slots)):
                source, target = slot_rows(slot)
                flip_ref[target, index * rows : (index + 1) * rows] = plain_ref[source, :]
        for slot in range(len(slots)):
            source, target = slot_rows(slot)
            side = cols_ref[source, :].astype(F32)
            side_ref[target, :] = jnp.broadcast_to(side[:, 0:1], side.shape)
            turned_ref[target, :] = jnp.broadcast_to(side[:, 1:2], side.shape)
        gain_ref[...] = jnp.zeros_like(gain_ref)
        shift_ref[...] = jnp.zeros_like(shift_ref)
        line_ref[...] = jnp.zeros_like(line_ref)

    def finish(crossed, line, weights, columns):
        wide = jnp.broadcast_to(line, (8, 2 * LANES))
        high = wide.astype(BF16)
        low = (wide - high.astype(F32)).astype(BF16)
        full = weights[...] if len(weights.shape) == 2 else jnp.concatenate([weights[0], weights[1]], axis=1)
        shift_ref[...] += contract_cols(high, full) + contract_cols(low, full)
        for index in range(len(slots)):
            source, target = slot_rows(index)
            part = crossed[index * block_rows : (index + 1) * block_rows, :]
            gain, shift = side_ref[target, :], turned_ref[target, :]
            out = 0 if index * block_rows < heights[0] else 1
            first = index * block_rows - (heights[0] if out else 0)
            total = gain_ref[target, :]
            for half in range(2):
                lanes = slice(half * LANES, (half + 1) * LANES)
                if len(weights.shape) == 2:
                    weight = weights[source, lanes]
                else:
                    weight = weights[half, source, :]
                total = total + weight.astype(F32) * part[:, lanes]
                grad = gain * part[:, lanes] + shift * line[:, lanes]
                outs[out][first : first + block_rows, pl.ds(columns[half], LANES)] = grad.astype(BF16)
            gain_ref[target, :] = total

    @pl.when(step < pairs)
    def _():
        crossed = product(flip_ref[:, :rows], dkvs[0][step])
        for index in range(1, ring):
            crossed += product(flip_ref[:, index * rows : (index + 1) * rows], dkvs[index][step])
        line = sums[0][step, 0:1, :]
        for other in sums[1:]:
            line = line + other[step, 0:1, :]
        at = pl.multiple_of(step * LANES, LANES)
        line_ref[3:4, pl.ds(at, LANES)] = line[:, LANES:]
        finish(crossed, line, wkv_ref.at[step], (at + width, at + 2 * width))

    @pl.when(step >= pairs)
    def _():
        pair = 2 * (step - pairs)
        grads = jnp.concatenate([dq_ref[pair], dq_ref[pair + 1]], axis=1)
        line = jnp.concatenate(
            [sums[-1][pair, 1:2, :LANES], sums[-1][pair + 1, 1:2, :LANES]], axis=1
        )
        at = pl.multiple_of(pair * LANES, LANES)
        line_ref[2:3, pl.ds(at, 2 * LANES)] = line
        finish(product(flip_ref[:, :rows], grads), line, wq_ref.at[pl.ds(pair, 2)], (at, at + LANES))

    @pl.when(step == pl.num_programs(0) - 1)
    def _():
        line_ref[1:2, :] = shift_ref[0:1, :]
        line_ref[4:12, :] = mid_ref[...]
        turned_ref[...] = jnp.transpose(line_ref[...])
        lane = lax.broadcasted_iota(jnp.int32, (block_rows, LANES), 1)
        for index in range(len(slots)):
            source, target = slot_rows(index)
            gain = jnp.sum(gain_ref[target, :], axis=1, keepdims=True)
            value = jnp.where(lane == 0, gain, turned_ref[source, :])
            out = 0 if index * block_rows < heights[0] else 1
            start = index * block_rows - (heights[0] if out else 0)
            outs[out][start : start + block_rows, 3 * width :] = value.astype(BF16)


def cross(here, exts, dq, dkvs, sums, mid_sums, w_query, w_kv, side, block_rows):
    ring = len(exts)
    pairs, rows, _ = dq.shape
    width = pairs * LANES
    kept, given = own_slots()
    heights = [len(part) * block_rows for part in (kept, given) if part]
    columns = 3 * width + LANES

    return call(
        functools.partial(cross_kernel, ring, kept + given, block_rows, heights),
        here,
        [*exts, dq, *dkvs, *sums, mid_sums, w_kv, w_query, side],
        [near()] * (3 * ring + 5),
        [struct((height, columns), BF16) for height in heights],
        [near()] * len(heights),
        grid=(pairs + pairs // 2,),
        scratch=[
            pltpu.VMEM((width, ring * rows), BF16),
            pltpu.VMEM((width, rows), BF16),
            pltpu.VMEM((width, LANES), F32),
            pltpu.VMEM((width, LANES), F32),
            pltpu.VMEM((width, LANES), F32),
            pltpu.VMEM((8, width), F32),
            pltpu.VMEM((LANES, width), F32),
        ],
        limit=20 << 20,
        cost=pl.CostEstimate(
            flops=2 * rows * width * width * (2 * ring + 1), bytes_accessed=2 * width * columns * 3, transcendentals=0
        ),
    )


def add_up(terms, start, stop):
    value = terms[0][:, start:stop].astype(F32)
    for term in terms[1:]:
        value = value + term[:, start:stop].astype(F32)
    return value


def wide_kernel(count, width, *refs):
    terms, refs = refs[:count], refs[count:]
    weight, first, second, grad_out, weight_out, first_out, second_out = refs
    hidden = weight.shape[2]
    spans = ((0, 3 * width, 0, width), (1, 0, width, hidden), (2, 0, width + hidden, hidden))
    for matrix, column, start, size in spans:
        grad = add_up(terms, start, start + size)
        at = slice(column, column + size)
        new_weight, new_first, new_second = adam_update(
            weight[matrix, :, at], grad, first[matrix, :, at], second[matrix, :, at], WEIGHT_DECAY, LEARN_RATE
        )
        grad_out[matrix, :, at] = grad
        weight_out[matrix, :, at] = new_weight
        first_out[matrix, :, at] = new_first
        second_out[matrix, :, at] = new_second


def wide_update(terms, width, mats, mats_m, mats_v):
    block = whole_block(mats.shape)
    return pl.pallas_call(
        functools.partial(wide_kernel, len(terms), width),
        grid=(1,),
        in_specs=[whole_block(term.shape) for term in terms] + [block] * 3,
        out_specs=[block] * 4,
        out_shape=[far_struct(mats.shape, F32)] * 4,
        compiler_params=pltpu.CompilerParams(vmem_limit_bytes=16 << 20),
        name="wide_update",
    )(*terms, *far(mats, mats_m, mats_v))


def narrow_kernel(count, *refs):
    terms, refs = refs[:count], refs[count:]
    weight, first, second, small, small_first, small_second = refs[:6]
    outs = refs[10:]
    size = weight.shape[2]
    grad = add_up(terms, 0, size)
    results = adam_update(weight[0], grad, first[0], second[0], WEIGHT_DECAY, LEARN_RATE)
    for out, value in zip(outs[:4], (grad, *results)):
        out[0] = value
    grad = jnp.transpose(add_up(terms, size, terms[0].shape[1]))[: small.shape[0], :]
    results = adam_update(small[...], grad, small_first[...], small_second[...], 0.0, SMALL_RATE)
    for out, value in zip(outs[4:], (grad, *results)):
        out[...] = value


def narrow_update(terms, width, mats, mats_m, mats_v, smalls, smalls_m, smalls_v, outs):
    count = len(terms)
    rows = mats.shape[1]
    block = pl.BlockSpec((1, rows, 3 * width), lambda i: (0, 0, 0))
    small = whole_block(smalls.shape)
    return pl.pallas_call(
        functools.partial(narrow_kernel, count),
        grid=(1,),
        in_specs=[whole_block(term.shape) for term in terms]
        + [block] * 3
        + [small] * 3
        + [pl.BlockSpec(memory_space=pl.ANY)] * 4,
        out_specs=[block] * 4 + [small] * 4,
        out_shape=[far_struct(mats.shape, F32)] * 4 + [struct(smalls.shape, F32)] * 4,
        input_output_aliases={count + 6 + index: index for index in range(4)},
        compiler_params=pltpu.CompilerParams(vmem_limit_bytes=12 << 20),
        name="narrow_update",
    )(*terms, *far(mats, mats_m, mats_v), smalls, smalls_m, smalls_v, *outs)


def groups(ring):
    ahead = [[i] for i in range(ring)]
    order = list(range(1, ring)) + [0]
    return ahead, [[i] for i in order]


def shards(frames, clip_ids, cotangent, mats, smalls, mats_m, mats_v, smalls_m, smalls_v):
    inputs = frames[0]
    upstream = cotangent[0]
    tok_rows, width = inputs.shape
    ring = lax.axis_size("seq")
    devices = ring * lax.axis_size("dp")
    block_rows = ring * mats.shape[1]
    total_rows = devices * mats.shape[1]
    here_dp = lax.axis_index("dp") if tuned() else jnp.int32(0)
    here = jnp.stack([here_dp, lax.axis_index("seq")]).astype(jnp.int32)

    normed_one, inv_one = normalize(inputs)
    id_row = clip_ids.astype(F32)
    id_rows = jnp.pad(id_row, ((0, 7), (0, width - tok_rows))).astype(BF16)
    piece = jnp.concatenate([normed_one.astype(BF16), id_rows], axis=0)
    normed_one, inv_one, piece = lax.optimization_barrier((normed_one, inv_one, piece))
    exts = [piece]
    for _ in range(1, ring):
        exts.append(turn(exts[-1]))

    mats_half = mats.astype(BF16)
    small_columns = jnp.pad(
        jnp.transpose(smalls.astype(BF16).astype(F32)), ((0, 0), (0, LANES - smalls.shape[0]))
    ).astype(BF16)
    chunk = jnp.concatenate([mats_half[0][:, : 3 * width], small_columns], axis=1)
    w_query, w_kv, side, small = assemble(
        gather_pieces(chunk, here, True), here, total_rows, block_rows
    )
    chunk = jnp.concatenate([mats_half[0][:, 3 * width :], mats_half[1]], axis=1)
    wide_pieces = [gather_pieces(chunk, here, False), gather_pieces(mats_half[2], here, False)]

    query, state = None, None
    kvs = [None] * ring
    ahead, back = groups(ring)
    for group in ahead:
        some, query, state = forward_block(
            here, [exts[i] for i in group], small, w_query, w_kv, id_row, query, state, group is ahead[-1]
        )
        for index, kv in zip(group, some):
            kvs[index] = kv
    mixed_half, stats = state

    output, grad_resid, grad_heads, mid_sums, *wide_grads = middle(
        here, inputs, mixed_half, upstream, small, wide_pieces, total_rows, block_rows
    )
    wide_terms = scatter_parts(wide_grads[0], wide_grads[-1], here, 3 * width)

    dq = None
    riding = None
    dkvs, sums = [None] * ring, []
    for group in back:
        dq, some, new_dkvs, parts = backward_block(
            here,
            query,
            grad_heads,
            mixed_half,
            stats,
            [kvs[i] for i in group],
            w_query,
            w_kv,
            id_row,
            [exts[i] for i in group],
            dq,
            group is back[-1],
        )
        sums.append(some)
        for index, dkv, part in zip(group, new_dkvs, parts):
            dkvs[index] = dkv
            if riding is not None:
                part = part + riding.astype(F32)
            if index:
                riding = turn(part.astype(BF16))
            else:
                grad_act_one = part

    cross_grads = cross(here, exts, dq, dkvs, sums, mid_sums, w_query, w_kv, side, block_rows)
    cross_terms = scatter_parts(cross_grads[0], cross_grads[-1], here, cross_grads[0].shape[1])
    grad_inputs = grad_resid + norm_backward(grad_act_one, normed_one, inv_one, small[0])

    begun = wide_update(wide_terms, width, mats, mats_m, mats_v)
    updated = narrow_update(
        cross_terms, width, mats, mats_m, mats_v, smalls, smalls_m, smalls_v, begun
    )
    mats_grad, new_mats, new_mats_m, new_mats_v = updated[:4]
    smalls_grad, new_smalls, new_smalls_m, new_smalls_v = updated[4:]
    return (
        output[None],
        grad_inputs[None],
        mats_grad,
        smalls_grad,
        new_mats,
        new_smalls,
        new_mats_m,
        new_mats_v,
        new_smalls_m,
        new_smalls_v,
    )


def solution(mesh):
    in_specs = (
        P("dp", "seq", None),
        P("dp", "seq"),
        P("dp", "seq", None),
        P(None, ("dp", "seq"), None),
        P(None, ("dp", "seq")),
        P(None, ("dp", "seq"), None),
        P(None, ("dp", "seq"), None),
        P(None, ("dp", "seq")),
        P(None, ("dp", "seq")),
    )
    out_specs = (
        P("dp", "seq", None),
        P("dp", "seq", None),
        P(None, ("dp", "seq"), None),
        P(None, ("dp", "seq")),
        P(None, ("dp", "seq"), None),
        P(None, ("dp", "seq")),
        P(None, ("dp", "seq"), None),
        P(None, ("dp", "seq"), None),
        P(None, ("dp", "seq")),
        P(None, ("dp", "seq")),
    )

    return jax.shard_map(shards, mesh=mesh, in_specs=in_specs, out_specs=out_specs, check_vma=False)
```
